32 devices in a mesh: group: 8 (over z, x), ctx: 2 (over y), wshard: 2 (over core).
Axes of the slice: x: 2, y: 2, z: 4, core: 2. Of those that a mesh axis runs over, the one named last changes fastest.
Arguments:
- inputs: bfloat16 [8192, 1536], P(('group', 'ctx', 'wshard')), may hold values from -6 to 6
- out_grad: bfloat16 [8192, 1536], P(('group', 'ctx', 'wshard')), may hold values from -6 to 6
- lengths: int32 [8, 4], P('group'), may hold values from 1 to 512, 1024 in all within a row
- permutation: int32 [8, 1024], P('group'), may hold values from 0 to 1023, each once within a row
- gain_attention: float32 [1536], replicated, may hold values from 0.5 to 1.5
- query_weight: bfloat16 [1536, 768], P('wshard'), may hold values from -0.0546875 to 0.0546875
- key_weight: bfloat16 [1536, 768], P('wshard'), may hold values from -0.0546875 to 0.0546875
- value_weight: bfloat16 [1536, 768], P('wshard'), may hold values from -0.15625 to 0.15625
- out_weight: bfloat16 [768, 1536], P('wshard'), may hold values from -3.5 to 3.5
- bucket_bias: float32 [32, 12], replicated, may hold values from -4 to 4
- gain_feedforward: float32 [1536], replicated, may hold values from 0.5 to 1.5
- gate_weight: bfloat16 [1536, 3968], P('wshard'), may hold values from -0.15625 to 0.15625
- up_weight: bfloat16 [1536, 3968], P('wshard'), may hold values from -0.15625 to 0.15625
- down_weight: bfloat16 [3968, 1536], P('wshard'), may hold values from -0.09375 to 0.09375
Outputs:
- outputs: bfloat16 [8192, 1536], P(('group', 'ctx', 'wshard'))
- input_grad: bfloat16 [8192, 1536], P(('group', 'ctx', 'wshard'))
- grad_gain_attention: float32 [1536], P(('ctx', 'wshard'))
- grad_query: float32 [1536, 768], P(('ctx', 'wshard'))
- grad_key: float32 [1536, 768], P(('ctx', 'wshard'))
- grad_value: float32 [1536, 768], P(('ctx', 'wshard'))
- grad_out: float32 [768, 1536], P(('ctx', 'wshard'))
- grad_bias: float32 [32, 12], replicated
- grad_gain_feedforward: float32 [1536], P(('ctx', 'wshard'))
- grad_gate: float32 [1536, 3968], P(('ctx', 'wshard'))
- grad_up: float32 [1536, 3968], P(('ctx', 'wshard'))
- grad_down: float32 [3968, 1536], P(None, ('ctx', 'wshard'))
The draws below stay inside these ranges and needn't reach their ends.
Inputs may be any that keep to these rules, and one draw needn't show every extreme that they name: `lengths`: each row sums to 1024; the largest entry is 512. `permutation`: each row holds every place of its group once.
All inputs are finite; a program needn't handle non-finite values.
Results may differ from the reference program's by a relative error of at most 0.02.
Values may be sent and summed in bfloat16 or wider, within the bound.
No kernel may reach another device: no remote copies, remote signals or barrier semaphores. Data moves between devices by JAX's collectives and lax.ppermute only.
A program may use at most 320 MiB of HBM per device.

```python
import math
import jax
import jax.numpy as jnp
import numpy as np
from jax import lax

D = 1536
H = 12
DK = 64
FF = 3968
NB = 32
SEQS = 4
HD = 768
GROUP_TOK = 1024
MAXLEN = 512
TOKENS = 8192
N_GROUP = 8


def block_scale(key, shape, pieces, least, high):
    gain, own = 1.0, jax.random.fold_in(key, 6)
    for dim, shards_of in pieces:
        draws = jnp.exp(jax.random.uniform(jax.random.fold_in(own, dim), (shards_of,), jnp.float32, least / len(pieces), high / len(pieces)))
        gain = gain * jnp.repeat(draws, shape[dim] // shards_of).reshape([-1 if axis == dim else 1 for axis in range(len(shape))])
    return gain


def profile(amount, total, limit, lean):
    weights = [(1 << 20) // math.isqrt(standing ** lean) + 1 for standing in range(2, amount + 1)]
    rest, counts = total - limit - (amount - 1), [1] * (amount - 1)
    while rest > 0:
        candidates = [i for i in range(amount - 1) if counts[i] < limit]
        pool, budget = sum([weights[i] for i in candidates]), rest
        for i in candidates:
            more = min(limit - counts[i], max(1, budget * weights[i] // pool), rest)
            counts[i] = counts[i] + more
            rest = rest - more
    return np.array([limit] + counts)


def ragged_sizes(stream_key, count, total, most, lean):
    if count == 2:
        one = jax.random.randint(stream_key, (), max(1, total - most), min(most, total - 1) + 1)
        return jnp.stack([one, total - one])
    sizes = jnp.asarray(profile(count, total, most, lean), jnp.int32)
    twos = (count - 1) // 2
    source_of, taker = sizes[1:1 + 2 * twos:2], sizes[2:2 + 2 * twos:2]
    margin = jnp.minimum(source_of - 1, most - taker)
    moved = jax.random.randint(jax.random.fold_in(stream_key, 1), (twos,), 0, 1 << 20) % (margin + 1)
    sizes = sizes.at[1:1 + 2 * twos:2].set(source_of - moved).at[2:2 + 2 * twos:2].set(taker + moved)
    return sizes[jax.random.permutation(jax.random.fold_in(stream_key, 2), count)]


def normal_values(rng, dims, deviation, reach, shards=(), held_as=jnp.bfloat16):
    loudness = block_scale(rng, dims, shards, -0.22, 0.18) if shards else 1.0
    drawn = jax.random.normal(rng, dims, jnp.float32) * deviation * loudness
    return jnp.minimum(jnp.maximum(drawn, -reach), reach).astype(held_as)


def setup_inputs(seed: int = 0) -> dict:
    key_list = jax.random.split(jax.random.key(seed), 15)
    inputs = normal_values(key_list[0], (TOKENS, D), 1.0, 6.0, ((0, 32),))
    out_grad = normal_values(key_list[1], (TOKENS, D), 1.0, 6.0, ((0, 32),))
    lengths = jax.vmap(lambda own: ragged_sizes(own, SEQS, GROUP_TOK, MAXLEN, 2))(jax.random.split(key_list[2], N_GROUP)).reshape((N_GROUP, SEQS)).astype(jnp.int32)
    permutation = jax.vmap(lambda own: jax.random.permutation(own, GROUP_TOK))(jax.random.split(key_list[3], N_GROUP)).reshape((N_GROUP, GROUP_TOK)).astype(jnp.int32)
    gain_attention = jnp.clip(1.0 + 0.1 * jax.random.normal(key_list[4], (D,), jnp.float32), 0.5, 1.5)
    query_weight = normal_values(key_list[5], (D, HD), (8 * D) ** -0.5, 0.0546875, ((0, 2),))
    key_weight = normal_values(key_list[6], (D, HD), (8 * D) ** -0.5, 0.0546875, ((0, 2),))
    value_weight = normal_values(key_list[7], (D, HD), D ** -0.5, 0.15625, ((0, 2),))
    out_weight = normal_values(key_list[8], (HD, D), (max(HD // 256, 1)) ** -0.5, 3.5, ((0, 2),))
    bucket_bias = normal_values(key_list[9], (NB, H), 1.0, 4.0, (), jnp.float32)
    gain_feedforward = jnp.clip(1.0 + 0.1 * jax.random.normal(key_list[10], (D,), jnp.float32), 0.5, 1.5)
    gate_weight = normal_values(key_list[11], (D, FF), D ** -0.5, 0.15625, ((0, 2),))
    up_weight = normal_values(key_list[12], (D, FF), D ** -0.5, 0.15625, ((0, 2),))
    down_weight = normal_values(key_list[13], (FF, D), FF ** -0.5, 0.09375, ((0, 2),))
    return {"inputs": inputs, "out_grad": out_grad, "lengths": lengths, "permutation": permutation, "gain_attention": gain_attention, "query_weight": query_weight, "key_weight": key_weight, "value_weight": value_weight, "out_weight": out_weight, "bucket_bias": bucket_bias, "gain_feedforward": gain_feedforward, "gate_weight": gate_weight, "up_weight": up_weight, "down_weight": down_weight}


epsilon = 1e-06
highest = lax.Precision.HIGHEST
thresholds = (12, 16, 23, 32, 46, 64, 91)

@jax.custom_vjp
def low(v):
    return lax.optimization_barrier(v.astype(jnp.bfloat16)).astype(jnp.float32)

@jax.custom_vjp
def low_back(v):
    return v

def low_keep(v):
    return (low(v), None)

def low_pass(kept, grad):
    return (grad,)

def back_keep(v):
    return (v, None)

def back_low(kept, grad):
    return (low(grad),)
low.defvjp(low_keep, low_pass)
low_back.defvjp(back_keep, back_low)

def bucket_of(offset):
    distance = jnp.abs(offset)
    beyond = 8 + sum(((distance >= border).astype(jnp.int32) for border in thresholds))
    near_far = jnp.where(distance < 8, distance, beyond)
    return (jnp.where(offset > 0, 16, 0) + near_far).astype(jnp.int32)

def rms_norm(values, gain_vector):
    return values * lax.rsqrt(lax.optimization_barrier(jnp.mean(values * values, axis=-1, keepdims=True)) + epsilon) * gain_vector

def matmul(left_side, right_side):
    return jnp.dot(left_side, right_side, precision=highest)

def attend_group(query_all, key_all, value_all, bucket_bias, lengths_row):
    seq_ends = jnp.cumsum(lengths_row).astype(jnp.int32)
    places = jnp.arange(GROUP_TOK, dtype=jnp.int32)
    sequence = lax.optimization_barrier(jnp.sum((places[:, None] >= seq_ends[None, :]).astype(jnp.int32), axis=1)).astype(jnp.int32)
    height = min(512, GROUP_TOK)

    @jax.checkpoint
    def one_block(block_start):
        block_query = lax.dynamic_slice_in_dim(query_all, block_start, height, 0)
        block_place = block_start + jnp.arange(height, dtype=jnp.int32)
        block_seq = lax.dynamic_slice_in_dim(sequence, block_start, height, 0)
        scores = jnp.einsum('qhd,khd->hqk', block_query, key_all, precision=highest)
        buckets = bucket_of(places[None, :] - block_place[:, None])
        scores = scores + jnp.transpose(jnp.take(bucket_bias, buckets, axis=0), (2, 0, 1))
        scores = low_back(scores)
        same_seq = (block_seq[:, None] == sequence[None, :])[None]
        scores = jnp.where(same_seq, scores, -1e+30)
        attn_probs = jax.nn.softmax(scores, axis=-1)
        return jnp.einsum('hqk,khd->qhd', low(attn_probs), value_all, precision=highest)
    starts = (jnp.arange(GROUP_TOK // height) * height).astype(jnp.int32)
    return lax.map(one_block, starts).reshape(GROUP_TOK, H, DK)

def forward(inputs, gain_attention, query_weight, key_weight, value_weight, out_weight, bucket_bias, gain_feedforward, gate_weight, up_weight, down_weight, lengths):
    normed = low(rms_norm(inputs, gain_attention))
    query_proj = low_back(low(matmul(normed, query_weight)))
    key_proj = low_back(low(matmul(normed, key_weight)))
    value_proj = low_back(low(matmul(normed, value_weight)))
    group_shape = (N_GROUP, GROUP_TOK, H, DK)

    def per_group(group_items):
        return attend_group(group_items[0], group_items[1], group_items[2], bucket_bias, group_items[3])
    attended = lax.map(per_group, (query_proj.reshape(group_shape), key_proj.reshape(group_shape), value_proj.reshape(group_shape), lengths))
    attended = low_back(low(attended.reshape(TOKENS, H * DK)))
    residual = inputs + low_back(matmul(attended, out_weight))
    normed_ff = low(rms_norm(residual, gain_feedforward))
    gate_proj = low_back(matmul(normed_ff, gate_weight))
    up_proj = low_back(matmul(normed_ff, up_weight))
    hidden = low(jax.nn.gelu(gate_proj, approximate=True) * up_proj)
    return residual + low_back(matmul(hidden, down_weight))

def inverse_row(order_row):
    return jnp.zeros((GROUP_TOK,), jnp.int32).at[order_row].set(jnp.arange(GROUP_TOK, dtype=jnp.int32))

def reference(inputs, out_grad, lengths, permutation, gain_attention, query_weight, key_weight, value_weight, out_weight, bucket_bias, gain_feedforward, gate_weight, up_weight, down_weight):
    inverse = jax.vmap(inverse_row)(permutation.astype(jnp.int32))
    arrived = inputs.astype(jnp.float32).reshape(N_GROUP, GROUP_TOK, D)
    ordered = jnp.take_along_axis(arrived, inverse[:, :, None], axis=1).reshape(TOKENS, D)

    def wrapped(*floats):
        return forward(*floats, lengths)
    primals = (ordered, gain_attention, query_weight.astype(jnp.float32), key_weight.astype(jnp.float32), value_weight.astype(jnp.float32), out_weight.astype(jnp.float32), bucket_bias, gain_feedforward, gate_weight.astype(jnp.float32), up_weight.astype(jnp.float32), down_weight.astype(jnp.float32))
    result, pull_back = jax.vjp(wrapped, *primals)
    gradients = pull_back(out_grad.astype(jnp.float32))
    return (result.astype(jnp.bfloat16), gradients[0].astype(jnp.bfloat16), gradients[1], gradients[2], gradients[3], gradients[4], gradients[5], gradients[6], gradients[7], gradients[8], gradients[9], gradients[10])
```

```python
import functools

import jax
import jax.numpy as jnp
from jax import lax
from jax.experimental import pallas as pl
from jax.experimental.pallas import tpu as pltpu
from jax.sharding import PartitionSpec as P

epsilon = 1e-06
highest = lax.Precision.HIGHEST
thresholds = (12, 16, 23, 32, 46, 64, 91)
masked_out = -1e30
bf16 = jnp.bfloat16
f32 = jnp.float32
peer_axes = ("ctx", "wshard")
vmem_bytes = 60 * 1024 * 1024

ladder_ring = (0, 2, 4, 6, 7, 5, 3, 1)


def bucket_of(offset):
    distance = jnp.abs(offset)
    beyond = 8 + sum(((distance >= border).astype(jnp.int32) for border in thresholds))
    near_far = jnp.where(distance < 8, distance, beyond)
    return jnp.where(offset > 0, 16, 0) + near_far


def rms_norm(values, gain_vector):
    return (
        values
        * lax.rsqrt(jnp.mean(values * values, axis=-1, keepdims=True) + epsilon)
        * gain_vector
    )


def dot(left_side, right_side, dims, precision=None):
    return lax.dot_general(
        left_side, right_side, (dims, ((), ())), precision=precision, preferred_element_type=f32
    )


def forward_product(left_side, right_side):
    return dot(left_side, right_side, ((1,), (0,)))


def backward_product(left_side, right_side):
    return dot(left_side, right_side, ((1,), (1,)))


def weight_product(left_side, right_side):
    return dot(left_side, right_side, ((0,), (0,)))


def iota(shape, dim):
    return lax.broadcasted_iota(jnp.int32, shape, dim)


def arrange_kernel(rows, count, me_ref, order_ref, gain_ref, weight_ref, *refs):
    blocks, (x_ref, normed_ref, qkv_ref) = refs[:-3], refs[-3:]
    me = me_ref[0]
    first = (me ^ pl.program_id(0)) * rows
    tokens = first + iota((rows, rows), 0)
    total = None
    for k in range(count):
        places = order_ref[pl.ds(me ^ k, 1), :]
        chosen = (places == tokens).astype(f32).astype(bf16)
        part = forward_product(chosen, blocks[k][...])
        total = part if total is None else total + part
    x_ref[...] = total.astype(bf16)
    normed = rms_norm(total, gain_ref[...]).astype(bf16)
    normed_ref[...] = normed
    qkv_ref[...] = forward_product(normed, weight_ref[...]).astype(bf16)


def bias_kernel(rows, heads_here, heads, buckets, me_ref, table_ref, out_ref):
    lanes = iota((8, 4 * rows), 1)
    ids = bucket_of(2 * rows - lanes)
    for h in range(heads_here):
        head = jnp.minimum(me_ref[0] * heads_here + h, heads - 1)
        base = jnp.zeros((8, 4 * rows), f32)
        for b in range(buckets):
            base = jnp.where(ids == b, table_ref[b, head], base)
        wide = jnp.broadcast_to(base[0:1], (rows, 4 * rows))
        rolled = pltpu.roll(wide, 0, 1, stride=1, stride_axis=0)
        out_ref[h, 0] = jnp.full((rows, rows), table_ref[buckets // 2 - 1, head], f32)
        out_ref[h, 4] = jnp.full((rows, rows), table_ref[buckets - 1, head], f32)
        for delta in (1, 0, -1):
            start = rows + rows * (1 - delta)
            out_ref[h, delta + 2] = rolled[:, start : start + rows]


def span_of(lengths_ref, seqs, first, last, rows, total):
    low, high, end = 0, total, 0
    ends = []
    for s in range(seqs):
        end = end + lengths_ref[s]
        ends.append(end)
    for s in range(seqs):
        low = jnp.where(ends[s] <= first, ends[s], low)
    for s in reversed(range(seqs)):
        high = jnp.where(ends[s] > last, ends[s], high)
    high = jnp.minimum(high, total)
    return ends, low // rows, (high + rows - 1) // rows


def sequence_ids(ends, first, shape, dim):
    places = first + iota(shape, dim)
    ids = jnp.zeros(shape, jnp.int32)
    for end in ends:
        ids = ids + (places >= end).astype(jnp.int32)
    return ids


def attend_kernel(
    rows, count, heads_here, size, seqs, me_ref, lengths_ref, qkv_ref, bias_ref, att_ref, wide_ref, lse_ref
):
    me = me_ref[0]
    width = heads_here * size
    here = pl.program_id(0)
    block = me ^ here
    ends, low, high = span_of(
        lengths_ref, seqs, block * rows, block * rows + rows - 1, rows, count * rows
    )
    query_seq = sequence_ids(ends, block * rows, (1, rows), 1)
    start = pl.multiple_of(here * rows, rows)
    queries = qkv_ref[pl.ds(start, rows), :][:, :width]
    for h in range(heads_here):
        query = queries[:, h * size : (h + 1) * size]

        def step(key_block, carry):
            top, total, acc = carry
            at = pl.multiple_of((key_block ^ me) * rows, rows)
            own = qkv_ref[pl.ds(at, rows), :]
            key = own[:, width + h * size : width + (h + 1) * size]
            value = own[:, 2 * width + h * size : 2 * width + (h + 1) * size]
            delta = jnp.clip(key_block - block, -2, 2) + 2
            scores = backward_product(key, query) + bias_ref[h, delta]
            key_seq = sequence_ids(ends, key_block * rows, (rows, 1), 0)
            scores = jnp.where(key_seq == query_seq, scores, masked_out)
            top_next = jnp.maximum(top, jnp.max(scores, axis=0, keepdims=True))
            probs = jnp.exp(scores - top_next)
            fade = jnp.exp(top - top_next)
            total = total * fade + jnp.sum(probs, axis=0, keepdims=True)
            acc = acc * fade + weight_product(value, probs.astype(bf16))
            return top_next, total, acc

        top, total, acc = lax.fori_loop(
            low,
            high,
            step,
            (
                jnp.full((1, rows), masked_out, f32),
                jnp.zeros((1, rows), f32),
                jnp.zeros((size, rows), f32),
            ),
        )
        lse_ref[h : h + 1, :] = top + jnp.log(total)
        out = (acc / total).T
        wide_ref[:, h * size : (h + 1) * size] = out
        att_ref[:, h * size : (h + 1) * size] = out.astype(bf16)


def attend_back_kernel(
    rows,
    count,
    heads_here,
    size,
    seqs,
    buckets,
    me_ref,
    lengths_ref,
    qkv_ref,
    bias_ref,
    lse_ref,
    delta_ref,
    d_att_ref,
    dqkv_ref,
    table_ref,
    dq_ref,
    sums_ref,
):
    me = me_ref[0]
    width = heads_here * size
    here = pl.program_id(0)
    block = me ^ here

    @pl.when(here == 0)
    def _():
        dq_ref[...] = jnp.zeros_like(dq_ref)
        sums_ref[...] = jnp.zeros_like(sums_ref)

    ends, low, high = span_of(
        lengths_ref, seqs, block * rows, block * rows + rows - 1, rows, count * rows
    )
    key_seq = sequence_ids(ends, block * rows, (rows, 1), 0)
    start = pl.multiple_of(here * rows, rows)
    own = qkv_ref[pl.ds(start, rows), :]
    for h in range(heads_here):
        key = own[:, width + h * size : width + (h + 1) * size]
        value = own[:, 2 * width + h * size : 2 * width + (h + 1) * size]

        def step(query_block, carry):
            d_key, d_value = carry
            rel = query_block ^ me
            at = pl.multiple_of(rel * rows, rows)
            query = qkv_ref[pl.ds(at, rows), :][:, h * size : (h + 1) * size]
            d_out = d_att_ref[pl.ds(at, rows), :][:, h * size : (h + 1) * size]
            near = jnp.clip(block - query_block, -2, 2) + 2
            scores = backward_product(key, query) + bias_ref[h, near]
            query_seq = sequence_ids(ends, query_block * rows, (1, rows), 1)
            lse = lse_ref[h : h + 1, pl.ds(at, rows)]
            soft = jnp.where(key_seq == query_seq, jnp.exp(scores - lse), 0.0)
            d_probs = backward_product(value, d_out)
            d_scores = (soft * (d_probs - delta_ref[h : h + 1, pl.ds(at, rows)])).astype(bf16)
            sums_ref[h, near] += d_scores.astype(f32)
            d_value = d_value + forward_product(soft.astype(bf16), d_out)
            d_key = d_key + forward_product(d_scores, query)
            dq_ref[h, rel] += weight_product(key, d_scores)
            return d_key, d_value

        zero = jnp.zeros((rows, size), f32)
        d_key, d_value = lax.fori_loop(low, high, step, (zero, zero))
        dqkv_ref[pl.ds(start, rows), width + h * size : width + (h + 1) * size] = d_key.astype(bf16)
        dqkv_ref[pl.ds(start, rows), 2 * width + h * size : 2 * width + (h + 1) * size] = (
            d_value.astype(bf16)
        )

    @pl.when(here == count - 1)
    def _():
        for h in range(heads_here):
            for k in range(count):
                dqkv_ref[k * rows : (k + 1) * rows, h * size : (h + 1) * size] = (
                    dq_ref[h, k].T.astype(bf16)
                )
        turned = (iota((rows, rows), 0) + iota((rows, rows), 1) == rows - 1).astype(f32)
        ids = bucket_of(2 * rows - 1 - iota((buckets, 4 * rows), 1))
        mine = ids == iota((buckets, 4 * rows), 0)
        bucket_rows = iota((buckets, 1), 0)
        lanes = iota((buckets, 128), 1)
        table = jnp.zeros((buckets, 128), f32)
        for h in range(heads_here):
            strip = jnp.concatenate(
                [forward_product_exact(turned, sums_ref[h, d]) for d in (3, 2, 1)]
                + [jnp.zeros((rows, rows), f32)],
                axis=1,
            )
            diagonals = jnp.sum(
                pltpu.roll(strip, 0, 1, stride=1, stride_axis=0), axis=0, keepdims=True
            )
            column = jnp.sum(jnp.where(mine, diagonals, 0.0), axis=1, keepdims=True)
            column = column + jnp.where(bucket_rows == buckets // 2 - 1, jnp.sum(sums_ref[h, 0]), 0.0)
            column = column + jnp.where(bucket_rows == buckets - 1, jnp.sum(sums_ref[h, 4]), 0.0)
            table = jnp.where(lanes == h, column, table)
        table_ref[...] = table


def forward_product_exact(left_side, right_side):
    return dot(left_side, right_side, ((1,), (0,)), highest)


def whole(shape):
    return pl.BlockSpec(shape, lambda *_: (0,) * len(shape))


def per_device(
    sizes,
    inputs,
    out_grad,
    lengths,
    permutation,
    gain_attention,
    query_weight,
    key_weight,
    value_weight,
    out_weight,
    bucket_bias,
    gain_feedforward,
    gate_weight,
    up_weight,
    down_weight,
):
    n_group, n_ctx, n_w = sizes
    n = n_ctx * n_w
    fast = (n_group, n_ctx, n_w) == (8, 2, 2)
    rows, model = inputs.shape
    buckets, heads = bucket_bias.shape
    hidden_units = gate_weight.shape[1]
    size = query_weight.shape[1] // heads
    seqs = lengths.shape[1]
    tokens = rows * n
    heads_here = -(-heads // n)
    width = heads_here * size
    units = -(-hidden_units // (128 * n)) * 128
    ctx, wsh = lax.axis_index("ctx"), lax.axis_index("wshard")
    me = lax.axis_index(peer_axes)
    rank = wsh * n_ctx + ctx
    flip_w = [(0, 1), (1, 0)]


    def mate(block):
        return lax.ppermute(block, "wshard", flip_w)

    def across(block):
        return lax.ppermute(block, "ctx", flip_w)

    def to_relative(stacked):
        return jnp.take(stacked, me ^ lax.iota(jnp.int32, n), axis=0)

    def gather_blocks(block):
        if fast:
            far = across(block)
            return [block, mate(block), far, mate(far)]
        stacked = to_relative(lax.all_gather(block, peer_axes, axis=0, tiled=False))
        return [stacked[k] for k in range(n)]

    def scatter_rows(partial):
        if fast:
            sent = partial.astype(bf16).reshape(n, rows, -1)
            pair = jnp.stack([sent[1], sent[3]])
            got = mate(pair)
            near = sent[0].astype(f32) + got[0].astype(f32)
            away = (sent[2].astype(f32) + got[1].astype(f32)).astype(bf16)
            return near + across(away).astype(f32)
        stacked = to_relative(partial.astype(bf16).reshape(n, rows, -1))
        return lax.psum_scatter(stacked, peer_axes, scatter_dimension=0, tiled=False).astype(f32)

    def columns_of(weight, which, wide):
        over = max(0, n * wide - weight.shape[1])
        padded = jnp.pad(weight, ((0, 0), (0, over))) if over else weight
        return lax.dynamic_slice_in_dim(padded, which * wide, wide, 1)

    def own_columns(parts, wide, own, mates):
        mine = jnp.concatenate([columns_of(part, own, wide) for part in parts], axis=1)
        given = mate(jnp.concatenate([columns_of(part, mates, wide) for part in parts], axis=1))
        upper = jnp.where(wsh == 0, mine, given)
        lower = jnp.where(wsh == 0, given, mine)
        return jnp.concatenate([upper, lower], axis=0)

    row_blocks = gather_blocks(inputs)
    qkv_weight = own_columns(
        (query_weight, key_weight, value_weight), width, me, ctx * n_w + (1 - wsh)
    )
    out_other = mate(out_weight)
    gate_up = own_columns((gate_weight, up_weight), units, rank, (1 - wsh) * n_ctx + ctx)
    half = down_weight.shape[0]
    extra = n_ctx * units - half
    down_other = mate(down_weight[:extra])
    down_wide = jnp.concatenate(
        [
            down_weight,
            jnp.where(wsh == 0, down_other, jnp.zeros_like(down_other)),
            jnp.zeros_like(down_other),
        ]
    )
    down_own = lax.dynamic_slice_in_dim(down_wide, wsh * extra + ctx * units, units, 0)
    dy = jnp.concatenate(gather_blocks(out_grad))
    out_full = jnp.concatenate(
        [jnp.where(wsh == 0, out_weight, out_other), jnp.where(wsh == 0, out_other, out_weight)]
    )
    out_full = jnp.pad(out_full, ((0, n * width - out_full.shape[0]), (0, 0)))
    out_blocks = [lax.dynamic_slice_in_dim(out_full, (me ^ k) * width, width, 0) for k in range(n)]

    me_1 = me.reshape(1).astype(jnp.int32)
    order = permutation.reshape(n, rows)
    params = pltpu.CompilerParams(vmem_limit_bytes=vmem_bytes)
    bias = pl.pallas_call(
        functools.partial(bias_kernel, rows, heads_here, heads, buckets),
        out_shape=jax.ShapeDtypeStruct((heads_here, 5, rows, rows), f32),
        in_specs=[
            pl.BlockSpec(memory_space=pltpu.SMEM),
            pl.BlockSpec(memory_space=pltpu.SMEM),
        ],
        out_specs=pl.BlockSpec(memory_space=pltpu.VMEM),
        compiler_params=params,
        name="bias_strips",
    )(me_1, bucket_bias)
    x_all, normed, qkv = pl.pallas_call(
        functools.partial(arrange_kernel, rows, n),
        out_shape=(
            jax.ShapeDtypeStruct((tokens, model), bf16),
            jax.ShapeDtypeStruct((tokens, model), bf16),
            jax.ShapeDtypeStruct((tokens, 3 * width), bf16),
        ),
        grid_spec=pltpu.PrefetchScalarGridSpec(
            num_scalar_prefetch=1,
            grid=(n,),
            in_specs=[whole((n, rows)), whole((1, model)), whole((model, 3 * width))]
            + [whole((rows, model))] * n,
            out_specs=[
                pl.BlockSpec((rows, model), lambda t, *_: (t, 0)),
                pl.BlockSpec((rows, model), lambda t, *_: (t, 0)),
                pl.BlockSpec((rows, 3 * width), lambda t, *_: (t, 0)),
            ],
        ),
        compiler_params=params,
        cost_estimate=pl.CostEstimate(
            flops=2 * tokens * model * (tokens + 3 * width),
            bytes_accessed=8 * tokens * model,
            transcendentals=0,
        ),
        name="arrange_project",
    )(me_1, order, gain_attention.reshape(1, model), qkv_weight, *row_blocks)
    lengths_row = lengths.reshape(seqs)
    attended, attended_wide, lse = pl.pallas_call(
        functools.partial(attend_kernel, rows, n, heads_here, size, seqs),
        out_shape=(
            jax.ShapeDtypeStruct((tokens, width), bf16),
            jax.ShapeDtypeStruct((tokens, width), f32),
            jax.ShapeDtypeStruct((heads_here, tokens), f32),
        ),
        grid_spec=pltpu.PrefetchScalarGridSpec(
            num_scalar_prefetch=2,
            grid=(n,),
            in_specs=[whole((tokens, 3 * width)), whole((heads_here, 5, rows, rows))],
            out_specs=[
                pl.BlockSpec((rows, width), lambda t, *_: (t, 0)),
                pl.BlockSpec((rows, width), lambda t, *_: (t, 0)),
                pl.BlockSpec((heads_here, rows), lambda t, *_: (0, t)),
            ],
        ),
        compiler_params=params,
        cost_estimate=pl.CostEstimate(
            flops=16 * tokens * tokens * width,
            bytes_accessed=16 * tokens * width,
            transcendentals=tokens * tokens * heads_here,
        ),
        name="attend",
    )(me_1, lengths_row, qkv, bias)

    attended_blocks = gather_blocks(attended)
    by_rows = [
        jnp.concatenate(
            [attended_blocks[k][(m ^ k) * rows : ((m ^ k) + 1) * rows] for m in range(n)]
        )
        for k in range(n)
    ]
    attended_all = jnp.concatenate(by_rows, axis=1)
    residual_all = x_all.astype(f32) + forward_product(
        attended_all, jnp.concatenate(out_blocks, axis=0)
    )
    residual = residual_all[:rows]
    normed_ff = rms_norm(residual_all, gain_feedforward).astype(bf16)
    gate_up_proj = forward_product(normed_ff, gate_up)
    gate_proj, up_proj = gate_up_proj[:, :units], gate_up_proj[:, units:]

    def activate(gate_in, up_in):
        return jax.nn.gelu(gate_in, approximate=True) * up_in

    hidden_wide, activate_back = jax.vjp(activate, gate_proj, up_proj)
    hidden = hidden_wide.astype(bf16)
    grad_down = weight_product(hidden, dy).astype(bf16)
    d_hidden = backward_product(dy, down_own)
    d_gate_wide, d_up_wide = activate_back(d_hidden)
    d_gate, d_up = d_gate_wide.astype(bf16), d_up_wide.astype(bf16)
    grad_gate = weight_product(normed_ff, d_gate).astype(bf16)
    grad_up = weight_product(normed_ff, d_up).astype(bf16)
    d_normed_ff = scatter_rows(
        backward_product(d_gate, gate_up[:, :units]) + backward_product(d_up, gate_up[:, units:])
    )
    outputs = (residual + scatter_rows(forward_product(hidden, down_own))).astype(bf16)

    norm_ff_back = jax.vjp(rms_norm, residual, gain_feedforward)[1]
    d_residual_norm, grad_gain_ff = norm_ff_back(d_normed_ff)
    d_residual = dy[:rows].astype(f32) + d_residual_norm
    d_branch = jnp.concatenate(gather_blocks(d_residual.astype(bf16)))
    d_attended = backward_product(d_branch, out_blocks[0]).astype(bf16)
    grad_out = weight_product(attended, d_branch).astype(bf16)
    delta = jnp.sum(
        (d_attended.astype(f32) * attended_wide).reshape(tokens, heads_here, size), axis=2
    ).T
    d_qkv, d_table = pl.pallas_call(
        functools.partial(attend_back_kernel, rows, n, heads_here, size, seqs, buckets),
        out_shape=(
            jax.ShapeDtypeStruct((tokens, 3 * width), bf16),
            jax.ShapeDtypeStruct((buckets, 128), f32),
        ),
        grid_spec=pltpu.PrefetchScalarGridSpec(
            num_scalar_prefetch=2,
            grid=(n,),
            in_specs=[
                whole((tokens, 3 * width)),
                whole((heads_here, 5, rows, rows)),
                whole((heads_here, tokens)),
                whole((heads_here, tokens)),
                whole((tokens, width)),
            ],
            out_specs=[whole((tokens, 3 * width)), whole((buckets, 128))],
            scratch_shapes=[
                pltpu.VMEM((heads_here, n, size, rows), f32),
                pltpu.VMEM((heads_here, 5, rows, rows), f32),
            ],
        ),
        compiler_params=params,
        cost_estimate=pl.CostEstimate(
            flops=40 * tokens * tokens * width,
            bytes_accessed=16 * tokens * width,
            transcendentals=tokens * tokens * heads_here,
        ),
        name="attend_back",
    )(me_1, lengths_row, qkv, bias, lse, delta, d_attended)
    grad_qkv = weight_product(normed, d_qkv).astype(bf16)
    d_normed = scatter_rows(backward_product(d_qkv, qkv_weight))
    norm_attn_back = jax.vjp(rms_norm, x_all[:rows].astype(f32), gain_attention)[1]
    d_input_norm, grad_gain_attn = norm_attn_back(d_normed)
    input_grad = (d_residual + d_input_norm).astype(bf16)

    table_here = jnp.pad(d_table[:, :heads_here], ((0, 0), (0, n * heads_here)))
    table_here = jnp.roll(table_here, me * heads_here, axis=1)[:, :heads]
    small = jnp.concatenate([grad_gain_attn, grad_gain_ff, table_here.reshape(-1)])
    if fast:
        for axis, bit, count in (
            ("wshard", 1, n_w),
            ("ctx", 1, n_ctx),
            ("group", 1, n_group),
            ("group", 2, n_group),
            ("group", 4, n_group),
        ):
            small = small + lax.ppermute(small, axis, [(g, g ^ bit) for g in range(count)])
    else:
        small = lax.psum(small, ("group",) + peer_axes)
    share = model // n
    gains = [lax.dynamic_slice_in_dim(small, k * model + me * share, share) for k in range(2)]
    grad_table = small[2 * model :].reshape(buckets, heads)

    if not fast:

        def place_columns(grad, which, wide, total):
            full = jnp.zeros((grad.shape[0], n * wide), bf16)
            full = lax.dynamic_update_slice_in_dim(full, grad, which * wide, 1)
            return full[:, :total]

        def finish(full, dim):
            full = lax.psum_scatter(full, peer_axes, scatter_dimension=dim, tiled=True)
            return lax.psum(full, "group").astype(f32)

        total_qkv = [
            finish(
                place_columns(grad_qkv[:, k * width : (k + 1) * width], me, width, heads * size), 0
            )
            for k in range(3)
        ]
        total_out = finish(place_columns(grad_out.T, me, width, heads * size).T, 0)
        total_gate = finish(place_columns(grad_gate, rank, units, hidden_units), 0)
        total_up = finish(place_columns(grad_up, rank, units, hidden_units), 0)
        total_down = finish(place_columns(grad_down.T, rank, units, hidden_units).T, 1)
    else:
        spot = jnp.asarray([ladder_ring.index(g) for g in range(n_group)], jnp.int32)[
            lax.axis_index("group")
        ]
        ahead = [(ladder_ring[k], ladder_ring[(k + 1) % n_group]) for k in range(n_group)]
        behind = [(b, a) for a, b in ahead]

        def piece(array, index, axis):
            index = lax.rem(index, n_group)
            return lax.squeeze(lax.dynamic_slice_in_dim(array, index, 1, axis), (axis,))

        def ring_scatter(halves, axis):
            one, two = piece(halves[0], spot + 7, axis), piece(halves[1], spot + 1, axis)
            for s in range(n_group - 1):
                one = lax.ppermute(one, "group", ahead) + piece(halves[0], spot + 14 - s, axis)
                two = lax.ppermute(two, "group", behind) + piece(halves[1], spot + 2 + s, axis)
            return one, two

        def ring_gather(one, two, out, write):
            out = write(out, one, spot, 0)
            out = write(out, two, spot, 1)
            for s in range(n_group - 1):
                one = lax.ppermute(one, "group", ahead)
                two = lax.ppermute(two, "group", behind)
                out = write(out, one, lax.rem(spot + 15 - s, n_group), 0)
                out = write(out, two, lax.rem(spot + 1 + s, n_group), 1)
            return out

        def exchange(block_for):
            return [
                block_for(0),
                mate(block_for(1)),
                across(block_for(2)),
                lax.ppermute(block_for(3), peer_axes, [(q, q ^ 3) for q in range(n)]),
            ]

        def rank_of(k):
            peer = me ^ k
            return (peer % n_w) * n_ctx + peer // n_w

        strip = model // n // n_group
        part = strip // 2

        def finish_columns(grad):
            cut = grad.reshape(n, n_group, 2, part, units)
            one, two = ring_scatter((cut[:, :, 0], cut[:, :, 1]), 1)
            both = jnp.stack([one, two], axis=1)
            came = exchange(lambda k: piece_at(both, me ^ k, 0))
            full = jnp.zeros((2, part, n * units), bf16)
            for k in range(n):
                full = lax.dynamic_update_slice_in_dim(full, came[k], rank_of(k) * units, 2)

            def write(out, block, at, h):
                return lax.dynamic_update_slice(
                    out, block[:, :hidden_units].astype(f32)[None, None], (at, h, 0, 0)
                )

            out = jnp.zeros((n_group, 2, part, hidden_units), f32)
            out = ring_gather(full[0], full[1], out, write)
            return out.reshape(model // n, hidden_units)

        def piece_at(array, index, axis):
            return lax.squeeze(lax.dynamic_slice_in_dim(array, index, 1, axis), (axis,))

        def finish_down(grad):
            step = units // n_group // 2
            cols = model // n
            cut = grad.reshape(n_group, 2, step, model)
            one, two = ring_scatter((cut[:, 0], cut[:, 1]), 0)
            both = jnp.stack([one, two])
            came = exchange(lambda k: lax.dynamic_slice_in_dim(both, (me ^ k) * cols, cols, 2))
            full = jnp.zeros((n, 2, step, cols), bf16)
            for k in range(n):
                full = lax.dynamic_update_slice_in_dim(full, came[k][None], rank_of(k), 0)

            def write(out, block, at, h):
                return lax.dynamic_update_slice(
                    out, block.astype(f32)[:, None, None], (0, at, h, 0, 0)
                )

            out = jnp.zeros((n, n_group, 2, step, cols), f32)
            out = ring_gather(full[:, 0], full[:, 1], out, write)
            return out.reshape(n * units, cols)[:hidden_units]

        def finish_qkv(grad):
            cut = grad.reshape(n, n_group, 2, part, 3 * width)
            one, two = ring_scatter((cut[:, :, 0], cut[:, :, 1]), 1)
            both = jnp.stack([one, two], axis=1)
            came = exchange(lambda k: piece_at(both, me ^ k, 0))
            full = jnp.zeros((2, part, 3, n * width), bf16)
            for k in range(n):
                full = lax.dynamic_update_slice_in_dim(
                    full, came[k].reshape(2, part, 3, width), (me ^ k) * width, 3
                )
            full = full.reshape(2, part, 3 * n * width)

            def write(outs, block, at, h):
                return [
                    lax.dynamic_update_slice(
                        out,
                        block[:, k * n * width : (k + 1) * n * width].astype(f32)[None, None],
                        (at, h, 0, 0),
                    )
                    for k, out in enumerate(outs)
                ]

            outs = [jnp.zeros((n_group, 2, part, n * width), f32) for _ in range(3)]
            outs = ring_gather(full[0], full[1], outs, write)
            return [out.reshape(model // n, n * width) for out in outs]

        def finish_out(grad):
            step, cols = width // n_group, model // 2
            cut = grad.reshape(n_group, step, model)
            one, two = ring_scatter((cut[:, :, :cols], cut[:, :, cols:]), 0)

            def write(out, block, at, h):
                return lax.dynamic_update_slice(out, block.astype(f32)[None], (at, 0, h * cols))

            out = ring_gather(one, two, jnp.zeros((n_group, step, model), f32), write)
            return out.reshape(width, model)

        total_down = finish_down(grad_down)
        total_gate = finish_columns(grad_gate)
        total_up = finish_columns(grad_up)
        total_out = finish_out(grad_out)
        total_qkv = finish_qkv(grad_qkv)
    return (
        outputs,
        input_grad,
        gains[0],
        total_qkv[0],
        total_qkv[1],
        total_qkv[2],
        total_out,
        grad_table,
        gains[1],
        total_gate,
        total_up,
        total_down,
    )


def solution(mesh):
    sizes = (mesh.shape["group"], mesh.shape["ctx"], mesh.shape["wshard"])
    return jax.shard_map(
        functools.partial(per_device, sizes),
        mesh=mesh,
        in_specs=(
            P(("group", "ctx", "wshard"), None),
            P(("group", "ctx", "wshard"), None),
            P("group", None),
            P("group", None),
            P(),
            P("wshard", None),
            P("wshard", None),
            P("wshard", None),
            P("wshard", None),
            P(),
            P(),
            P("wshard", None),
            P("wshard", None),
            P("wshard", None),
        ),
        out_specs=(
            P(("group", "ctx", "wshard"), None),
            P(("group", "ctx", "wshard"), None),
            P(("ctx", "wshard")),
            P(("ctx", "wshard"), None),
            P(("ctx", "wshard"), None),
            P(("ctx", "wshard"), None),
            P(("ctx", "wshard"), None),
            P(),
            P(("ctx", "wshard")),
            P(("ctx", "wshard"), None),
            P(("ctx", "wshard"), None),
            P(None, ("ctx", "wshard")),
        ),
        check_vma=False,
    )
```

```python
import functools

import jax
import jax.numpy as jnp
from jax import lax
from jax.experimental import pallas as pl
from jax.experimental.pallas import tpu as pltpu
from jax.sharding import PartitionSpec as P

epsilon = 1e-06
highest = lax.Precision.HIGHEST
thresholds = (12, 16, 23, 32, 46, 64, 91)
masked_out = -1e30
bf16 = jnp.bfloat16
f32 = jnp.float32
peer_axes = ("ctx", "wshard")
vmem_bytes = 60 * 1024 * 1024

ladder_ring = (0, 2, 4, 6, 7, 5, 3, 1)


def bucket_of(offset):
    distance = jnp.abs(offset)
    beyond = 8 + sum(((distance >= border).astype(jnp.int32) for border in thresholds))
    near_far = jnp.where(distance < 8, distance, beyond)
    return jnp.where(offset > 0, 16, 0) + near_far


def rms_norm(values, gain_vector):
    return (
        values
        * lax.rsqrt(jnp.mean(values * values, axis=-1, keepdims=True) + epsilon)
        * gain_vector
    )


def dot(left_side, right_side, dims, precision=None):
    return lax.dot_general(
        left_side, right_side, (dims, ((), ())), precision=precision, preferred_element_type=f32
    )


def forward_product(left_side, right_side):
    return dot(left_side, right_side, ((1,), (0,)))


def backward_product(left_side, right_side):
    return dot(left_side, right_side, ((1,), (1,)))


def weight_product(left_side, right_side):
    return dot(left_side, right_side, ((0,), (0,)))


def iota(shape, dim):
    return lax.broadcasted_iota(jnp.int32, shape, dim)


def arrange_kernel(rows, count, me_ref, order_ref, gain_ref, weight_ref, *refs):
    blocks, (x_ref, normed_ref, qkv_ref) = refs[:-3], refs[-3:]
    me = me_ref[0]
    first = (me ^ pl.program_id(0)) * rows
    tokens = first + iota((rows, rows), 0)
    total = None
    for k in range(count):
        places = order_ref[pl.ds(me ^ k, 1), :]
        chosen = (places == tokens).astype(f32).astype(bf16)
        part = forward_product(chosen, blocks[k][...])
        total = part if total is None else total + part
    x_ref[...] = total.astype(bf16)
    normed = rms_norm(total, gain_ref[...]).astype(bf16)
    normed_ref[...] = normed
    qkv_ref[...] = forward_product(normed, weight_ref[...]).astype(bf16)


def bias_kernel(rows, heads_here, heads, buckets, me_ref, table_ref, out_ref):
    lanes = iota((8, 4 * rows), 1)
    ids = bucket_of(2 * rows - lanes)
    for h in range(heads_here):
        head = jnp.minimum(me_ref[0] * heads_here + h, heads - 1)
        base = jnp.zeros((8, 4 * rows), f32)
        for b in range(buckets):
            base = jnp.where(ids == b, table_ref[b, head], base)
        wide = jnp.broadcast_to(base[0:1], (rows, 4 * rows))
        rolled = pltpu.roll(wide, 0, 1, stride=1, stride_axis=0)
        out_ref[h, 0] = jnp.full((rows, rows), table_ref[buckets // 2 - 1, head], f32)
        out_ref[h, 4] = jnp.full((rows, rows), table_ref[buckets - 1, head], f32)
        for delta in (1, 0, -1):
            start = rows + rows * (1 - delta)
            out_ref[h, delta + 2] = rolled[:, start : start + rows]


def span_of(lengths_ref, seqs, first, last, rows, total):
    low, high, end = 0, total, 0
    ends = []
    for s in range(seqs):
        end = end + lengths_ref[s]
        ends.append(end)
    for s in range(seqs):
        low = jnp.where(ends[s] <= first, ends[s], low)
    for s in reversed(range(seqs)):
        high = jnp.where(ends[s] > last, ends[s], high)
    high = jnp.minimum(high, total)
    return ends, low // rows, (high + rows - 1) // rows


def sequence_ids(ends, first, shape, dim):
    places = first + iota(shape, dim)
    ids = jnp.zeros(shape, jnp.int32)
    for end in ends:
        ids = ids + (places >= end).astype(jnp.int32)
    return ids


def attend_kernel(
    rows, count, heads_here, size, seqs, me_ref, lengths_ref, qkv_ref, bias_ref, att_ref, wide_ref, lse_ref
):
    me = me_ref[0]
    width = heads_here * size
    here = pl.program_id(0)
    block = me ^ here
    ends, low, high = span_of(
        lengths_ref, seqs, block * rows, block * rows + rows - 1, rows, count * rows
    )
    query_seq = sequence_ids(ends, block * rows, (1, rows), 1)
    start = pl.multiple_of(here * rows, rows)
    queries = qkv_ref[pl.ds(start, rows), :][:, :width]
    for h in range(heads_here):
        query = queries[:, h * size : (h + 1) * size]

        def step(key_block, carry):
            top, total, acc = carry
            at = pl.multiple_of((key_block ^ me) * rows, rows)
            own = qkv_ref[pl.ds(at, rows), :]
            key = own[:, width + h * size : width + (h + 1) * size]
            value = own[:, 2 * width + h * size : 2 * width + (h + 1) * size]
            delta = jnp.clip(key_block - block, -2, 2) + 2
            scores = backward_product(key, query) + bias_ref[h, delta]
            key_seq = sequence_ids(ends, key_block * rows, (rows, 1), 0)
            scores = jnp.where(key_seq == query_seq, scores, masked_out)
            top_next = jnp.maximum(top, jnp.max(scores, axis=0, keepdims=True))
            probs = jnp.exp(scores - top_next)
            fade = jnp.exp(top - top_next)
            total = total * fade + jnp.sum(probs, axis=0, keepdims=True)
            acc = acc * fade + weight_product(value, probs.astype(bf16))
            return top_next, total, acc

        top, total, acc = lax.fori_loop(
            low,
            high,
            step,
            (
                jnp.full((1, rows), masked_out, f32),
                jnp.zeros((1, rows), f32),
                jnp.zeros((size, rows), f32),
            ),
        )
        lse_ref[h : h + 1, :] = top + jnp.log(total)
        out = (acc / total).T
        wide_ref[:, h * size : (h + 1) * size] = out
        att_ref[:, h * size : (h + 1) * size] = out.astype(bf16)


def attend_back_kernel(
    rows,
    count,
    heads_here,
    size,
    seqs,
    buckets,
    me_ref,
    lengths_ref,
    qkv_ref,
    bias_ref,
    lse_ref,
    delta_ref,
    d_att_ref,
    dqkv_ref,
    table_ref,
    dq_ref,
    sums_ref,
):
    me = me_ref[0]
    width = heads_here * size
    here = pl.program_id(0)
    block = me ^ here

    @pl.when(here == 0)
    def _():
        dq_ref[...] = jnp.zeros_like(dq_ref)
        sums_ref[...] = jnp.zeros_like(sums_ref)

    ends, low, high = span_of(
        lengths_ref, seqs, block * rows, block * rows + rows - 1, rows, count * rows
    )
    key_seq = sequence_ids(ends, block * rows, (rows, 1), 0)
    start = pl.multiple_of(here * rows, rows)
    own = qkv_ref[pl.ds(start, rows), :]
    for h in range(heads_here):
        key = own[:, width + h * size : width + (h + 1) * size]
        value = own[:, 2 * width + h * size : 2 * width + (h + 1) * size]

        def step(query_block, carry):
            d_key, d_value = carry
            rel = query_block ^ me
            at = pl.multiple_of(rel * rows, rows)
            query = qkv_ref[pl.ds(at, rows), :][:, h * size : (h + 1) * size]
            d_out = d_att_ref[pl.ds(at, rows), :][:, h * size : (h + 1) * size]
            near = jnp.clip(block - query_block, -2, 2) + 2
            scores = backward_product(key, query) + bias_ref[h, near]
            query_seq = sequence_ids(ends, query_block * rows, (1, rows), 1)
            lse = lse_ref[h : h + 1, pl.ds(at, rows)]
            soft = jnp.where(key_seq == query_seq, jnp.exp(scores - lse), 0.0)
            d_probs = backward_product(value, d_out)
            d_scores = (soft * (d_probs - delta_ref[h : h + 1, pl.ds(at, rows)])).astype(bf16)
            sums_ref[h, near] += d_scores.astype(f32)
            d_value = d_value + forward_product(soft.astype(bf16), d_out)
            d_key = d_key + forward_product(d_scores, query)
            dq_ref[h, rel] += weight_product(key, d_scores)
            return d_key, d_value

        zero = jnp.zeros((rows, size), f32)
        d_key, d_value = lax.fori_loop(low, high, step, (zero, zero))
        dqkv_ref[pl.ds(start, rows), width + h * size : width + (h + 1) * size] = d_key.astype(bf16)
        dqkv_ref[pl.ds(start, rows), 2 * width + h * size : 2 * width + (h + 1) * size] = (
            d_value.astype(bf16)
        )

    @pl.when(here == count - 1)
    def _():
        for h in range(heads_here):
            for k in range(count):
                dqkv_ref[k * rows : (k + 1) * rows, h * size : (h + 1) * size] = (
                    dq_ref[h, k].T.astype(bf16)
                )
        turned = (iota((rows, rows), 0) + iota((rows, rows), 1) == rows - 1).astype(f32)
        ids = bucket_of(2 * rows - 1 - iota((buckets, 4 * rows), 1))
        mine = ids == iota((buckets, 4 * rows), 0)
        bucket_rows = iota((buckets, 1), 0)
        lanes = iota((buckets, 128), 1)
        table = jnp.zeros((buckets, 128), f32)
        for h in range(heads_here):
            strip = jnp.concatenate(
                [forward_product_exact(turned, sums_ref[h, d]) for d in (3, 2, 1)]
                + [jnp.zeros((rows, rows), f32)],
                axis=1,
            )
            diagonals = jnp.sum(
                pltpu.roll(strip, 0, 1, stride=1, stride_axis=0), axis=0, keepdims=True
            )
            column = jnp.sum(jnp.where(mine, diagonals, 0.0), axis=1, keepdims=True)
            column = column + jnp.where(bucket_rows == buckets // 2 - 1, jnp.sum(sums_ref[h, 0]), 0.0)
            column = column + jnp.where(bucket_rows == buckets - 1, jnp.sum(sums_ref[h, 4]), 0.0)
            table = jnp.where(lanes == h, column, table)
        table_ref[...] = table


def forward_product_exact(left_side, right_side):
    return dot(left_side, right_side, ((1,), (0,)), highest)


def whole(shape):
    return pl.BlockSpec(shape, lambda *_: (0,) * len(shape))


def per_device(
    sizes,
    inputs,
    out_grad,
    lengths,
    permutation,
    gain_attention,
    query_weight,
    key_weight,
    value_weight,
    out_weight,
    bucket_bias,
    gain_feedforward,
    gate_weight,
    up_weight,
    down_weight,
):
    n_group, n_ctx, n_w = sizes
    n = n_ctx * n_w
    fast = (n_group, n_ctx, n_w) == (8, 2, 2)
    rows, model = inputs.shape
    buckets, heads = bucket_bias.shape
    hidden_units = gate_weight.shape[1]
    size = query_weight.shape[1] // heads
    seqs = lengths.shape[1]
    tokens = rows * n
    heads_here = -(-heads // n)
    width = heads_here * size
    units = -(-hidden_units // (128 * n)) * 128
    ctx, wsh = lax.axis_index("ctx"), lax.axis_index("wshard")
    me = lax.axis_index(peer_axes)
    rank = wsh * n_ctx + ctx
    flip_w = [(0, 1), (1, 0)]


    def mate(block):
        return lax.ppermute(block, "wshard", flip_w)

    def across(block):
        return lax.ppermute(block, "ctx", flip_w)

    def to_relative(stacked):
        return jnp.take(stacked, me ^ lax.iota(jnp.int32, n), axis=0)

    def gather_blocks(block):
        if fast:
            far = across(block)
            return [block, mate(block), far, mate(far)]
        stacked = to_relative(lax.all_gather(block, peer_axes, axis=0, tiled=False))
        return [stacked[k] for k in range(n)]

    def columns_of(weight, which, wide):
        over = max(0, n * wide - weight.shape[1])
        padded = jnp.pad(weight, ((0, 0), (0, over))) if over else weight
        return lax.dynamic_slice_in_dim(padded, which * wide, wide, 1)

    def own_columns(parts, wide, own, mates):
        mine = jnp.concatenate([columns_of(part, own, wide) for part in parts], axis=1)
        given = mate(jnp.concatenate([columns_of(part, mates, wide) for part in parts], axis=1))
        upper = jnp.where(wsh == 0, mine, given)
        lower = jnp.where(wsh == 0, given, mine)
        return jnp.concatenate([upper, lower], axis=0)

    row_blocks = gather_blocks(inputs)
    far_first, out_grad = lax.optimization_barrier((row_blocks[2], out_grad))
    qkv_weight = own_columns(
        (query_weight, key_weight, value_weight), width, me, ctx * n_w + (1 - wsh)
    )
    out_other = mate(out_weight)
    gate_up = own_columns((gate_weight, up_weight), units, rank, (1 - wsh) * n_ctx + ctx)
    half = down_weight.shape[0]
    extra = n_ctx * units - half
    down_other = mate(down_weight[:extra])
    down_wide = jnp.concatenate(
        [
            down_weight,
            jnp.where(wsh == 0, down_other, jnp.zeros_like(down_other)),
            jnp.zeros_like(down_other),
        ]
    )
    down_own = lax.dynamic_slice_in_dim(down_wide, wsh * extra + ctx * units, units, 0)
    dy = jnp.concatenate(gather_blocks(out_grad))
    out_full = jnp.concatenate(
        [jnp.where(wsh == 0, out_weight, out_other), jnp.where(wsh == 0, out_other, out_weight)]
    )
    out_full = jnp.pad(out_full, ((0, n * width - out_full.shape[0]), (0, 0)))
    out_blocks = [lax.dynamic_slice_in_dim(out_full, (me ^ k) * width, width, 0) for k in range(n)]

    me_1 = me.reshape(1).astype(jnp.int32)
    order = permutation.reshape(n, rows)
    params = pltpu.CompilerParams(vmem_limit_bytes=vmem_bytes)
    bias = pl.pallas_call(
        functools.partial(bias_kernel, rows, heads_here, heads, buckets),
        out_shape=jax.ShapeDtypeStruct((heads_here, 5, rows, rows), f32),
        in_specs=[
            pl.BlockSpec(memory_space=pltpu.SMEM),
            pl.BlockSpec(memory_space=pltpu.SMEM),
        ],
        out_specs=pl.BlockSpec(memory_space=pltpu.VMEM),
        compiler_params=params,
        name="bias_strips",
    )(me_1, bucket_bias)
    x_all, normed, qkv = pl.pallas_call(
        functools.partial(arrange_kernel, rows, n),
        out_shape=(
            jax.ShapeDtypeStruct((tokens, model), bf16),
            jax.ShapeDtypeStruct((tokens, model), bf16),
            jax.ShapeDtypeStruct((tokens, 3 * width), bf16),
        ),
        grid_spec=pltpu.PrefetchScalarGridSpec(
            num_scalar_prefetch=1,
            grid=(n,),
            in_specs=[whole((n, rows)), whole((1, model)), whole((model, 3 * width))]
            + [whole((rows, model))] * n,
            out_specs=[
                pl.BlockSpec((rows, model), lambda t, *_: (t, 0)),
                pl.BlockSpec((rows, model), lambda t, *_: (t, 0)),
                pl.BlockSpec((rows, 3 * width), lambda t, *_: (t, 0)),
            ],
        ),
        compiler_params=params,
        cost_estimate=pl.CostEstimate(
            flops=2 * tokens * model * (tokens + 3 * width),
            bytes_accessed=8 * tokens * model,
            transcendentals=0,
        ),
        name="arrange_project",
    )(me_1, order, gain_attention.reshape(1, model), qkv_weight, *row_blocks)
    lengths_row = lengths.reshape(seqs)
    attended, attended_wide, lse = pl.pallas_call(
        functools.partial(attend_kernel, rows, n, heads_here, size, seqs),
        out_shape=(
            jax.ShapeDtypeStruct((tokens, width), bf16),
            jax.ShapeDtypeStruct((tokens, width), f32),
            jax.ShapeDtypeStruct((heads_here, tokens), f32),
        ),
        grid_spec=pltpu.PrefetchScalarGridSpec(
            num_scalar_prefetch=2,
            grid=(n,),
            in_specs=[whole((tokens, 3 * width)), whole((heads_here, 5, rows, rows))],
            out_specs=[
                pl.BlockSpec((rows, width), lambda t, *_: (t, 0)),
                pl.BlockSpec((rows, width), lambda t, *_: (t, 0)),
                pl.BlockSpec((heads_here, rows), lambda t, *_: (0, t)),
            ],
        ),
        compiler_params=params,
        cost_estimate=pl.CostEstimate(
            flops=16 * tokens * tokens * width,
            bytes_accessed=16 * tokens * width,
            transcendentals=tokens * tokens * heads_here,
        ),
        name="attend",
    )(me_1, lengths_row, qkv, bias)

    strip = model // n // n_group
    part = strip // 2
    if fast:
        group = lax.axis_index("group")
        spot = jnp.where(group % 2 == 0, group // 2, n_group - 1 - group // 2)
        ahead = [(ladder_ring[k], ladder_ring[(k + 1) % n_group]) for k in range(n_group)]
        behind = [(b, a) for a, b in ahead]

    def forward(block):
        return lax.ppermute(block, "group", ahead)

    def backward(block):
        return lax.ppermute(block, "group", behind)

    def diagonal(block):
        return lax.ppermute(block, peer_axes, [(q, q ^ 3) for q in range(n)])

    def pick(array, index, axis):
        return lax.squeeze(lax.dynamic_slice_in_dim(array, index, 1, axis), (axis,))

    def rank_of(k):
        peer = me ^ k
        return (peer % n_w) * n_ctx + peer // n_w

    def ring(take, swap, write):
        both_ways = (forward, backward)
        one, two = take(0, lax.rem(spot + 7, n_group)), take(1, lax.rem(spot + 1, n_group))
        for s in range(n_group - 1):
            came = yield (one, two), both_ways
            one = came[0] + take(0, lax.rem(spot + 14 - s, n_group))
            two = came[1] + take(1, lax.rem(spot + 2 + s, n_group))
        blocks, join = swap(jnp.stack([one, two], axis=1))
        came = yield tuple(blocks[1:]), (mate, across, diagonal)
        one, two = join([blocks[0], *came])
        out = write(write(None, one, spot, 0), two, spot, 1)
        for s in range(n_group - 1):
            one, two = yield (one, two), both_ways
            out = write(out, one, lax.rem(spot + 15 - s, n_group), 0)
            out = write(out, two, lax.rem(spot + 1 + s, n_group), 1)
        return out

    class Stream:
        def __init__(self, steps):
            self.steps, self.result = steps, None
            self.pending = next(steps)

        def advance(self, came):
            try:
                self.pending = self.steps.send(came)
            except StopIteration as stop:
                self.pending, self.result = None, stop.value

    def tick(values, *streams):
        live = [stream for stream in streams if stream is not None and stream.pending is not None]
        if not live:
            return values
        operands, values = lax.optimization_barrier(
            ([stream.pending[0] for stream in live], values)
        )
        for stream, sent in zip(live, operands):
            stream.advance([send(x) for send, x in zip(stream.pending[1], sent)])
        return values

    def rows_cut(grad):
        return grad.reshape(n, n_group, 2, part, grad.shape[1])

    def put(out, block, at, h):
        if out is None:
            out = jnp.zeros((n_group, 2) + block.shape, block.dtype)
        return lax.dynamic_update_slice(out, block[None, None], (at, h) + (0,) * block.ndim)

    def wide_ring(grad_gate_up, grad_down):
        one, two = rows_cut(grad_gate_up), rows_cut(grad_down)
        kinds = 3

        def take(h, index):
            return jnp.concatenate(
                [pick(one[:, :, h], index, 1), pick(two[:, :, h], index, 1)], axis=-1
            )

        def swap(both):
            def join(came):
                full = jnp.zeros((2, part, kinds * n * units), bf16)
                for k in range(n):
                    for t in range(kinds):
                        full = lax.dynamic_update_slice_in_dim(
                            full,
                            came[k][:, :, t * units : (t + 1) * units],
                            t * n * units + rank_of(k) * units,
                            2,
                        )
                return full[0], full[1]

            return [pick(both, me ^ k, 0) for k in range(n)], join

        def write(outs, block, at, h):
            outs = outs or [None] * kinds
            cuts = [block[:, t * n * units :][:, :hidden_units] for t in range(kinds)]
            cuts = [cuts[0].astype(f32), cuts[1].astype(f32), cuts[2]]
            return [put(out, cut, at, h) for out, cut in zip(outs, cuts)]

        return ring(take, swap, write)

    def small_ring(grad_qkv, grad_out):
        grad = rows_cut(jnp.concatenate([grad_qkv, grad_out], axis=1))

        def take(h, index):
            return pick(grad[:, :, h], index, 1)

        def swap(both):
            own = jnp.concatenate([both[k, :, :, 3 * width :] for k in range(n)], axis=2)

            def join(came):
                stacked = jnp.stack(came)
                came = [pick(stacked, me ^ r, 0) for r in range(n)]
                full = jnp.concatenate(
                    [came[r][:, :, k * width : (k + 1) * width] for k in range(3) for r in range(n)]
                    + [own],
                    axis=2,
                )
                return full[0], full[1]

            return [pick(both, me ^ k, 0)[:, :, : 3 * width] for k in range(n)], join

        def write(outs, block, at, h):
            outs = outs or [None] * 4
            across_heads = n * width
            cuts = [
                block[:, k * across_heads : (k + 1) * across_heads].astype(f32) for k in range(4)
            ]
            return [put(out, cut, at, h) for out, cut in zip(outs, cuts)]

        return ring(take, swap, write)

    def sum_ring(small):
        for axis, bit, count in (
            ("wshard", 1, n_w),
            ("ctx", 1, n_ctx),
            ("group", 1, n_group),
            ("group", 2, n_group),
            ("group", 4, n_group),
        ):
            pairs = [(g, g ^ bit) for g in range(count)]
            came = yield (small,), (lambda x: lax.ppermute(x, axis, pairs),)
            small = small + came[0]
        return small

    def scatter_near(partial):
        sent = partial.reshape(n, rows, -1)
        if not fast:
            total = lax.psum_scatter(to_relative(sent), peer_axes, scatter_dimension=0, tiled=False)
            return total.astype(f32), None
        got = mate(jnp.stack([sent[1], sent[3]]))
        near = sent[0].astype(f32) + got[0].astype(f32)
        return near, (sent[2].astype(f32) + got[1].astype(f32)).astype(bf16)

    def scatter_far(near, away):
        return near + across(away).astype(f32) if fast else near

    attended_blocks = gather_blocks(attended)
    by_rows = [
        jnp.concatenate(
            [attended_blocks[k][(m ^ k) * rows : ((m ^ k) + 1) * rows] for m in range(n)]
        )
        for k in range(n)
    ]
    attended_all = jnp.concatenate(by_rows, axis=1)
    residual_all = x_all.astype(f32) + forward_product(
        attended_all, jnp.concatenate(out_blocks, axis=0)
    )
    residual = residual_all[:rows]
    normed_ff = rms_norm(residual_all, gain_feedforward).astype(bf16)
    gate_up_proj = forward_product(normed_ff, gate_up)
    gate_proj, up_proj = gate_up_proj[:, :units], gate_up_proj[:, units:]

    def activate(gate_in, up_in):
        return jax.nn.gelu(gate_in, approximate=True) * up_in

    hidden_wide, activate_back = jax.vjp(activate, gate_proj, up_proj)
    hidden = hidden_wide.astype(bf16)
    d_hidden = backward_product(dy, down_own)
    d_gate_wide, d_up_wide = activate_back(d_hidden)
    d_gate_up = jnp.concatenate([d_gate_wide.astype(bf16), d_up_wide.astype(bf16)], axis=1)
    grad_gate_up = weight_product(normed_ff, d_gate_up).astype(bf16)
    grad_down = weight_product(dy, hidden).astype(bf16)
    wide = Stream(wide_ring(grad_gate_up, grad_down)) if fast else None
    d_gate_up, hidden = tick((d_gate_up, hidden), wide)

    back = backward_product(d_gate_up, gate_up).astype(bf16)
    back, hidden = tick((back, hidden), wide)
    near, away = scatter_near(back)
    out_partial = forward_product(hidden, down_own).astype(bf16)
    near, away, out_partial = tick((near, away, out_partial), wide)
    d_normed_ff = scatter_far(near, away)
    out_near, out_away = scatter_near(out_partial)
    out_near, out_away = tick((out_near, out_away), wide)
    norm_ff_back = jax.vjp(rms_norm, residual, gain_feedforward)[1]
    d_residual_norm, grad_gain_ff = norm_ff_back(d_normed_ff)
    d_residual = dy[:rows].astype(f32) + d_residual_norm
    branch = d_residual.astype(bf16)
    branch, out_away = tick((branch, out_away), wide)
    if fast:
        branch_far, branch_mate = across(branch), mate(branch)
        (branch_mate,) = tick((branch_mate,), wide)
        branch_far, out_away = tick((branch_far, out_away), wide)
        branch_blocks = [branch, branch_mate, branch_far, mate(branch_far)]
    else:
        branch_blocks = gather_blocks(branch)
    outputs = (residual + scatter_far(out_near, out_away)).astype(bf16)

    d_branch = jnp.concatenate(branch_blocks)
    d_attended = backward_product(d_branch, out_blocks[0]).astype(bf16)
    delta = jnp.sum(
        (d_attended.astype(f32) * attended_wide).reshape(tokens, heads_here, size), axis=2
    ).T
    d_attended, delta = tick((d_attended, delta), wide)
    d_qkv, d_table = pl.pallas_call(
        functools.partial(attend_back_kernel, rows, n, heads_here, size, seqs, buckets),
        out_shape=(
            jax.ShapeDtypeStruct((tokens, 3 * width), bf16),
            jax.ShapeDtypeStruct((buckets, 128), f32),
        ),
        grid_spec=pltpu.PrefetchScalarGridSpec(
            num_scalar_prefetch=2,
            grid=(n,),
            in_specs=[
                whole((tokens, 3 * width)),
                whole((heads_here, 5, rows, rows)),
                whole((heads_here, tokens)),
                whole((heads_here, tokens)),
                whole((tokens, width)),
            ],
            out_specs=[whole((tokens, 3 * width)), whole((buckets, 128))],
            scratch_shapes=[
                pltpu.VMEM((heads_here, n, size, rows), f32),
                pltpu.VMEM((heads_here, 5, rows, rows), f32),
            ],
        ),
        compiler_params=params,
        cost_estimate=pl.CostEstimate(
            flops=40 * tokens * tokens * width,
            bytes_accessed=16 * tokens * width,
            transcendentals=tokens * tokens * heads_here,
        ),
        name="attend_back",
    )(me_1, lengths_row, qkv, bias, lse, delta, d_attended)
    d_qkv, d_branch = tick((d_qkv, d_branch), wide)
    grad_qkv = weight_product(normed, d_qkv).astype(bf16)
    grad_out = weight_product(d_branch, attended).astype(bf16)
    narrow = Stream(small_ring(grad_qkv, grad_out)) if fast else None
    (d_qkv,) = tick((d_qkv,), wide, narrow)

    back = backward_product(d_qkv, qkv_weight).astype(bf16)
    (back,) = tick((back,), narrow)
    near, away = scatter_near(back)
    near, away = tick((near, away), wide, narrow)
    d_normed = scatter_far(near, away)
    (d_normed,) = tick((d_normed,), narrow)
    norm_attn_back = jax.vjp(rms_norm, x_all[:rows].astype(f32), gain_attention)[1]
    d_input_norm, grad_gain_attn = norm_attn_back(d_normed)
    input_grad = (d_residual + d_input_norm).astype(bf16)

    table_here = jnp.pad(d_table[:, :heads_here], ((0, 0), (0, n * heads_here)))
    table_here = jnp.roll(table_here, me * heads_here, axis=1)[:, :heads]
    small = jnp.concatenate([grad_gain_attn, grad_gain_ff, table_here.reshape(-1)])
    if fast:
        sums = Stream(sum_ring(small))
        while wide.pending or narrow.pending or sums.pending:
            tick((), wide, narrow, sums)
            tick((), narrow)
        small = sums.result
    else:
        small = lax.psum(small, ("group",) + peer_axes)
    share = model // n
    gains = [lax.dynamic_slice_in_dim(small, k * model + me * share, share) for k in range(2)]
    grad_table = small[2 * model :].reshape(buckets, heads)

    if fast:
        total_gate, total_up = [x.reshape(model // n, hidden_units) for x in wide.result[:2]]
        total_down = wide.result[2].reshape(model // n, hidden_units).T.astype(f32)
        total_qkv = [x.reshape(model // n, n * width) for x in narrow.result[:3]]
        total_out = narrow.result[3].reshape(-1, n, width).transpose(2, 1, 0).reshape(width, model)
    else:

        def place_columns(grad, which, wide, total):
            full = jnp.zeros((grad.shape[0], n * wide), bf16)
            full = lax.dynamic_update_slice_in_dim(full, grad, which * wide, 1)
            return full[:, :total]

        def finish(full, dim):
            full = lax.psum_scatter(full, peer_axes, scatter_dimension=dim, tiled=True)
            return lax.psum(full, "group").astype(f32)

        total_qkv = [
            finish(
                place_columns(grad_qkv[:, k * width : (k + 1) * width], me, width, heads * size), 0
            )
            for k in range(3)
        ]
        total_out = finish(place_columns(grad_out, me, width, heads * size).T, 0)
        total_gate = finish(place_columns(grad_gate_up[:, :units], rank, units, hidden_units), 0)
        total_up = finish(place_columns(grad_gate_up[:, units:], rank, units, hidden_units), 0)
        total_down = finish(place_columns(grad_down, rank, units, hidden_units).T, 1)
    return (
        outputs,
        input_grad,
        gains[0],
        total_qkv[0],
        total_qkv[1],
        total_qkv[2],
        total_out,
        grad_table,
        gains[1],
        total_gate,
        total_up,
        total_down,
    )


def solution(mesh):
    sizes = (mesh.shape["group"], mesh.shape["ctx"], mesh.shape["wshard"])
    return jax.shard_map(
        functools.partial(per_device, sizes),
        mesh=mesh,
        in_specs=(
            P(("group", "ctx", "wshard"), None),
            P(("group", "ctx", "wshard"), None),
            P("group", None),
            P("group", None),
            P(),
            P("wshard", None),
            P("wshard", None),
            P("wshard", None),
            P("wshard", None),
            P(),
            P(),
            P("wshard", None),
            P("wshard", None),
            P("wshard", None),
        ),
        out_specs=(
            P(("group", "ctx", "wshard"), None),
            P(("group", "ctx", "wshard"), None),
            P(("ctx", "wshard")),
            P(("ctx", "wshard"), None),
            P(("ctx", "wshard"), None),
            P(("ctx", "wshard"), None),
            P(("ctx", "wshard"), None),
            P(),
            P(("ctx", "wshard")),
            P(("ctx", "wshard"), None),
            P(("ctx", "wshard"), None),
            P(None, ("ctx", "wshard")),
        ),
        check_vma=False,
    )
```

```python
import functools

import jax
import jax.numpy as jnp
from jax import lax
from jax.experimental import pallas as pl
from jax.experimental.pallas import tpu as pltpu
from jax.sharding import PartitionSpec as P

epsilon = 1e-06
highest = lax.Precision.HIGHEST
thresholds = (12, 16, 23, 32, 46, 64, 91)
masked_out = -1e30
bf16 = jnp.bfloat16
f32 = jnp.float32
peer_axes = ("ctx", "wshard")
vmem_bytes = 60 * 1024 * 1024

ladder_ring = (0, 2, 4, 6, 7, 5, 3, 1)


def bucket_of(offset):
    distance = jnp.abs(offset)
    beyond = 8 + sum(((distance >= border).astype(jnp.int32) for border in thresholds))
    near_far = jnp.where(distance < 8, distance, beyond)
    return jnp.where(offset > 0, 16, 0) + near_far


def rms_norm(values, gain_vector):
    return (
        values
        * lax.rsqrt(jnp.mean(values * values, axis=-1, keepdims=True) + epsilon)
        * gain_vector
    )


def dot(left_side, right_side, dims, precision=None):
    return lax.dot_general(
        left_side, right_side, (dims, ((), ())), precision=precision, preferred_element_type=f32
    )


def forward_product(left_side, right_side):
    return dot(left_side, right_side, ((1,), (0,)))


def backward_product(left_side, right_side):
    return dot(left_side, right_side, ((1,), (1,)))


def weight_product(left_side, right_side):
    return dot(left_side, right_side, ((0,), (0,)))


def iota(shape, dim):
    return lax.broadcasted_iota(jnp.int32, shape, dim)


def arrange_kernel(rows, count, me_ref, order_ref, gain_ref, weight_ref, *refs):
    blocks, (x_ref, normed_ref, qkv_ref) = refs[:-3], refs[-3:]
    me = me_ref[0]
    first = (me ^ pl.program_id(0)) * rows
    tokens = first + iota((rows, rows), 0)
    total = None
    for k in range(count):
        places = order_ref[pl.ds(me ^ k, 1), :]
        chosen = (places == tokens).astype(f32).astype(bf16)
        part = forward_product(chosen, blocks[k][...])
        total = part if total is None else total + part
    x_ref[...] = total.astype(bf16)
    normed = rms_norm(total, gain_ref[...]).astype(bf16)
    normed_ref[...] = normed
    qkv_ref[...] = forward_product(normed, weight_ref[...]).astype(bf16)


def own_heads_kernel(width, count, n_w, me_ref, *refs):
    mine, given, out_ref = refs[:3], refs[3:6], refs[6]
    me = me_ref[0]
    half, columns = mine[0].shape
    for m in range(count):

        @pl.when(me == m)
        def _():
            for t in range(3):
                for w in range(n_w):
                    source = mine[t] if m % n_w == w else given[t]
                    place = slice(w * half, (w + 1) * half), slice(t * width, (t + 1) * width)
                    if (m + 1) * width <= columns:
                        out_ref[place] = source[:, m * width : (m + 1) * width]
                    else:
                        out_ref[place] = jnp.zeros((half, width), out_ref.dtype)


def bias_kernel(rows, heads_here, heads, buckets, me_ref, table_ref, out_ref):
    lanes = iota((8, 4 * rows), 1)
    ids = bucket_of(2 * rows - lanes)
    for h in range(heads_here):
        head = jnp.minimum(me_ref[0] * heads_here + h, heads - 1)
        base = jnp.zeros((8, 4 * rows), f32)
        for b in range(buckets):
            base = jnp.where(ids == b, table_ref[b, head], base)
        wide = jnp.broadcast_to(base[0:1], (rows, 4 * rows))
        rolled = pltpu.roll(wide, 0, 1, stride=1, stride_axis=0)
        out_ref[h, 0] = jnp.full((rows, rows), table_ref[buckets // 2 - 1, head], f32)
        out_ref[h, 4] = jnp.full((rows, rows), table_ref[buckets - 1, head], f32)
        for delta in (1, 0, -1):
            start = rows + rows * (1 - delta)
            out_ref[h, delta + 2] = rolled[:, start : start + rows]


def span_of(lengths_ref, seqs, first, last, rows, total):
    low, high, end = 0, total, 0
    ends = []
    for s in range(seqs):
        end = end + lengths_ref[s]
        ends.append(end)
    for s in range(seqs):
        low = jnp.where(ends[s] <= first, ends[s], low)
    for s in reversed(range(seqs)):
        high = jnp.where(ends[s] > last, ends[s], high)
    high = jnp.minimum(high, total)
    return ends, low // rows, (high + rows - 1) // rows


def sequence_ids(ends, first, shape, dim):
    places = first + iota(shape, dim)
    ids = jnp.zeros(shape, jnp.int32)
    for end in ends:
        ids = ids + (places >= end).astype(jnp.int32)
    return ids


def attend_kernel(
    rows, count, heads_here, size, seqs, me_ref, lengths_ref, qkv_ref, bias_ref, att_ref, wide_ref, lse_ref
):
    me = me_ref[0]
    width = heads_here * size
    here = pl.program_id(0)
    block = me ^ here
    ends, low, high = span_of(
        lengths_ref, seqs, block * rows, block * rows + rows - 1, rows, count * rows
    )
    query_seq = sequence_ids(ends, block * rows, (1, rows), 1)
    start = pl.multiple_of(here * rows, rows)
    queries = qkv_ref[pl.ds(start, rows), :][:, :width]

    def step(key_block, carry):
        at = pl.multiple_of((key_block ^ me) * rows, rows)
        own = qkv_ref[pl.ds(at, rows), :]
        delta = jnp.clip(key_block - block, -2, 2) + 2
        same = sequence_ids(ends, key_block * rows, (rows, 1), 0) == query_seq
        after = []
        for h in range(heads_here):
            top, total, acc = carry[h]
            query = queries[:, h * size : (h + 1) * size]
            key = own[:, width + h * size : width + (h + 1) * size]
            value = own[:, 2 * width + h * size : 2 * width + (h + 1) * size]
            scores = backward_product(key, query) + bias_ref[h, delta]
            scores = jnp.where(same, scores, masked_out)
            top_next = jnp.maximum(top, jnp.max(scores, axis=0, keepdims=True))
            probs = jnp.exp(scores - top_next)
            fade = jnp.exp(top - top_next)
            total = total * fade + jnp.sum(probs, axis=0, keepdims=True)
            acc = acc * fade + weight_product(value, probs.astype(bf16))
            after.append((top_next, total, acc))
        return tuple(after)

    fresh = (
        jnp.full((1, rows), masked_out, f32),
        jnp.zeros((1, rows), f32),
        jnp.zeros((size, rows), f32),
    )
    done = lax.fori_loop(low, high, step, (fresh,) * heads_here)
    for h in range(heads_here):
        top, total, acc = done[h]
        lse_ref[h : h + 1, :] = top + jnp.log(total)
        out = (acc / total).T
        wide_ref[:, h * size : (h + 1) * size] = out
        att_ref[:, h * size : (h + 1) * size] = out.astype(bf16)


def attend_back_kernel(
    rows,
    count,
    heads_here,
    size,
    seqs,
    buckets,
    me_ref,
    lengths_ref,
    qkv_ref,
    bias_ref,
    lse_ref,
    wide_ref,
    d_att_ref,
    dqkv_ref,
    table_ref,
    dq_ref,
    sums_ref,
    delta_ref,
):
    me = me_ref[0]
    width = heads_here * size
    here = pl.program_id(0)
    block = me ^ here

    @pl.when(here == 0)
    def _():
        dq_ref[...] = jnp.zeros_like(dq_ref)
        sums_ref[...] = jnp.zeros_like(sums_ref)
        for k in range(count):
            part = slice(k * rows, (k + 1) * rows)
            both = d_att_ref[part, :].astype(f32) * wide_ref[part, :]
            for h in range(heads_here):
                delta_ref[h : h + 1, part] = jnp.sum(
                    both[:, h * size : (h + 1) * size].T, axis=0, keepdims=True
                )

    ends, low, high = span_of(
        lengths_ref, seqs, block * rows, block * rows + rows - 1, rows, count * rows
    )
    key_seq = sequence_ids(ends, block * rows, (rows, 1), 0)
    start = pl.multiple_of(here * rows, rows)
    own = qkv_ref[pl.ds(start, rows), :]

    def step(query_block, carry):
        rel = query_block ^ me
        at = pl.multiple_of(rel * rows, rows)
        queries = qkv_ref[pl.ds(at, rows), :][:, :width]
        d_outs = d_att_ref[pl.ds(at, rows), :]
        near = jnp.clip(block - query_block, -2, 2) + 2
        same = key_seq == sequence_ids(ends, query_block * rows, (1, rows), 1)
        after = []
        for h in range(heads_here):
            d_key, d_value = carry[h]
            key = own[:, width + h * size : width + (h + 1) * size]
            value = own[:, 2 * width + h * size : 2 * width + (h + 1) * size]
            query = queries[:, h * size : (h + 1) * size]
            d_out = d_outs[:, h * size : (h + 1) * size]
            scores = backward_product(key, query) + bias_ref[h, near]
            lse = lse_ref[h : h + 1, pl.ds(at, rows)]
            soft = jnp.where(same, jnp.exp(scores - lse), 0.0)
            d_probs = backward_product(value, d_out)
            d_scores = (soft * (d_probs - delta_ref[h : h + 1, pl.ds(at, rows)])).astype(bf16)
            sums_ref[h, near] += d_scores.astype(f32)
            d_value = d_value + forward_product(soft.astype(bf16), d_out)
            d_key = d_key + forward_product(d_scores, query)
            dq_ref[h, rel] += weight_product(key, d_scores)
            after.append((d_key, d_value))
        return tuple(after)

    zero = jnp.zeros((rows, size), f32)
    done = lax.fori_loop(low, high, step, ((zero, zero),) * heads_here)
    for h in range(heads_here):
        d_key, d_value = done[h]
        dqkv_ref[pl.ds(start, rows), width + h * size : width + (h + 1) * size] = d_key.astype(bf16)
        dqkv_ref[pl.ds(start, rows), 2 * width + h * size : 2 * width + (h + 1) * size] = (
            d_value.astype(bf16)
        )

    @pl.when(here == count - 1)
    def _():
        for h in range(heads_here):
            for k in range(count):
                dqkv_ref[k * rows : (k + 1) * rows, h * size : (h + 1) * size] = (
                    dq_ref[h, k].T.astype(bf16)
                )
        turned = (iota((rows, rows), 0) + iota((rows, rows), 1) == rows - 1).astype(f32)
        ids = bucket_of(2 * rows - 1 - iota((buckets, 4 * rows), 1))
        mine = ids == iota((buckets, 4 * rows), 0)
        bucket_rows = iota((buckets, 1), 0)
        lanes = iota((buckets, 128), 1)
        table = jnp.zeros((buckets, 128), f32)
        for h in range(heads_here):
            strip = jnp.concatenate(
                [forward_product_exact(turned, sums_ref[h, d]) for d in (3, 2, 1)]
                + [jnp.zeros((rows, rows), f32)],
                axis=1,
            )
            diagonals = jnp.sum(
                pltpu.roll(strip, 0, 1, stride=1, stride_axis=0), axis=0, keepdims=True
            )
            column = jnp.sum(jnp.where(mine, diagonals, 0.0), axis=1, keepdims=True)
            column = column + jnp.where(bucket_rows == buckets // 2 - 1, jnp.sum(sums_ref[h, 0]), 0.0)
            column = column + jnp.where(bucket_rows == buckets - 1, jnp.sum(sums_ref[h, 4]), 0.0)
            table = jnp.where(lanes == h, column, table)
        table_ref[...] = table


def place_kernel(groups, part, units_all, hidden_units, heads_all, width, spot_ref, *refs):
    spot = spot_ref[0]
    wide, refs = refs[: 4 * groups], refs[4 * groups :]
    narrow, refs = refs[: 2 * groups], refs[2 * groups :]
    outs, scratch, sems = refs[:7], refs[7:-1], refs[-1]
    gate, up, down, turned, query, key, value, out_rows, out_turned = scratch
    middle = 3 * units_all // 2

    def row_of(j, h):
        index = lax.rem(spot + groups - j, groups) if h == 0 else lax.rem(spot + j, groups)
        return pl.multiple_of((2 * index + h) * part, 8)

    def copy(k, source):
        return pltpu.make_async_copy(source, outs[k], sems.at[k])

    def gather(target, t):
        for c in range(2):
            low = max(c * middle, t * units_all)
            high = min((c + 1) * middle, t * units_all + hidden_units)
            if low < high:
                for j in range(groups):
                    for h in range(2):
                        block = wide[(j * 2 + c) * 2 + h]
                        target[pl.ds(row_of(j, h), part), low - t * units_all : high - t * units_all] = (
                            block[:, low - c * middle : high - c * middle].astype(f32)
                        )

    gather(gate, 0)
    copy(0, gate).start()
    gather(up, 1)
    copy(1, up).start()
    gather(down, 2)
    for first in range(0, hidden_units, 128):
        turned[first : first + 128, :] = down[:, first : first + 128].T
    copy(2, turned).start()
    for k, target in enumerate((query, key, value)):
        for j in range(groups):
            for h in range(2):
                target[pl.ds(row_of(j, h), part), :] = (
                    narrow[j * 2 + h][:, k * heads_all : (k + 1) * heads_all].astype(f32)
                )
        copy(3 + k, target).start()
    count = heads_all // width
    for q in range(count):
        for j in range(groups):
            for h in range(2):
                first = 3 * heads_all + q * width
                out_rows[q, pl.ds(row_of(j, h), part), :] = (
                    narrow[j * 2 + h][:, first : first + width].astype(f32)
                )
        rows = out_rows.shape[1]
        out_turned[:, q * rows : (q + 1) * rows] = out_rows[q].T
    copy(6, out_turned).start()
    for k, source in enumerate((gate, up, turned, query, key, value, out_turned)):
        copy(k, source).wait()


def forward_product_exact(left_side, right_side):
    return dot(left_side, right_side, ((1,), (0,)), highest)


def whole(shape):
    return pl.BlockSpec(shape, lambda *_: (0,) * len(shape))


def per_device(
    sizes,
    inputs,
    out_grad,
    lengths,
    permutation,
    gain_attention,
    query_weight,
    key_weight,
    value_weight,
    out_weight,
    bucket_bias,
    gain_feedforward,
    gate_weight,
    up_weight,
    down_weight,
):
    n_group, n_ctx, n_w = sizes
    n = n_ctx * n_w
    fast = (n_group, n_ctx, n_w) == (8, 2, 2)
    rows, model = inputs.shape
    buckets, heads = bucket_bias.shape
    hidden_units = gate_weight.shape[1]
    size = query_weight.shape[1] // heads
    seqs = lengths.shape[1]
    tokens = rows * n
    heads_here = -(-heads // n)
    width = heads_here * size
    units = -(-hidden_units // (128 * n)) * 128
    ctx, wsh = lax.axis_index("ctx"), lax.axis_index("wshard")
    me = lax.axis_index(peer_axes)
    rank = wsh * n_ctx + ctx
    flip_w = [(0, 1), (1, 0)]


    def mate(block):
        return lax.ppermute(block, "wshard", flip_w)

    def across(block):
        return lax.ppermute(block, "ctx", flip_w)

    def to_relative(stacked):
        return jnp.take(stacked, me ^ lax.iota(jnp.int32, n), axis=0)

    def gather_blocks(block):
        if fast:
            far = across(block)
            return [block, mate(block), far, mate(far)]
        stacked = to_relative(lax.all_gather(block, peer_axes, axis=0, tiled=False))
        return [stacked[k] for k in range(n)]

    def columns_of(weight, which, wide):
        over = max(0, n * wide - weight.shape[1])
        padded = jnp.pad(weight, ((0, 0), (0, over))) if over else weight
        return lax.dynamic_slice_in_dim(padded, which * wide, wide, 1)

    def own_columns(parts, wide, which):
        return jnp.concatenate([columns_of(part, which, wide) for part in parts], axis=1)

    def in_order(mine, given):
        upper = jnp.where(wsh == 0, mine, given)
        lower = jnp.where(wsh == 0, given, mine)
        return jnp.concatenate([upper, lower], axis=0)

    hold = lax.optimization_barrier

    if fast:
        row_far, row_mate = across(inputs), mate(inputs)
    heads_mine = (query_weight, key_weight, value_weight)
    heads_given = [mate(weight) for weight in heads_mine]
    out_other = mate(out_weight)
    gate_up_mine = own_columns((gate_weight, up_weight), units, rank)
    gate_up_sent = own_columns((gate_weight, up_weight), units, (1 - wsh) * n_ctx + ctx)
    half = down_weight.shape[0]
    extra = n_ctx * units - half
    down_other = mate(down_weight[:extra])
    down_wide = jnp.concatenate(
        [
            down_weight,
            jnp.where(wsh == 0, down_other, jnp.zeros_like(down_other)),
            jnp.zeros_like(down_other),
        ]
    )
    down_own = lax.dynamic_slice_in_dim(down_wide, wsh * extra + ctx * units, units, 0)
    me_1 = me.reshape(1).astype(jnp.int32)
    order = permutation.reshape(n, rows)
    params = pltpu.CompilerParams(vmem_limit_bytes=vmem_bytes)
    qkv_weight = pl.pallas_call(
        functools.partial(own_heads_kernel, width, n, n_w),
        out_shape=jax.ShapeDtypeStruct((model, 3 * width), bf16),
        in_specs=[pl.BlockSpec(memory_space=pltpu.SMEM)]
        + [pl.BlockSpec(memory_space=pltpu.VMEM)] * 6,
        out_specs=pl.BlockSpec(memory_space=pltpu.VMEM),
        compiler_params=params,
        name="own_heads",
    )(me_1, *heads_mine, *heads_given)
    bias = pl.pallas_call(
        functools.partial(bias_kernel, rows, heads_here, heads, buckets),
        out_shape=jax.ShapeDtypeStruct((heads_here, 5, rows, rows), f32),
        in_specs=[
            pl.BlockSpec(memory_space=pltpu.SMEM),
            pl.BlockSpec(memory_space=pltpu.SMEM),
        ],
        out_specs=pl.BlockSpec(memory_space=pltpu.VMEM),
        compiler_params=params,
        name="bias_strips",
    )(me_1, bucket_bias)
    if fast:
        row_far, out_grad, qkv_weight, bias, gate_up_mine, gate_up_sent = hold(
            (row_far, out_grad, qkv_weight, bias, gate_up_mine, gate_up_sent)
        )
        row_blocks = [inputs, row_mate, row_far, mate(row_far)]
    else:
        row_blocks = gather_blocks(inputs)
    gate_up_given = mate(gate_up_sent)
    dy = jnp.concatenate(gather_blocks(out_grad))

    x_all, normed, qkv = pl.pallas_call(
        functools.partial(arrange_kernel, rows, n),
        out_shape=(
            jax.ShapeDtypeStruct((tokens, model), bf16),
            jax.ShapeDtypeStruct((tokens, model), bf16),
            jax.ShapeDtypeStruct((tokens, 3 * width), bf16),
        ),
        grid_spec=pltpu.PrefetchScalarGridSpec(
            num_scalar_prefetch=1,
            grid=(n,),
            in_specs=[whole((n, rows)), whole((1, model)), whole((model, 3 * width))]
            + [whole((rows, model))] * n,
            out_specs=[
                pl.BlockSpec((rows, model), lambda t, *_: (t, 0)),
                pl.BlockSpec((rows, model), lambda t, *_: (t, 0)),
                pl.BlockSpec((rows, 3 * width), lambda t, *_: (t, 0)),
            ],
        ),
        compiler_params=params,
        cost_estimate=pl.CostEstimate(
            flops=2 * tokens * model * (tokens + 3 * width),
            bytes_accessed=8 * tokens * model,
            transcendentals=0,
        ),
        name="arrange_project",
    )(me_1, order, gain_attention.reshape(1, model), qkv_weight, *row_blocks)
    lengths_row = lengths.reshape(seqs)
    attended, attended_wide, lse = pl.pallas_call(
        functools.partial(attend_kernel, rows, n, heads_here, size, seqs),
        out_shape=(
            jax.ShapeDtypeStruct((tokens, width), bf16),
            jax.ShapeDtypeStruct((tokens, width), f32),
            jax.ShapeDtypeStruct((heads_here, tokens), f32),
        ),
        grid_spec=pltpu.PrefetchScalarGridSpec(
            num_scalar_prefetch=2,
            grid=(n,),
            in_specs=[whole((tokens, 3 * width)), whole((heads_here, 5, rows, rows))],
            out_specs=[
                pl.BlockSpec((rows, width), lambda t, *_: (t, 0)),
                pl.BlockSpec((rows, width), lambda t, *_: (t, 0)),
                pl.BlockSpec((heads_here, rows), lambda t, *_: (0, t)),
            ],
        ),
        compiler_params=params,
        cost_estimate=pl.CostEstimate(
            flops=16 * tokens * tokens * width,
            bytes_accessed=16 * tokens * width,
            transcendentals=tokens * tokens * heads_here,
        ),
        name="attend",
    )(me_1, lengths_row, qkv, bias)

    strip = model // n // n_group
    part = strip // 2
    if fast:
        group = lax.axis_index("group")
        spot = jnp.where(group % 2 == 0, group // 2, n_group - 1 - group // 2)
        ahead = [(ladder_ring[k], ladder_ring[(k + 1) % n_group]) for k in range(n_group)]
        behind = [(b, a) for a, b in ahead]

    def forward(block):
        return lax.ppermute(block, "group", ahead)

    def backward(block):
        return lax.ppermute(block, "group", behind)

    def diagonal(block):
        return lax.ppermute(block, peer_axes, [(q, q ^ 3) for q in range(n)])

    def pick(array, index, axis):
        return lax.squeeze(lax.dynamic_slice_in_dim(array, index, 1, axis), (axis,))

    def rank_of(k):
        peer = me ^ k
        return (peer % n_w) * n_ctx + peer // n_w

    def ring(take, swap, pieces):
        both_ways = (forward, backward)
        one, two = take(0, lax.rem(spot + 7, n_group)), take(1, lax.rem(spot + 1, n_group))
        for s in range(n_group - 1):
            came = yield (one, two), both_ways
            one = came[0] + take(0, lax.rem(spot + 14 - s, n_group))
            two = came[1] + take(1, lax.rem(spot + 2 + s, n_group))
        blocks, join = swap(one, two)
        came = yield tuple(blocks[1:]), (mate, across, diagonal)
        pairs = join([blocks[0], *came])
        for pair in pairs:
            pieces.extend(pair)
        for s in range(n_group - 1):
            for c, pair in enumerate(pairs):
                pairs[c] = yield pair, both_ways
                pieces.extend(pairs[c])

    class Stream:
        def __init__(self, steps):
            self.steps, self.result, self.came = steps, None, None
            self.pending = next(steps)

        def advance(self, came):
            try:
                self.pending = self.steps.send(came)
            except StopIteration as stop:
                self.pending, self.result = None, stop.value

    order_token = [me]

    def tick(values, *streams):
        live = [stream for stream in streams if stream is not None and stream.pending is not None]
        if not live:
            return values
        arrived, values = hold(([stream.came for stream in live if stream.came], values))
        for stream in live:
            if stream.came:
                stream.advance(arrived.pop(0))
        live = [stream for stream in live if stream.pending is not None]
        operands, values, order_token[0] = hold(
            ([stream.pending[0] for stream in live], values, order_token[0])
        )
        for stream, sent in zip(live, operands):
            stream.came = [send(x) for send, x in zip(stream.pending[1], sent)]
        return values

    def rows_cut(grad):
        return grad.reshape(n, n_group, 2, part, grad.shape[1])

    wide_pieces, narrow_pieces = [], []

    def wide_ring(grad_gate_up, grad_down):
        one, two = rows_cut(grad_gate_up), rows_cut(grad_down)
        columns = 3 * n * units

        def take(h, index):
            return jnp.concatenate([pick(x[:, :, h], index, 1) for x in (one, two)], axis=-1)

        def swap(one, two):
            both = jnp.stack([one, two], axis=1)

            def join(came):
                full = jnp.zeros((2, part, columns), bf16)
                for k in range(n):
                    for t in range(3):
                        full = lax.dynamic_update_slice_in_dim(
                            full,
                            came[k][:, :, t * units : (t + 1) * units],
                            t * n * units + rank_of(k) * units,
                            2,
                        )
                middle = columns // 2
                return [(full[0, :, :middle], full[1, :, :middle])] + [
                    (full[0, :, middle:], full[1, :, middle:])
                ]

            return [pick(both, me ^ k, 0) for k in range(n)], join

        return ring(take, swap, wide_pieces)

    def small_ring(grad_qkv, grad_out):
        one, two = rows_cut(grad_qkv), rows_cut(grad_out)

        def take(h, index):
            return jnp.concatenate(
                [pick(one[:, :, h], index, 1), pick(two[:, :, h], index, 1)], axis=-1
            )

        def swap(one, two):
            both = jnp.stack([one, two], axis=1)
            own = jnp.concatenate([both[k, :, :, 3 * width :] for k in range(n)], axis=2)

            def join(came):
                stacked = jnp.stack(came)
                came = [pick(stacked, me ^ r, 0) for r in range(n)]
                full = jnp.concatenate(
                    [came[r][:, :, k * width : (k + 1) * width] for k in range(3) for r in range(n)]
                    + [own],
                    axis=2,
                )
                return [(full[0], full[1])]

            return [pick(both, me ^ k, 0)[:, :, : 3 * width] for k in range(n)], join

        return ring(take, swap, narrow_pieces)

    def sum_ring(small):
        for axis, bit, count in (
            ("wshard", 1, n_w),
            ("ctx", 1, n_ctx),
            ("group", 1, n_group),
            ("group", 2, n_group),
            ("group", 4, n_group),
        ):
            pairs = [(g, g ^ bit) for g in range(count)]
            came = yield (small,), (lambda x: lax.ppermute(x, axis, pairs),)
            small = small + came[0]
        return small

    def scatter_near(partial):
        sent = partial.reshape(n, rows, -1)
        if not fast:
            total = lax.psum_scatter(to_relative(sent), peer_axes, scatter_dimension=0, tiled=False)
            return total.astype(f32), None
        got = mate(jnp.stack([sent[1], sent[3]]))
        near = sent[0].astype(f32) + got[0].astype(f32)
        return near, (sent[2].astype(f32) + got[1].astype(f32)).astype(bf16)

    def scatter_far(near, away):
        return near + across(away).astype(f32) if fast else near

    attended, out_mine, out_other, gate_up_mine = hold(
        (attended, out_weight, out_other, gate_up_mine)
    )
    gate_up = in_order(gate_up_mine, gate_up_given)
    if fast:
        attended_far, attended_mate = across(attended), mate(attended)
        attended_far, gate_up = hold((attended_far, gate_up))
        attended_blocks = [attended, attended_mate, attended_far, mate(attended_far)]
    else:
        attended_blocks = gather_blocks(attended)
    out_full = in_order(out_mine, out_other)
    out_full = jnp.pad(out_full, ((0, n * width - out_full.shape[0]), (0, 0)))
    out_blocks = [lax.dynamic_slice_in_dim(out_full, (me ^ k) * width, width, 0) for k in range(n)]
    out_relative = jnp.concatenate(out_blocks, axis=0)
    by_rows = [
        jnp.concatenate(
            [attended_blocks[k][(m ^ k) * rows : ((m ^ k) + 1) * rows] for m in range(n)]
        )
        for k in range(n)
    ]
    attended_all = jnp.concatenate(by_rows, axis=1)
    residual_all = x_all.astype(f32) + forward_product(
        attended_all, out_relative
    )
    residual = residual_all[:rows]
    normed_ff = rms_norm(residual_all, gain_feedforward).astype(bf16)
    gate_up_proj = forward_product(normed_ff, gate_up)
    gate_proj, up_proj = gate_up_proj[:, :units], gate_up_proj[:, units:]

    def activate(gate_in, up_in):
        return jax.nn.gelu(gate_in, approximate=True) * up_in

    hidden_wide, activate_back = jax.vjp(activate, gate_proj, up_proj)
    hidden = hidden_wide.astype(bf16)
    d_hidden = backward_product(dy, down_own)
    d_gate_wide, d_up_wide = activate_back(d_hidden)
    d_gate_up = jnp.concatenate([d_gate_wide.astype(bf16), d_up_wide.astype(bf16)], axis=1)

    grad_gate_up = weight_product(normed_ff, d_gate_up).astype(bf16)
    grad_down = weight_product(dy, hidden).astype(bf16)
    wide = Stream(wide_ring(grad_gate_up, grad_down)) if fast else None
    d_gate_up, hidden = tick((d_gate_up, hidden), wide)

    back = backward_product(d_gate_up, gate_up).astype(bf16)
    back, hidden = tick((back, hidden), wide)
    near, away = scatter_near(back)
    out_partial = forward_product(hidden, down_own).astype(bf16)
    near, away, out_partial = tick((near, away, out_partial), wide)
    d_normed_ff = scatter_far(near, away)
    d_normed_ff, residual = tick((d_normed_ff, residual), wide)
    norm_ff_back = jax.vjp(rms_norm, residual, gain_feedforward)[1]
    d_residual_norm, grad_gain_ff = norm_ff_back(d_normed_ff)
    d_residual = dy[:rows].astype(f32) + d_residual_norm
    branch = d_residual.astype(bf16)

    if fast:
        d_rows = backward_product(branch, out_relative).astype(bf16)
        d_rows = [d_rows[:, k * width : (k + 1) * width] for k in range(n)]
        d_rows = [d_rows[0], mate(d_rows[1]), across(d_rows[2]), diagonal(d_rows[3])]
        d_attended, branch = hold((jnp.concatenate(d_rows), branch))
    else:
        branch_blocks = gather_blocks(branch)
        d_attended = backward_product(jnp.concatenate(branch_blocks), out_blocks[0]).astype(bf16)
    d_attended, branch = tick((d_attended, branch), wide)
    if fast:
        branch_blocks = gather_blocks(branch)
    d_qkv, d_table = pl.pallas_call(
        functools.partial(attend_back_kernel, rows, n, heads_here, size, seqs, buckets),
        out_shape=(
            jax.ShapeDtypeStruct((tokens, 3 * width), bf16),
            jax.ShapeDtypeStruct((buckets, 128), f32),
        ),
        grid_spec=pltpu.PrefetchScalarGridSpec(
            num_scalar_prefetch=2,
            grid=(n,),
            in_specs=[
                whole((tokens, 3 * width)),
                whole((heads_here, 5, rows, rows)),
                whole((heads_here, tokens)),
                whole((tokens, width)),
                whole((tokens, width)),
            ],
            out_specs=[whole((tokens, 3 * width)), whole((buckets, 128))],
            scratch_shapes=[
                pltpu.VMEM((heads_here, n, size, rows), f32),
                pltpu.VMEM((heads_here, 5, rows, rows), f32),
                pltpu.VMEM((heads_here, tokens), f32),
            ],
        ),
        compiler_params=params,
        cost_estimate=pl.CostEstimate(
            flops=40 * tokens * tokens * width,
            bytes_accessed=16 * tokens * width,
            transcendentals=tokens * tokens * heads_here,
        ),
        name="attend_back",
    )(me_1, lengths_row, qkv, bias, lse, attended_wide, d_attended)
    d_qkv, branch_far, out_partial = tick((d_qkv, branch_blocks[2], out_partial), wide)
    branch_blocks[2] = branch_far
    grad_qkv = weight_product(normed, d_qkv).astype(bf16)
    grad_out = sum(
        weight_product(branch_blocks[k], attended[k * rows : (k + 1) * rows]) for k in range(n)
    ).astype(bf16)
    grad_qkv, grad_out, d_qkv = tick((grad_qkv, grad_out, d_qkv), wide)
    back = backward_product(d_qkv, qkv_weight).astype(bf16)
    narrow = Stream(small_ring(grad_qkv, grad_out)) if fast else None
    (back,) = tick((back,), wide, narrow)

    near, away = scatter_near(back)
    near, away = tick((near, away), narrow)
    (away,) = tick((away,), wide)
    d_normed = scatter_far(near, away)
    tick((), narrow)
    tick((), wide)
    d_normed, x_own = tick((d_normed, x_all[:rows]), narrow)
    norm_attn_back = jax.vjp(rms_norm, x_own.astype(f32), gain_attention)[1]
    d_input_norm, grad_gain_attn = norm_attn_back(d_normed)
    input_grad = (d_residual + d_input_norm).astype(bf16)
    out_near, out_away = scatter_near(out_partial)
    out_away, grad_gain_attn = tick((out_away, grad_gain_attn), wide)
    outputs = (residual + scatter_far(out_near, out_away)).astype(bf16)

    table_here = jnp.pad(d_table[:, :heads_here], ((0, 0), (0, n * heads_here)))
    table_here = jnp.roll(table_here, me * heads_here, axis=1)[:, :heads]
    small = jnp.concatenate([grad_gain_attn, grad_gain_ff, table_here.reshape(-1)])
    if fast:
        sums = Stream(sum_ring(small))
        while wide.pending or narrow.pending or sums.pending:
            tick((), narrow, sums)
            tick((), wide)
        small = sums.result
    else:
        small = lax.psum(small, ("group",) + peer_axes)
    share = model // n
    gains = [lax.dynamic_slice_in_dim(small, k * model + order_token[0] * share, share) for k in range(2)]
    grad_table = small[2 * model :].reshape(buckets, heads)

    if fast:
        own_rows, all_heads = model // n, n * width
        wide_shape, down_shape = (own_rows, hidden_units), (hidden_units, own_rows)
        out_shapes = [wide_shape, wide_shape, down_shape]
        out_shapes += [(own_rows, all_heads)] * 3 + [(width, model)]
        scratch = [wide_shape, wide_shape, wide_shape, down_shape]
        scratch += [(own_rows, all_heads)] * 3 + [(n, own_rows, width), (width, model)]
        total_gate, total_up, total_down, *total_qkv, total_out = pl.pallas_call(
            functools.partial(
                place_kernel, n_group, part, n * units, hidden_units, all_heads, width
            ),
            out_shape=[jax.ShapeDtypeStruct(shape, f32) for shape in out_shapes],
            in_specs=[pl.BlockSpec(memory_space=pltpu.SMEM)]
            + [pl.BlockSpec(memory_space=pltpu.VMEM)] * (6 * n_group),
            out_specs=[pl.BlockSpec(memory_space=pl.ANY)] * 7,
            scratch_shapes=[pltpu.VMEM(shape, f32) for shape in scratch]
            + [pltpu.SemaphoreType.DMA((7,))],
            compiler_params=params,
            name="place",
        )(spot.reshape(1).astype(jnp.int32), *wide_pieces, *narrow_pieces)
    else:

        def place_columns(grad, which, wide, total):
            full = jnp.zeros((grad.shape[0], n * wide), bf16)
            full = lax.dynamic_update_slice_in_dim(full, grad, which * wide, 1)
            return full[:, :total]

        def finish(full, dim):
            full = lax.psum_scatter(full, peer_axes, scatter_dimension=dim, tiled=True)
            return lax.psum(full, "group").astype(f32)

        total_qkv = [
            finish(
                place_columns(grad_qkv[:, k * width : (k + 1) * width], me, width, heads * size), 0
            )
            for k in range(3)
        ]
        total_out = finish(place_columns(grad_out, me, width, heads * size).T, 0)
        total_gate = finish(place_columns(grad_gate_up[:, :units], rank, units, hidden_units), 0)
        total_up = finish(place_columns(grad_gate_up[:, units:], rank, units, hidden_units), 0)
        total_down = finish(place_columns(grad_down, rank, units, hidden_units).T, 1)
    return (
        outputs,
        input_grad,
        gains[0],
        total_qkv[0],
        total_qkv[1],
        total_qkv[2],
        total_out,
        grad_table,
        gains[1],
        total_gate,
        total_up,
        total_down,
    )


def solution(mesh):
    sizes = (mesh.shape["group"], mesh.shape["ctx"], mesh.shape["wshard"])
    return jax.shard_map(
        functools.partial(per_device, sizes),
        mesh=mesh,
        in_specs=(
            P(("group", "ctx", "wshard"), None),
            P(("group", "ctx", "wshard"), None),
            P("group", None),
            P("group", None),
            P(),
            P("wshard", None),
            P("wshard", None),
            P("wshard", None),
            P("wshard", None),
            P(),
            P(),
            P("wshard", None),
            P("wshard", None),
            P("wshard", None),
        ),
        out_specs=(
            P(("group", "ctx", "wshard"), None),
            P(("group", "ctx", "wshard"), None),
            P(("ctx", "wshard")),
            P(("ctx", "wshard"), None),
            P(("ctx", "wshard"), None),
            P(("ctx", "wshard"), None),
            P(("ctx", "wshard"), None),
            P(),
            P(("ctx", "wshard")),
            P(("ctx", "wshard"), None),
            P(("ctx", "wshard"), None),
            P(None, ("ctx", "wshard")),
        ),
        check_vma=False,
    )
```

```python
import functools

import jax
import jax.numpy as jnp
from jax import lax
from jax.experimental import pallas as pl
from jax.experimental.layout import Layout, with_layout_constraint
from jax.experimental.pallas import tpu as pltpu
from jax.sharding import PartitionSpec as P

epsilon = 1e-06
highest = lax.Precision.HIGHEST
thresholds = (12, 16, 23, 32, 46, 64, 91)
masked_out = -1e30
bf16 = jnp.bfloat16
f32 = jnp.float32
peer_axes = ("ctx", "wshard")
vmem_bytes = 60 * 1024 * 1024

ladder_ring = (0, 2, 4, 6, 7, 5, 3, 1)


def bucket_of(offset):
    distance = jnp.abs(offset)
    beyond = 8 + sum(((distance >= border).astype(jnp.int32) for border in thresholds))
    near_far = jnp.where(distance < 8, distance, beyond)
    return jnp.where(offset > 0, 16, 0) + near_far


def rms_norm(values, gain_vector):
    return (
        values
        * lax.rsqrt(jnp.mean(values * values, axis=-1, keepdims=True) + epsilon)
        * gain_vector
    )


def dot(left_side, right_side, dims, precision=None):
    return lax.dot_general(
        left_side, right_side, (dims, ((), ())), precision=precision, preferred_element_type=f32
    )


def forward_product(left_side, right_side):
    return dot(left_side, right_side, ((1,), (0,)))


def backward_product(left_side, right_side):
    return dot(left_side, right_side, ((1,), (1,)))


def weight_product(left_side, right_side):
    return dot(left_side, right_side, ((0,), (0,)))


def iota(shape, dim):
    return lax.broadcasted_iota(jnp.int32, shape, dim)


def arrange_kernel(rows, count, me_ref, order_ref, gain_ref, weight_ref, *refs):
    blocks, (x_ref, normed_ref, qkv_ref) = refs[:-3], refs[-3:]
    me = me_ref[0]
    first = (me ^ pl.program_id(0)) * rows
    tokens = first + iota((rows, rows), 0)
    total = None
    for k in range(count):
        places = order_ref[pl.ds(me ^ k, 1), :]
        chosen = (places == tokens).astype(f32).astype(bf16)
        part = forward_product(chosen, blocks[k][...])
        total = part if total is None else total + part
    x_ref[...] = total.astype(bf16)
    normed = rms_norm(total, gain_ref[...]).astype(bf16)
    normed_ref[...] = normed
    qkv_ref[...] = forward_product(normed, weight_ref[...]).astype(bf16)


def own_heads_kernel(width, count, n_w, me_ref, *refs):
    mine, given, out_ref = refs[:3], refs[3:6], refs[6]
    me = me_ref[0]
    half, columns = mine[0].shape
    for m in range(count):

        @pl.when(me == m)
        def _():
            for t in range(3):
                for w in range(n_w):
                    source = mine[t] if m % n_w == w else given[t]
                    place = slice(w * half, (w + 1) * half), slice(t * width, (t + 1) * width)
                    if (m + 1) * width <= columns:
                        out_ref[place] = source[:, m * width : (m + 1) * width]
                    else:
                        out_ref[place] = jnp.zeros((half, width), out_ref.dtype)


def bias_kernel(rows, heads_here, heads, buckets, me_ref, table_ref, out_ref):
    lanes = iota((8, 4 * rows), 1)
    ids = bucket_of(2 * rows - lanes)
    for h in range(heads_here):
        head = jnp.minimum(me_ref[0] * heads_here + h, heads - 1)
        base = jnp.zeros((8, 4 * rows), f32)
        for b in range(buckets):
            base = jnp.where(ids == b, table_ref[b, head], base)
        wide = jnp.broadcast_to(base[0:1], (rows, 4 * rows))
        rolled = pltpu.roll(wide, 0, 1, stride=1, stride_axis=0)
        out_ref[h, 0] = jnp.full((rows, rows), table_ref[buckets // 2 - 1, head], f32)
        out_ref[h, 4] = jnp.full((rows, rows), table_ref[buckets - 1, head], f32)
        for delta in (1, 0, -1):
            start = rows + rows * (1 - delta)
            out_ref[h, delta + 2] = rolled[:, start : start + rows]


def span_of(lengths_ref, seqs, first, last, rows, total):
    low, high, end = 0, total, 0
    ends = []
    for s in range(seqs):
        end = end + lengths_ref[s]
        ends.append(end)
    for s in range(seqs):
        low = jnp.where(ends[s] <= first, ends[s], low)
    for s in reversed(range(seqs)):
        high = jnp.where(ends[s] > last, ends[s], high)
    high = jnp.minimum(high, total)
    return ends, low // rows, (high + rows - 1) // rows


def sequence_ids(ends, first, shape, dim):
    places = first + iota(shape, dim)
    ids = jnp.zeros(shape, jnp.int32)
    for end in ends:
        ids = ids + (places >= end).astype(jnp.int32)
    return ids


def attend_kernel(
    rows, count, heads_here, size, seqs, me_ref, lengths_ref, qkv_ref, bias_ref, att_ref, wide_ref, lse_ref
):
    me = me_ref[0]
    width = heads_here * size
    here = pl.program_id(0)
    block = me ^ here
    ends, low, high = span_of(
        lengths_ref, seqs, block * rows, block * rows + rows - 1, rows, count * rows
    )
    query_seq = sequence_ids(ends, block * rows, (1, rows), 1)
    start = pl.multiple_of(here * rows, rows)
    queries = qkv_ref[pl.ds(start, rows), :][:, :width]

    def step(key_block, carry):
        at = pl.multiple_of((key_block ^ me) * rows, rows)
        own = qkv_ref[pl.ds(at, rows), :]
        delta = jnp.clip(key_block - block, -2, 2) + 2
        same = sequence_ids(ends, key_block * rows, (rows, 1), 0) == query_seq
        after = []
        for h in range(heads_here):
            top, total, acc = carry[h]
            query = queries[:, h * size : (h + 1) * size]
            key = own[:, width + h * size : width + (h + 1) * size]
            value = own[:, 2 * width + h * size : 2 * width + (h + 1) * size]
            scores = backward_product(key, query) + bias_ref[h, delta]
            scores = jnp.where(same, scores, masked_out)
            top_next = jnp.maximum(top, jnp.max(scores, axis=0, keepdims=True))
            probs = jnp.exp(scores - top_next)
            fade = jnp.exp(top - top_next)
            total = total * fade + jnp.sum(probs, axis=0, keepdims=True)
            acc = acc * fade + weight_product(value, probs.astype(bf16))
            after.append((top_next, total, acc))
        return tuple(after)

    fresh = (
        jnp.full((1, rows), masked_out, f32),
        jnp.zeros((1, rows), f32),
        jnp.zeros((size, rows), f32),
    )
    done = lax.fori_loop(low, high, step, (fresh,) * heads_here)
    for h in range(heads_here):
        top, total, acc = done[h]
        lse_ref[h : h + 1, :] = top + jnp.log(total)
        out = (acc / total).T
        wide_ref[:, h * size : (h + 1) * size] = out
        att_ref[:, h * size : (h + 1) * size] = out.astype(bf16)


def attend_back_kernel(
    rows,
    count,
    heads_here,
    size,
    seqs,
    buckets,
    me_ref,
    lengths_ref,
    qkv_ref,
    bias_ref,
    lse_ref,
    wide_ref,
    d_att_ref,
    dqkv_ref,
    table_ref,
    dq_ref,
    sums_ref,
    delta_ref,
):
    me = me_ref[0]
    width = heads_here * size
    here = pl.program_id(0)
    block = me ^ here

    @pl.when(here == 0)
    def _():
        dq_ref[...] = jnp.zeros_like(dq_ref)
        sums_ref[...] = jnp.zeros_like(sums_ref)
        for k in range(count):
            part = slice(k * rows, (k + 1) * rows)
            both = d_att_ref[part, :].astype(f32) * wide_ref[part, :]
            for h in range(heads_here):
                delta_ref[h : h + 1, part] = jnp.sum(
                    both[:, h * size : (h + 1) * size].T, axis=0, keepdims=True
                )

    ends, low, high = span_of(
        lengths_ref, seqs, block * rows, block * rows + rows - 1, rows, count * rows
    )
    key_seq = sequence_ids(ends, block * rows, (rows, 1), 0)
    start = pl.multiple_of(here * rows, rows)
    own = qkv_ref[pl.ds(start, rows), :]

    def step(query_block, carry):
        rel = query_block ^ me
        at = pl.multiple_of(rel * rows, rows)
        queries = qkv_ref[pl.ds(at, rows), :][:, :width]
        d_outs = d_att_ref[pl.ds(at, rows), :]
        near = jnp.clip(block - query_block, -2, 2) + 2
        same = key_seq == sequence_ids(ends, query_block * rows, (1, rows), 1)
        after = []
        for h in range(heads_here):
            d_key, d_value = carry[h]
            key = own[:, width + h * size : width + (h + 1) * size]
            value = own[:, 2 * width + h * size : 2 * width + (h + 1) * size]
            query = queries[:, h * size : (h + 1) * size]
            d_out = d_outs[:, h * size : (h + 1) * size]
            scores = backward_product(key, query) + bias_ref[h, near]
            lse = lse_ref[h : h + 1, pl.ds(at, rows)]
            soft = jnp.where(same, jnp.exp(scores - lse), 0.0)
            d_probs = backward_product(value, d_out)
            d_scores = (soft * (d_probs - delta_ref[h : h + 1, pl.ds(at, rows)])).astype(bf16)
            sums_ref[h, near] += d_scores.astype(f32)
            d_value = d_value + forward_product(soft.astype(bf16), d_out)
            d_key = d_key + forward_product(d_scores, query)
            dq_ref[h, rel] += weight_product(key, d_scores)
            after.append((d_key, d_value))
        return tuple(after)

    zero = jnp.zeros((rows, size), f32)
    done = lax.fori_loop(low, high, step, ((zero, zero),) * heads_here)
    for h in range(heads_here):
        d_key, d_value = done[h]
        dqkv_ref[pl.ds(start, rows), width + h * size : width + (h + 1) * size] = d_key.astype(bf16)
        dqkv_ref[pl.ds(start, rows), 2 * width + h * size : 2 * width + (h + 1) * size] = (
            d_value.astype(bf16)
        )

    @pl.when(here == count - 1)
    def _():
        for h in range(heads_here):
            for k in range(count):
                dqkv_ref[k * rows : (k + 1) * rows, h * size : (h + 1) * size] = (
                    dq_ref[h, k].T.astype(bf16)
                )
        turned = (iota((rows, rows), 0) + iota((rows, rows), 1) == rows - 1).astype(f32)
        ids = bucket_of(2 * rows - 1 - iota((buckets, 4 * rows), 1))
        mine = ids == iota((buckets, 4 * rows), 0)
        bucket_rows = iota((buckets, 1), 0)
        lanes = iota((buckets, 128), 1)
        table = jnp.zeros((buckets, 128), f32)
        for h in range(heads_here):
            strip = jnp.concatenate(
                [forward_product_exact(turned, sums_ref[h, d]) for d in (3, 2, 1)]
                + [jnp.zeros((rows, rows), f32)],
                axis=1,
            )
            diagonals = jnp.sum(
                pltpu.roll(strip, 0, 1, stride=1, stride_axis=0), axis=0, keepdims=True
            )
            column = jnp.sum(jnp.where(mine, diagonals, 0.0), axis=1, keepdims=True)
            column = column + jnp.where(bucket_rows == buckets // 2 - 1, jnp.sum(sums_ref[h, 0]), 0.0)
            column = column + jnp.where(bucket_rows == buckets - 1, jnp.sum(sums_ref[h, 4]), 0.0)
            table = jnp.where(lanes == h, column, table)
        table_ref[...] = table


def collect_kernel(n, n_w, me_ref, *refs):
    blocks, (gate_up, out), results, sems = refs[:n], (refs[n : n + 2], refs[n + 2 : n + 4]), refs[-4:-1], refs[-1]
    me = me_ref[0]
    mine = lax.rem(me, n_w)
    rows, half, own = blocks[0].shape[0], gate_up[0].shape[0], out[0].shape[0]
    width = own * n_w // n
    copies = [
        pltpu.make_async_copy(block, results[0].at[k * rows : (k + 1) * rows], sems.at[k])
        for k, block in enumerate(blocks)
    ]
    for k, place in enumerate((mine, n_w - 1 - mine)):
        at = pl.ds(pl.multiple_of(place * half, half), half)
        copies.append(pltpu.make_async_copy(gate_up[k], results[1].at[at], sems.at[n + k]))
    for copy in copies:
        copy.start()
    for k in range(n):
        head = me ^ k
        source = pl.ds(pl.multiple_of(lax.rem(head, n // n_w) * width, width), width)
        target = results[2].at[k * width : (k + 1) * width]
        for which in range(2):
            copy = pltpu.make_async_copy(out[which].at[source], target, sems.at[n + 2 + k])

            @pl.when((head // (n // n_w) == mine) == (which == 0))
            def _():
                copy.start()

        copies.append(copy)
    for copy in copies:
        copy.wait()


def place_kernel(groups, part, units_all, hidden_units, heads_all, width, spot_ref, *refs):
    spot = spot_ref[0]
    wide, refs = refs[: 4 * groups], refs[4 * groups :]
    narrow, refs = refs[: 2 * groups], refs[2 * groups :]
    outs, scratch, sems = refs[:7], refs[7:-1], refs[-1]
    gate, up, down, turned, query, key, value, out_rows, out_turned = scratch
    count = heads_all // width
    units = units_all // count
    middle = 3 * units // 2

    def row_of(j, h):
        index = lax.rem(spot + groups - j, groups) if h == 0 else lax.rem(spot + j, groups)
        return pl.multiple_of((2 * index + h) * part, 8)

    def copy(k, source):
        return pltpu.make_async_copy(source, outs[k], sems.at[k])

    def gather(target, t):
        for c in range(2):
            low, high = max(c * middle, t * units), min((c + 1) * middle, (t + 1) * units)
            for r in range(count):
                first = r * units + low - t * units
                size = min(high - low, hidden_units - first)
                if low >= high or size <= 0:
                    continue
                start = r * middle + low - c * middle
                for j in range(groups):
                    for h in range(2):
                        block = wide[(j * 2 + c) * 2 + h]
                        target[pl.ds(row_of(j, h), part), first : first + size] = (
                            block[:, start : start + size].astype(f32)
                        )

    gather(gate, 0)
    copy(0, gate).start()
    gather(up, 1)
    copy(1, up).start()
    gather(down, 2)
    for first in range(0, hidden_units, 128):
        turned[first : first + 128, :] = down[:, first : first + 128].T
    copy(2, turned).start()
    for k, target in enumerate((query, key, value)):
        for j in range(groups):
            for h in range(2):
                target[pl.ds(row_of(j, h), part), :] = (
                    narrow[j * 2 + h][:, k * heads_all : (k + 1) * heads_all].astype(f32)
                )
        copy(3 + k, target).start()
    for q in range(count):
        for j in range(groups):
            for h in range(2):
                first = 3 * heads_all + q * width
                out_rows[q, pl.ds(row_of(j, h), part), :] = (
                    narrow[j * 2 + h][:, first : first + width].astype(f32)
                )
        rows = out_rows.shape[1]
        out_turned[:, q * rows : (q + 1) * rows] = out_rows[q].T
    copy(6, out_turned).start()
    for k, source in enumerate((gate, up, turned, query, key, value, out_turned)):
        copy(k, source).wait()


def forward_product_exact(left_side, right_side):
    return dot(left_side, right_side, ((1,), (0,)), highest)


def whole(shape):
    return pl.BlockSpec(shape, lambda *_: (0,) * len(shape))


def per_device(
    sizes,
    inputs,
    out_grad,
    lengths,
    permutation,
    gain_attention,
    query_weight,
    key_weight,
    value_weight,
    out_weight,
    bucket_bias,
    gain_feedforward,
    gate_weight,
    up_weight,
    down_weight,
):
    n_group, n_ctx, n_w = sizes
    n = n_ctx * n_w
    fast = (n_group, n_ctx, n_w) == (8, 2, 2)
    rows, model = inputs.shape
    buckets, heads = bucket_bias.shape
    hidden_units = gate_weight.shape[1]
    size = query_weight.shape[1] // heads
    seqs = lengths.shape[1]
    tokens = rows * n
    heads_here = -(-heads // n)
    width = heads_here * size
    units = -(-hidden_units // (128 * n)) * 128
    ctx, wsh = lax.axis_index("ctx"), lax.axis_index("wshard")
    me = lax.axis_index(peer_axes)
    rank = wsh * n_ctx + ctx
    flip_w = [(0, 1), (1, 0)]


    def mate(block):
        return lax.ppermute(block, "wshard", flip_w)

    def across(block):
        return lax.ppermute(block, "ctx", flip_w)

    def to_relative(stacked):
        return jnp.take(stacked, me ^ lax.iota(jnp.int32, n), axis=0)

    def gather_blocks(block):
        if fast:
            far = across(block)
            return [block, mate(block), far, mate(far)]
        stacked = to_relative(lax.all_gather(block, peer_axes, axis=0, tiled=False))
        return [stacked[k] for k in range(n)]

    def columns_of(weight, which, wide):
        over = max(0, n * wide - weight.shape[1])
        padded = jnp.pad(weight, ((0, 0), (0, over))) if over else weight
        return lax.dynamic_slice_in_dim(padded, which * wide, wide, 1)

    def own_columns(parts, wide, which):
        return jnp.concatenate([columns_of(part, which, wide) for part in parts], axis=1)

    def in_order(mine, given):
        upper = jnp.where(wsh == 0, mine, given)
        lower = jnp.where(wsh == 0, given, mine)
        return jnp.concatenate([upper, lower], axis=0)

    hold = lax.optimization_barrier

    if fast:
        row_far, row_mate = across(inputs), mate(inputs)
    heads_mine = (query_weight, key_weight, value_weight)
    heads_given = [mate(weight) for weight in heads_mine]
    out_other = mate(out_weight)
    gate_up_mine = own_columns((gate_weight, up_weight), units, rank)
    gate_up_sent = own_columns((gate_weight, up_weight), units, (1 - wsh) * n_ctx + ctx)
    half = down_weight.shape[0]
    extra = n_ctx * units - half
    down_other = mate(down_weight[:extra])
    down_wide = jnp.concatenate(
        [
            down_weight,
            jnp.where(wsh == 0, down_other, jnp.zeros_like(down_other)),
            jnp.zeros_like(down_other),
        ]
    )
    down_own = lax.dynamic_slice_in_dim(down_wide, wsh * extra + ctx * units, units, 0)
    me_1 = me.reshape(1).astype(jnp.int32)
    order = permutation.reshape(n, rows)
    params = pltpu.CompilerParams(vmem_limit_bytes=vmem_bytes)
    qkv_weight = pl.pallas_call(
        functools.partial(own_heads_kernel, width, n, n_w),
        out_shape=jax.ShapeDtypeStruct((model, 3 * width), bf16),
        in_specs=[pl.BlockSpec(memory_space=pltpu.SMEM)]
        + [pl.BlockSpec(memory_space=pltpu.VMEM)] * 6,
        out_specs=pl.BlockSpec(memory_space=pltpu.VMEM),
        compiler_params=params,
        name="own_heads",
    )(me_1, *heads_mine, *heads_given)
    bias = pl.pallas_call(
        functools.partial(bias_kernel, rows, heads_here, heads, buckets),
        out_shape=jax.ShapeDtypeStruct((heads_here, 5, rows, rows), f32),
        in_specs=[
            pl.BlockSpec(memory_space=pltpu.SMEM),
            pl.BlockSpec(memory_space=pltpu.SMEM),
        ],
        out_specs=pl.BlockSpec(memory_space=pltpu.VMEM),
        compiler_params=params,
        name="bias_strips",
    )(me_1, bucket_bias)
    if fast:
        row_far, out_grad, qkv_weight, bias, gate_up_mine, gate_up_sent = hold(
            (row_far, out_grad, qkv_weight, bias, gate_up_mine, gate_up_sent)
        )
        row_blocks = [inputs, row_mate, row_far, mate(row_far)]
    else:
        row_blocks = gather_blocks(inputs)
    gate_up_given = mate(gate_up_sent)
    dy_blocks = gather_blocks(out_grad)

    x_all, normed, qkv = pl.pallas_call(
        functools.partial(arrange_kernel, rows, n),
        out_shape=(
            jax.ShapeDtypeStruct((tokens, model), bf16),
            jax.ShapeDtypeStruct((tokens, model), bf16),
            jax.ShapeDtypeStruct((tokens, 3 * width), bf16),
        ),
        grid_spec=pltpu.PrefetchScalarGridSpec(
            num_scalar_prefetch=1,
            grid=(n,),
            in_specs=[whole((n, rows)), whole((1, model)), whole((model, 3 * width))]
            + [whole((rows, model))] * n,
            out_specs=[
                pl.BlockSpec((rows, model), lambda t, *_: (t, 0)),
                pl.BlockSpec((rows, model), lambda t, *_: (t, 0)),
                pl.BlockSpec((rows, 3 * width), lambda t, *_: (t, 0)),
            ],
        ),
        compiler_params=params,
        cost_estimate=pl.CostEstimate(
            flops=2 * tokens * model * (tokens + 3 * width),
            bytes_accessed=8 * tokens * model,
            transcendentals=0,
        ),
        name="arrange_project",
    )(me_1, order, gain_attention.reshape(1, model), qkv_weight, *row_blocks)
    lengths_row = lengths.reshape(seqs)
    attended, attended_wide, lse = pl.pallas_call(
        functools.partial(attend_kernel, rows, n, heads_here, size, seqs),
        out_shape=(
            jax.ShapeDtypeStruct((tokens, width), bf16),
            jax.ShapeDtypeStruct((tokens, width), f32),
            jax.ShapeDtypeStruct((heads_here, tokens), f32),
        ),
        grid_spec=pltpu.PrefetchScalarGridSpec(
            num_scalar_prefetch=2,
            grid=(n,),
            in_specs=[whole((tokens, 3 * width)), whole((heads_here, 5, rows, rows))],
            out_specs=[
                pl.BlockSpec((rows, width), lambda t, *_: (t, 0)),
                pl.BlockSpec((rows, width), lambda t, *_: (t, 0)),
                pl.BlockSpec((heads_here, rows), lambda t, *_: (0, t)),
            ],
        ),
        compiler_params=params,
        cost_estimate=pl.CostEstimate(
            flops=16 * tokens * tokens * width,
            bytes_accessed=16 * tokens * width,
            transcendentals=tokens * tokens * heads_here,
        ),
        name="attend",
    )(me_1, lengths_row, qkv, bias)

    strip = model // n // n_group
    part = strip // 2
    if fast:
        group = lax.axis_index("group")
        spot = jnp.where(group % 2 == 0, group // 2, n_group - 1 - group // 2)
        ahead = [(ladder_ring[k], ladder_ring[(k + 1) % n_group]) for k in range(n_group)]
        behind = [(b, a) for a, b in ahead]

    def forward(block):
        return lax.ppermute(block, "group", ahead)

    def backward(block):
        return lax.ppermute(block, "group", behind)

    def diagonal(block):
        return lax.ppermute(block, peer_axes, [(q, q ^ 3) for q in range(n)])

    def pick(array, index, axis):
        return lax.squeeze(lax.dynamic_slice_in_dim(array, index, 1, axis), (axis,))

    def rank_of(k):
        peer = me ^ k
        return (peer % n_w) * n_ctx + peer // n_w

    def ring(take, swap, pieces):
        both_ways = (forward, backward)
        one, two = take(0, lax.rem(spot + 7, n_group)), take(1, lax.rem(spot + 1, n_group))
        for s in range(n_group - 1):
            came = yield (one, two), both_ways
            one = came[0] + take(0, lax.rem(spot + 14 - s, n_group))
            two = came[1] + take(1, lax.rem(spot + 2 + s, n_group))
        pairs, (blocks, join) = [], swap(one, two)
        for block in blocks:
            came = yield tuple(block[1:]), (mate, across, diagonal)
            pairs.append(join([block[0], *came]))
        for pair in pairs:
            pieces.extend(pair)
        for s in range(n_group - 1):
            for c, pair in enumerate(pairs):
                pairs[c] = yield pair, both_ways
                pieces.extend(pairs[c])

    class Stream:
        def __init__(self, steps):
            self.steps, self.result, self.came = steps, None, None
            self.pending = next(steps)

        def advance(self, came):
            try:
                self.pending = self.steps.send(came)
            except StopIteration as stop:
                self.pending, self.result = None, stop.value

    order_token = [me]

    def tick(values, *streams):
        live = [stream for stream in streams if stream is not None and stream.pending is not None]
        if not live:
            return values
        arrived, values = hold(([stream.came for stream in live if stream.came], values))
        for stream in live:
            if stream.came:
                stream.advance(arrived.pop(0))
        live = [stream for stream in live if stream.pending is not None]
        operands, values, order_token[0] = hold(
            ([stream.pending[0] for stream in live], values, order_token[0])
        )
        for stream, sent in zip(live, operands):
            stream.came = [send(x) for send, x in zip(stream.pending[1], sent)]
        return values

    def piece_of(cut, index, h):
        zero = jnp.zeros((), index.dtype)
        starts = (zero, index, zero + h, zero, zero)
        return lax.squeeze(
            lax.dynamic_slice(cut, starts, (n, 1, 1, part, cut.shape[4])), (1, 2)
        )

    def rows_cut(grad):
        return grad.reshape(n, n_group, 2, part, grad.shape[1])

    wide_pieces, narrow_pieces = [], []

    def wide_ring(grad_gate_up, grad_down):
        one, two = rows_cut(grad_gate_up), rows_cut(grad_down)

        def take(h, index):
            return jnp.concatenate([piece_of(x, index, h) for x in (one, two)], axis=-1)

        def swap(one, two):
            both = jnp.stack([one, two], axis=1)
            middle = 3 * units // 2

            def join(came):
                full = jnp.zeros((2, part, n * middle), bf16)
                for k in range(n):
                    full = lax.dynamic_update_slice_in_dim(full, came[k], rank_of(k) * middle, 2)
                return full[0], full[1]

            halves = [both[..., :middle], both[..., middle:]]
            return [[pick(half, me ^ k, 0) for k in range(n)] for half in halves], join

        return ring(take, swap, wide_pieces)

    def small_ring(grad_qkv, grad_out):
        one, two = rows_cut(grad_qkv), rows_cut(grad_out)

        def take(h, index):
            return jnp.concatenate([piece_of(x, index, h) for x in (one, two)], axis=-1)

        def swap(one, two):
            both = jnp.stack([one, two], axis=1)
            own = jnp.concatenate([both[k, :, :, 3 * width :] for k in range(n)], axis=2)

            def join(came):
                stacked = jnp.stack(came)
                came = [pick(stacked, me ^ r, 0) for r in range(n)]
                full = jnp.concatenate(
                    [came[r][:, :, k * width : (k + 1) * width] for k in range(3) for r in range(n)]
                    + [own],
                    axis=2,
                )
                return full[0], full[1]

            return [[pick(both, me ^ k, 0)[:, :, : 3 * width] for k in range(n)]], join

        return ring(take, swap, narrow_pieces)

    def sum_ring(small):
        for axis, bit, count in (
            ("wshard", 1, n_w),
            ("ctx", 1, n_ctx),
            ("group", 1, n_group),
            ("group", 2, n_group),
            ("group", 4, n_group),
        ):
            pairs = [(g, g ^ bit) for g in range(count)]
            came = yield (small,), (lambda x: lax.ppermute(x, axis, pairs),)
            small = small + came[0]
        return small

    def scatter_near(partial):
        sent = partial.reshape(n, rows, -1)
        if not fast:
            total = lax.psum_scatter(to_relative(sent), peer_axes, scatter_dimension=0, tiled=False)
            return total.astype(f32), None
        got = mate(jnp.stack([sent[1], sent[3]]))
        near = sent[0].astype(f32) + got[0].astype(f32)
        return near, (sent[2].astype(f32) + got[1].astype(f32)).astype(bf16)

    def scatter_far(near, away):
        return near + across(away).astype(f32) if fast else near

    attended, out_mine, out_other, gate_up_mine = hold(
        (attended, out_weight, out_other, gate_up_mine)
    )
    if fast:
        attended_far, attended_mate = across(attended), mate(attended)
        anywhere = pl.BlockSpec(memory_space=pl.ANY)
        shapes = [(tokens, model), (model, 2 * units), (n * width, model)]
        dy, gate_up, out_relative = pl.pallas_call(
            functools.partial(collect_kernel, n, n_w),
            out_shape=[jax.ShapeDtypeStruct(shape, bf16) for shape in shapes],
            in_specs=[pl.BlockSpec(memory_space=pltpu.SMEM)] + [anywhere] * (n + 4),
            out_specs=[anywhere] * 3,
            scratch_shapes=[pltpu.SemaphoreType.DMA((2 * n + 2,))],
            compiler_params=params,
            cost_estimate=pl.CostEstimate(
                flops=0,
                bytes_accessed=4 * sum(a * b for a, b in shapes),
                transcendentals=0,
            ),
            name="collect",
        )(me_1, *dy_blocks, gate_up_mine, gate_up_given, out_mine, out_other)
        attended_far, dy, gate_up, out_relative = hold((attended_far, dy, gate_up, out_relative))
        attended_blocks = [attended, attended_mate, attended_far, mate(attended_far)]
    else:
        dy = jnp.concatenate(dy_blocks)
        gate_up = in_order(gate_up_mine, gate_up_given)
        attended_blocks = gather_blocks(attended)
        out_full = in_order(out_mine, out_other)
        out_full = jnp.pad(out_full, ((0, n * width - out_full.shape[0]), (0, 0)))
        out_relative = jnp.concatenate(
            [lax.dynamic_slice_in_dim(out_full, (me ^ k) * width, width, 0) for k in range(n)]
        )
    by_rows = [
        jnp.concatenate(
            [attended_blocks[k][(m ^ k) * rows : ((m ^ k) + 1) * rows] for m in range(n)]
        )
        for k in range(n)
    ]
    attended_all = jnp.concatenate(by_rows, axis=1)
    residual_all = x_all.astype(f32) + forward_product(
        attended_all, out_relative
    )
    residual = residual_all[:rows]
    normed_ff = rms_norm(residual_all, gain_feedforward).astype(bf16)
    gate_up_proj = forward_product(normed_ff, gate_up)
    gate_proj, up_proj = gate_up_proj[:, :units], gate_up_proj[:, units:]

    def activate(gate_in, up_in):
        return jax.nn.gelu(gate_in, approximate=True) * up_in

    hidden_wide, activate_back = jax.vjp(activate, gate_proj, up_proj)
    hidden = hidden_wide.astype(bf16)
    d_hidden = backward_product(dy, down_own)
    d_gate_wide, d_up_wide = activate_back(d_hidden)
    d_gate_up = jnp.concatenate([d_gate_wide.astype(bf16), d_up_wide.astype(bf16)], axis=1)

    grad_gate_up = weight_product(normed_ff, d_gate_up).astype(bf16)
    grad_down = weight_product(dy, hidden).astype(bf16)
    wide = Stream(wide_ring(grad_gate_up, grad_down)) if fast else None
    d_gate_up, hidden = tick((d_gate_up, hidden), wide)

    back = backward_product(d_gate_up, gate_up).astype(bf16)
    back, hidden = tick((back, hidden), wide)
    near, away = scatter_near(back)
    out_partial = forward_product(hidden, down_own).astype(bf16)
    near, away, out_partial = tick((near, away, out_partial), wide)
    d_normed_ff = scatter_far(near, away)
    d_normed_ff, residual = tick((d_normed_ff, residual), wide)
    norm_ff_back = jax.vjp(rms_norm, residual, gain_feedforward)[1]
    d_residual_norm, grad_gain_ff = norm_ff_back(d_normed_ff)
    d_residual = out_grad.astype(f32) + d_residual_norm
    branch = d_residual.astype(bf16)

    if fast:
        d_rows = backward_product(branch, out_relative).astype(bf16)
        d_rows = [d_rows[:, k * width : (k + 1) * width] for k in range(n)]
        d_rows = [d_rows[0], mate(d_rows[1]), across(d_rows[2]), diagonal(d_rows[3])]
        d_attended, branch = hold((jnp.concatenate(d_rows), branch))
    else:
        branch_blocks = gather_blocks(branch)
        d_attended = backward_product(jnp.concatenate(branch_blocks), out_relative[:width]).astype(bf16)
    d_attended, branch = tick((d_attended, branch), wide)
    if fast:
        branch_blocks = gather_blocks(branch)
    d_qkv, d_table = pl.pallas_call(
        functools.partial(attend_back_kernel, rows, n, heads_here, size, seqs, buckets),
        out_shape=(
            jax.ShapeDtypeStruct((tokens, 3 * width), bf16),
            jax.ShapeDtypeStruct((buckets, 128), f32),
        ),
        grid_spec=pltpu.PrefetchScalarGridSpec(
            num_scalar_prefetch=2,
            grid=(n,),
            in_specs=[
                whole((tokens, 3 * width)),
                whole((heads_here, 5, rows, rows)),
                whole((heads_here, tokens)),
                whole((tokens, width)),
                whole((tokens, width)),
            ],
            out_specs=[whole((tokens, 3 * width)), whole((buckets, 128))],
            scratch_shapes=[
                pltpu.VMEM((heads_here, n, size, rows), f32),
                pltpu.VMEM((heads_here, 5, rows, rows), f32),
                pltpu.VMEM((heads_here, tokens), f32),
            ],
        ),
        compiler_params=params,
        cost_estimate=pl.CostEstimate(
            flops=40 * tokens * tokens * width,
            bytes_accessed=16 * tokens * width,
            transcendentals=tokens * tokens * heads_here,
        ),
        name="attend_back",
    )(me_1, lengths_row, qkv, bias, lse, attended_wide, d_attended)
    d_qkv, branch_far, out_partial = tick((d_qkv, branch_blocks[2], out_partial), wide)
    branch_blocks[2] = branch_far
    grad_qkv = weight_product(normed, d_qkv).astype(bf16)
    grad_out = sum(
        weight_product(branch_blocks[k], attended[k * rows : (k + 1) * rows]) for k in range(n)
    ).astype(bf16)
    grad_qkv, grad_out = [
        with_layout_constraint(grad, Layout(major_to_minor=(0, 1))) for grad in (grad_qkv, grad_out)
    ]
    grad_qkv, grad_out, d_qkv = tick((grad_qkv, grad_out, d_qkv), wide)
    back = backward_product(d_qkv, qkv_weight).astype(bf16)
    narrow = Stream(small_ring(grad_qkv, grad_out)) if fast else None
    (back,) = tick((back,), wide, narrow)

    near, away = scatter_near(back)
    near, away = tick((near, away), narrow)
    (away,) = tick((away,), wide)
    d_normed = scatter_far(near, away)
    tick((), narrow)
    tick((), wide)
    d_normed, x_own = tick((d_normed, x_all[:rows]), narrow)
    norm_attn_back = jax.vjp(rms_norm, x_own.astype(f32), gain_attention)[1]
    d_input_norm, grad_gain_attn = norm_attn_back(d_normed)
    input_grad = (d_residual + d_input_norm).astype(bf16)
    out_near, out_away = scatter_near(out_partial)
    out_away, grad_gain_attn = tick((out_away, grad_gain_attn), wide)
    outputs = (residual + scatter_far(out_near, out_away)).astype(bf16)

    table_here = jnp.pad(d_table[:, :heads_here], ((0, 0), (0, n * heads_here)))
    table_here = jnp.roll(table_here, me * heads_here, axis=1)[:, :heads]
    small = jnp.concatenate([grad_gain_attn, grad_gain_ff, table_here.reshape(-1)])
    if fast:
        sums = Stream(sum_ring(small))
        while wide.pending or narrow.pending or sums.pending:
            tick((), narrow, sums)
            tick((), wide)
        small = sums.result
    else:
        small = lax.psum(small, ("group",) + peer_axes)
    share = model // n
    gains = [lax.dynamic_slice_in_dim(small, k * model + order_token[0] * share, share) for k in range(2)]
    grad_table = small[2 * model :].reshape(buckets, heads)

    if fast:
        own_rows, all_heads = model // n, n * width
        wide_shape, down_shape = (own_rows, hidden_units), (hidden_units, own_rows)
        out_shapes = [wide_shape, wide_shape, down_shape]
        out_shapes += [(own_rows, all_heads)] * 3 + [(width, model)]
        scratch = [wide_shape, wide_shape, wide_shape, down_shape]
        scratch += [(own_rows, all_heads)] * 3 + [(n, own_rows, width), (width, model)]
        total_gate, total_up, total_down, *total_qkv, total_out = pl.pallas_call(
            functools.partial(
                place_kernel, n_group, part, n * units, hidden_units, all_heads, width
            ),
            out_shape=[jax.ShapeDtypeStruct(shape, f32) for shape in out_shapes],
            in_specs=[pl.BlockSpec(memory_space=pltpu.SMEM)]
            + [pl.BlockSpec(memory_space=pltpu.VMEM)] * (6 * n_group),
            out_specs=[pl.BlockSpec(memory_space=pl.ANY)] * 7,
            scratch_shapes=[pltpu.VMEM(shape, f32) for shape in scratch]
            + [pltpu.SemaphoreType.DMA((7,))],
            compiler_params=params,
            name="place",
        )(spot.reshape(1).astype(jnp.int32), *wide_pieces, *narrow_pieces)
    else:

        def place_columns(grad, which, wide, total):
            full = jnp.zeros((grad.shape[0], n * wide), bf16)
            full = lax.dynamic_update_slice_in_dim(full, grad, which * wide, 1)
            return full[:, :total]

        def finish(full, dim):
            full = lax.psum_scatter(full, peer_axes, scatter_dimension=dim, tiled=True)
            return lax.psum(full, "group").astype(f32)

        total_qkv = [
            finish(
                place_columns(grad_qkv[:, k * width : (k + 1) * width], me, width, heads * size), 0
            )
            for k in range(3)
        ]
        total_out = finish(place_columns(grad_out, me, width, heads * size).T, 0)
        total_gate = finish(place_columns(grad_gate_up[:, :units], rank, units, hidden_units), 0)
        total_up = finish(place_columns(grad_gate_up[:, units:], rank, units, hidden_units), 0)
        total_down = finish(place_columns(grad_down, rank, units, hidden_units).T, 1)
    return (
        outputs,
        input_grad,
        gains[0],
        total_qkv[0],
        total_qkv[1],
        total_qkv[2],
        total_out,
        grad_table,
        gains[1],
        total_gate,
        total_up,
        total_down,
    )


def solution(mesh):
    sizes = (mesh.shape["group"], mesh.shape["ctx"], mesh.shape["wshard"])
    return jax.shard_map(
        functools.partial(per_device, sizes),
        mesh=mesh,
        in_specs=(
            P(("group", "ctx", "wshard"), None),
            P(("group", "ctx", "wshard"), None),
            P("group", None),
            P("group", None),
            P(),
            P("wshard", None),
            P("wshard", None),
            P("wshard", None),
            P("wshard", None),
            P(),
            P(),
            P("wshard", None),
            P("wshard", None),
            P("wshard", None),
        ),
        out_specs=(
            P(("group", "ctx", "wshard"), None),
            P(("group", "ctx", "wshard"), None),
            P(("ctx", "wshard")),
            P(("ctx", "wshard"), None),
            P(("ctx", "wshard"), None),
            P(("ctx", "wshard"), None),
            P(("ctx", "wshard"), None),
            P(),
            P(("ctx", "wshard")),
            P(("ctx", "wshard"), None),
            P(("ctx", "wshard"), None),
            P(None, ("ctx", "wshard")),
        ),
        check_vma=False,
    )
```

```python
import functools

import jax
import jax.numpy as jnp
from jax import lax
from jax.experimental import pallas as pl
from jax.experimental.layout import Layout, with_layout_constraint
from jax.experimental.pallas import tpu as pltpu
from jax.sharding import PartitionSpec as P

epsilon = 1e-06
highest = lax.Precision.HIGHEST
thresholds = (12, 16, 23, 32, 46, 64, 91)
masked_out = -1e30
bf16 = jnp.bfloat16
f32 = jnp.float32
peer_axes = ("ctx", "wshard")
vmem_bytes = 60 * 1024 * 1024

ladder_ring = (0, 2, 4, 6, 7, 5, 3, 1)


def bucket_of(offset):
    distance = jnp.abs(offset)
    beyond = 8 + sum(((distance >= border).astype(jnp.int32) for border in thresholds))
    near_far = jnp.where(distance < 8, distance, beyond)
    return jnp.where(offset > 0, 16, 0) + near_far


def rms_norm(values, gain_vector):
    return (
        values
        * lax.rsqrt(jnp.mean(values * values, axis=-1, keepdims=True) + epsilon)
        * gain_vector
    )


def dot(left_side, right_side, dims, precision=None):
    return lax.dot_general(
        left_side, right_side, (dims, ((), ())), precision=precision, preferred_element_type=f32
    )


def forward_product(left_side, right_side):
    return dot(left_side, right_side, ((1,), (0,)))


def backward_product(left_side, right_side):
    return dot(left_side, right_side, ((1,), (1,)))


def weight_product(left_side, right_side):
    return dot(left_side, right_side, ((0,), (0,)))


def iota(shape, dim):
    return lax.broadcasted_iota(jnp.int32, shape, dim)


def arrange_kernel(rows, count, me_ref, order_ref, gain_ref, weight_ref, *refs):
    blocks, (x_ref, normed_ref, qkv_ref) = refs[:-3], refs[-3:]
    me = me_ref[0]
    first = (me ^ pl.program_id(0)) * rows
    tokens = first + iota((rows, rows), 0)
    total = None
    for k in range(count):
        places = order_ref[pl.ds(me ^ k, 1), :]
        chosen = (places == tokens).astype(f32).astype(bf16)
        part = forward_product(chosen, blocks[k][...])
        total = part if total is None else total + part
    x_ref[...] = total.astype(bf16)
    normed = rms_norm(total, gain_ref[...]).astype(bf16)
    normed_ref[...] = normed
    qkv_ref[...] = forward_product(normed, weight_ref[...]).astype(bf16)


def own_heads_kernel(width, count, n_w, me_ref, *refs):
    mine, given, out_ref = refs[:3], refs[3:6], refs[6]
    me = me_ref[0]
    half, columns = mine[0].shape
    for m in range(count):

        @pl.when(me == m)
        def _():
            for t in range(3):
                for w in range(n_w):
                    source = mine[t] if m % n_w == w else given[t]
                    place = slice(w * half, (w + 1) * half), slice(t * width, (t + 1) * width)
                    if (m + 1) * width <= columns:
                        out_ref[place] = source[:, m * width : (m + 1) * width]
                    else:
                        out_ref[place] = jnp.zeros((half, width), out_ref.dtype)


def bias_kernel(rows, heads_here, heads, buckets, me_ref, table_ref, out_ref):
    lanes = iota((8, 4 * rows), 1)
    ids = bucket_of(2 * rows - lanes)
    for h in range(heads_here):
        head = jnp.minimum(me_ref[0] * heads_here + h, heads - 1)
        base = jnp.zeros((8, 4 * rows), f32)
        for b in range(buckets):
            base = jnp.where(ids == b, table_ref[b, head], base)
        wide = jnp.broadcast_to(base[0:1], (rows, 4 * rows))
        rolled = pltpu.roll(wide, 0, 1, stride=1, stride_axis=0)
        out_ref[h, 0] = jnp.full((rows, rows), table_ref[buckets // 2 - 1, head], f32)
        out_ref[h, 4] = jnp.full((rows, rows), table_ref[buckets - 1, head], f32)
        for delta in (1, 0, -1):
            start = rows + rows * (1 - delta)
            out_ref[h, delta + 2] = rolled[:, start : start + rows]


def span_of(lengths_ref, seqs, first, last, rows, total):
    low, high, end = 0, total, 0
    ends = []
    for s in range(seqs):
        end = end + lengths_ref[s]
        ends.append(end)
    for s in range(seqs):
        low = jnp.where(ends[s] <= first, ends[s], low)
    for s in reversed(range(seqs)):
        high = jnp.where(ends[s] > last, ends[s], high)
    high = jnp.minimum(high, total)
    return ends, low // rows, (high + rows - 1) // rows


def sequence_ids(ends, first, shape, dim):
    places = first + iota(shape, dim)
    ids = jnp.zeros(shape, jnp.int32)
    for end in ends:
        ids = ids + (places >= end).astype(jnp.int32)
    return ids


def attend_kernel(
    rows, count, heads_here, size, seqs, me_ref, lengths_ref, qkv_ref, bias_ref, att_ref, wide_ref, lse_ref
):
    me = me_ref[0]
    width = heads_here * size
    here = pl.program_id(0)
    block = me ^ here
    ends, low, high = span_of(
        lengths_ref, seqs, block * rows, block * rows + rows - 1, rows, count * rows
    )
    query_seq = sequence_ids(ends, block * rows, (1, rows), 1)
    start = pl.multiple_of(here * rows, rows)
    queries = qkv_ref[pl.ds(start, rows), :][:, :width]

    def step(key_block, carry):
        at = pl.multiple_of((key_block ^ me) * rows, rows)
        own = qkv_ref[pl.ds(at, rows), :]
        delta = jnp.clip(key_block - block, -2, 2) + 2
        same = sequence_ids(ends, key_block * rows, (rows, 1), 0) == query_seq
        after = []
        for h in range(heads_here):
            top, total, acc = carry[h]
            query = queries[:, h * size : (h + 1) * size]
            key = own[:, width + h * size : width + (h + 1) * size]
            value = own[:, 2 * width + h * size : 2 * width + (h + 1) * size]
            scores = backward_product(key, query) + bias_ref[h, delta]
            scores = jnp.where(same, scores, masked_out)
            top_next = jnp.maximum(top, jnp.max(scores, axis=0, keepdims=True))
            probs = jnp.exp(scores - top_next)
            fade = jnp.exp(top - top_next)
            total = total * fade + jnp.sum(probs, axis=0, keepdims=True)
            acc = acc * fade + weight_product(value, probs.astype(bf16))
            after.append((top_next, total, acc))
        return tuple(after)

    fresh = (
        jnp.full((1, rows), masked_out, f32),
        jnp.zeros((1, rows), f32),
        jnp.zeros((size, rows), f32),
    )
    done = lax.fori_loop(low, high, step, (fresh,) * heads_here)
    for h in range(heads_here):
        top, total, acc = done[h]
        lse_ref[h : h + 1, :] = top + jnp.log(total)
        out = (acc / total).T
        wide_ref[:, h * size : (h + 1) * size] = out
        att_ref[:, h * size : (h + 1) * size] = out.astype(bf16)


def attend_back_kernel(
    rows,
    count,
    heads_here,
    size,
    seqs,
    buckets,
    me_ref,
    lengths_ref,
    qkv_ref,
    bias_ref,
    lse_ref,
    wide_ref,
    d_att_ref,
    dqkv_ref,
    table_ref,
    dq_ref,
    sums_ref,
    delta_ref,
):
    me = me_ref[0]
    width = heads_here * size
    here = pl.program_id(0)
    block = me ^ here

    @pl.when(here == 0)
    def _():
        dq_ref[...] = jnp.zeros_like(dq_ref)
        sums_ref[...] = jnp.zeros_like(sums_ref)
        for k in range(count):
            part = slice(k * rows, (k + 1) * rows)
            both = d_att_ref[part, :].astype(f32) * wide_ref[part, :]
            for h in range(heads_here):
                delta_ref[h : h + 1, part] = jnp.sum(
                    both[:, h * size : (h + 1) * size].T, axis=0, keepdims=True
                )

    ends, low, high = span_of(
        lengths_ref, seqs, block * rows, block * rows + rows - 1, rows, count * rows
    )
    key_seq = sequence_ids(ends, block * rows, (rows, 1), 0)
    start = pl.multiple_of(here * rows, rows)
    own = qkv_ref[pl.ds(start, rows), :]

    def step(query_block, carry):
        rel = query_block ^ me
        at = pl.multiple_of(rel * rows, rows)
        queries = qkv_ref[pl.ds(at, rows), :][:, :width]
        d_outs = d_att_ref[pl.ds(at, rows), :]
        near = jnp.clip(block - query_block, -2, 2) + 2
        same = key_seq == sequence_ids(ends, query_block * rows, (1, rows), 1)
        after = []
        for h in range(heads_here):
            d_key, d_value = carry[h]
            key = own[:, width + h * size : width + (h + 1) * size]
            value = own[:, 2 * width + h * size : 2 * width + (h + 1) * size]
            query = queries[:, h * size : (h + 1) * size]
            d_out = d_outs[:, h * size : (h + 1) * size]
            scores = backward_product(key, query) + bias_ref[h, near]
            lse = lse_ref[h : h + 1, pl.ds(at, rows)]
            soft = jnp.where(same, jnp.exp(scores - lse), 0.0)
            d_probs = backward_product(value, d_out)
            d_scores = (soft * (d_probs - delta_ref[h : h + 1, pl.ds(at, rows)])).astype(bf16)
            sums_ref[h, near] += d_scores.astype(f32)
            d_value = d_value + forward_product(soft.astype(bf16), d_out)
            d_key = d_key + forward_product(d_scores, query)
            dq_ref[h, rel] += weight_product(key, d_scores)
            after.append((d_key, d_value))
        return tuple(after)

    zero = jnp.zeros((rows, size), f32)
    done = lax.fori_loop(low, high, step, ((zero, zero),) * heads_here)
    for h in range(heads_here):
        d_key, d_value = done[h]
        dqkv_ref[pl.ds(start, rows), width + h * size : width + (h + 1) * size] = d_key.astype(bf16)
        dqkv_ref[pl.ds(start, rows), 2 * width + h * size : 2 * width + (h + 1) * size] = (
            d_value.astype(bf16)
        )

    @pl.when(here == count - 1)
    def _():
        for h in range(heads_here):
            for k in range(count):
                dqkv_ref[k * rows : (k + 1) * rows, h * size : (h + 1) * size] = (
                    dq_ref[h, k].T.astype(bf16)
                )
        turned = (iota((rows, rows), 0) + iota((rows, rows), 1) == rows - 1).astype(f32)
        ids = bucket_of(2 * rows - 1 - iota((buckets, 4 * rows), 1))
        mine = ids == iota((buckets, 4 * rows), 0)
        bucket_rows = iota((buckets, 1), 0)
        lanes = iota((buckets, 128), 1)
        table = jnp.zeros((buckets, 128), f32)
        for h in range(heads_here):
            strip = jnp.concatenate(
                [forward_product_exact(turned, sums_ref[h, d]) for d in (3, 2, 1)]
                + [jnp.zeros((rows, rows), f32)],
                axis=1,
            )
            diagonals = jnp.sum(
                pltpu.roll(strip, 0, 1, stride=1, stride_axis=0), axis=0, keepdims=True
            )
            column = jnp.sum(jnp.where(mine, diagonals, 0.0), axis=1, keepdims=True)
            column = column + jnp.where(bucket_rows == buckets // 2 - 1, jnp.sum(sums_ref[h, 0]), 0.0)
            column = column + jnp.where(bucket_rows == buckets - 1, jnp.sum(sums_ref[h, 4]), 0.0)
            table = jnp.where(lanes == h, column, table)
        table_ref[...] = table


def place_kernel(groups, part, units_all, hidden_units, heads_all, width, spot_ref, *refs):
    spot = spot_ref[0]
    wide, refs = refs[: 4 * groups], refs[4 * groups :]
    narrow, refs = refs[: 2 * groups], refs[2 * groups :]
    outs, scratch, sems = refs[:7], refs[7:-1], refs[-1]
    gate, up, down, turned, query, key, value, out_rows, out_turned = scratch
    count = heads_all // width
    units = units_all // count
    middle = 3 * units // 2

    def row_of(j, h):
        index = lax.rem(spot + groups - j, groups) if h == 0 else lax.rem(spot + j, groups)
        return pl.multiple_of((2 * index + h) * part, 8)

    def copy(k, source):
        return pltpu.make_async_copy(source, outs[k], sems.at[k])

    def gather(target, t):
        for c in range(2):
            low, high = max(c * middle, t * units), min((c + 1) * middle, (t + 1) * units)
            for r in range(count):
                first = r * units + low - t * units
                size = min(high - low, hidden_units - first)
                if low >= high or size <= 0:
                    continue
                start = r * middle + low - c * middle
                for j in range(groups):
                    for h in range(2):
                        block = wide[(j * 2 + c) * 2 + h]
                        target[pl.ds(row_of(j, h), part), first : first + size] = (
                            block[:, start : start + size].astype(f32)
                        )

    gather(gate, 0)
    copy(0, gate).start()
    gather(up, 1)
    copy(1, up).start()
    gather(down, 2)
    for first in range(0, hidden_units, 128):
        turned[first : first + 128, :] = down[:, first : first + 128].T
    copy(2, turned).start()
    for k, target in enumerate((query, key, value)):
        for j in range(groups):
            for h in range(2):
                target[pl.ds(row_of(j, h), part), :] = (
                    narrow[j * 2 + h][:, k * heads_all : (k + 1) * heads_all].astype(f32)
                )
        copy(3 + k, target).start()
    for q in range(count):
        for j in range(groups):
            for h in range(2):
                first = 3 * heads_all + q * width
                out_rows[q, pl.ds(row_of(j, h), part), :] = (
                    narrow[j * 2 + h][:, first : first + width].astype(f32)
                )
        rows = out_rows.shape[1]
        out_turned[:, q * rows : (q + 1) * rows] = out_rows[q].T
    copy(6, out_turned).start()
    for k, source in enumerate((gate, up, turned, query, key, value, out_turned)):
        copy(k, source).wait()


def forward_product_exact(left_side, right_side):
    return dot(left_side, right_side, ((1,), (0,)), highest)


def whole(shape):
    return pl.BlockSpec(shape, lambda *_: (0,) * len(shape))


def per_device(
    sizes,
    inputs,
    out_grad,
    lengths,
    permutation,
    gain_attention,
    query_weight,
    key_weight,
    value_weight,
    out_weight,
    bucket_bias,
    gain_feedforward,
    gate_weight,
    up_weight,
    down_weight,
):
    n_group, n_ctx, n_w = sizes
    n = n_ctx * n_w
    fast = (n_group, n_ctx, n_w) == (8, 2, 2)
    rows, model = inputs.shape
    buckets, heads = bucket_bias.shape
    hidden_units = gate_weight.shape[1]
    size = query_weight.shape[1] // heads
    seqs = lengths.shape[1]
    tokens = rows * n
    heads_here = -(-heads // n)
    width = heads_here * size
    units = -(-hidden_units // (128 * n)) * 128
    ctx, wsh = lax.axis_index("ctx"), lax.axis_index("wshard")
    me = lax.axis_index(peer_axes)
    rank = wsh * n_ctx + ctx
    flip_w = [(0, 1), (1, 0)]


    def mate(block):
        return lax.ppermute(block, "wshard", flip_w)

    def across(block):
        return lax.ppermute(block, "ctx", flip_w)

    def to_relative(stacked):
        return jnp.take(stacked, me ^ lax.iota(jnp.int32, n), axis=0)

    def gather_blocks(block):
        if fast:
            far = across(block)
            return [block, mate(block), far, mate(far)]
        stacked = to_relative(lax.all_gather(block, peer_axes, axis=0, tiled=False))
        return [stacked[k] for k in range(n)]

    def columns_of(weight, which, wide):
        over = max(0, n * wide - weight.shape[1])
        padded = jnp.pad(weight, ((0, 0), (0, over))) if over else weight
        return lax.dynamic_slice_in_dim(padded, which * wide, wide, 1)

    def own_columns(parts, wide, which):
        return jnp.concatenate([columns_of(part, which, wide) for part in parts], axis=1)

    def in_order(mine, given):
        upper = jnp.where(wsh == 0, mine, given)
        lower = jnp.where(wsh == 0, given, mine)
        return jnp.concatenate([upper, lower], axis=0)

    hold = lax.optimization_barrier

    if fast:
        row_far, row_mate = across(inputs), mate(inputs)
    heads_mine = (query_weight, key_weight, value_weight)
    heads_given = [mate(weight) for weight in heads_mine]
    out_other = mate(out_weight)
    gate_up_mine = own_columns((gate_weight, up_weight), units, rank)
    gate_up_sent = own_columns((gate_weight, up_weight), units, (1 - wsh) * n_ctx + ctx)
    half = down_weight.shape[0]
    extra = n_ctx * units - half
    down_other = mate(down_weight[:extra])
    down_wide = jnp.concatenate(
        [
            down_weight,
            jnp.where(wsh == 0, down_other, jnp.zeros_like(down_other)),
            jnp.zeros_like(down_other),
        ]
    )
    down_own = lax.dynamic_slice_in_dim(down_wide, wsh * extra + ctx * units, units, 0)
    me_1 = me.reshape(1).astype(jnp.int32)
    order = permutation.reshape(n, rows)
    params = pltpu.CompilerParams(vmem_limit_bytes=vmem_bytes)
    qkv_weight = pl.pallas_call(
        functools.partial(own_heads_kernel, width, n, n_w),
        out_shape=jax.ShapeDtypeStruct((model, 3 * width), bf16),
        in_specs=[pl.BlockSpec(memory_space=pltpu.SMEM)]
        + [pl.BlockSpec(memory_space=pltpu.VMEM)] * 6,
        out_specs=pl.BlockSpec(memory_space=pltpu.VMEM),
        compiler_params=params,
        name="own_heads",
    )(me_1, *heads_mine, *heads_given)
    bias = pl.pallas_call(
        functools.partial(bias_kernel, rows, heads_here, heads, buckets),
        out_shape=jax.ShapeDtypeStruct((heads_here, 5, rows, rows), f32),
        in_specs=[
            pl.BlockSpec(memory_space=pltpu.SMEM),
            pl.BlockSpec(memory_space=pltpu.SMEM),
        ],
        out_specs=pl.BlockSpec(memory_space=pltpu.VMEM),
        compiler_params=params,
        name="bias_strips",
    )(me_1, bucket_bias)
    if fast:
        row_far, out_grad, qkv_weight, bias, gate_up_mine, gate_up_sent = hold(
            (row_far, out_grad, qkv_weight, bias, gate_up_mine, gate_up_sent)
        )
        row_blocks = [inputs, row_mate, row_far, mate(row_far)]
    else:
        row_blocks = gather_blocks(inputs)
    gate_up_given = mate(gate_up_sent)
    dy = jnp.concatenate(gather_blocks(out_grad))

    x_all, normed, qkv = pl.pallas_call(
        functools.partial(arrange_kernel, rows, n),
        out_shape=(
            jax.ShapeDtypeStruct((tokens, model), bf16),
            jax.ShapeDtypeStruct((tokens, model), bf16),
            jax.ShapeDtypeStruct((tokens, 3 * width), bf16),
        ),
        grid_spec=pltpu.PrefetchScalarGridSpec(
            num_scalar_prefetch=1,
            grid=(n,),
            in_specs=[whole((n, rows)), whole((1, model)), whole((model, 3 * width))]
            + [whole((rows, model))] * n,
            out_specs=[
                pl.BlockSpec((rows, model), lambda t, *_: (t, 0)),
                pl.BlockSpec((rows, model), lambda t, *_: (t, 0)),
                pl.BlockSpec((rows, 3 * width), lambda t, *_: (t, 0)),
            ],
        ),
        compiler_params=params,
        cost_estimate=pl.CostEstimate(
            flops=2 * tokens * model * (tokens + 3 * width),
            bytes_accessed=8 * tokens * model,
            transcendentals=0,
        ),
        name="arrange_project",
    )(me_1, order, gain_attention.reshape(1, model), qkv_weight, *row_blocks)
    lengths_row = lengths.reshape(seqs)
    attended, attended_wide, lse = pl.pallas_call(
        functools.partial(attend_kernel, rows, n, heads_here, size, seqs),
        out_shape=(
            jax.ShapeDtypeStruct((tokens, width), bf16),
            jax.ShapeDtypeStruct((tokens, width), f32),
            jax.ShapeDtypeStruct((heads_here, tokens), f32),
        ),
        grid_spec=pltpu.PrefetchScalarGridSpec(
            num_scalar_prefetch=2,
            grid=(n,),
            in_specs=[whole((tokens, 3 * width)), whole((heads_here, 5, rows, rows))],
            out_specs=[
                pl.BlockSpec((rows, width), lambda t, *_: (t, 0)),
                pl.BlockSpec((rows, width), lambda t, *_: (t, 0)),
                pl.BlockSpec((heads_here, rows), lambda t, *_: (0, t)),
            ],
        ),
        compiler_params=params,
        cost_estimate=pl.CostEstimate(
            flops=16 * tokens * tokens * width,
            bytes_accessed=16 * tokens * width,
            transcendentals=tokens * tokens * heads_here,
        ),
        name="attend",
    )(me_1, lengths_row, qkv, bias)

    strip = model // n // n_group
    part = strip // 2
    if fast:
        group = lax.axis_index("group")
        spot = jnp.where(group % 2 == 0, group // 2, n_group - 1 - group // 2)
        ahead = [(ladder_ring[k], ladder_ring[(k + 1) % n_group]) for k in range(n_group)]
        behind = [(b, a) for a, b in ahead]

    def forward(block):
        return lax.ppermute(block, "group", ahead)

    def backward(block):
        return lax.ppermute(block, "group", behind)

    def diagonal(block):
        return lax.ppermute(block, peer_axes, [(q, q ^ 3) for q in range(n)])

    def pick(array, index, axis):
        return lax.squeeze(lax.dynamic_slice_in_dim(array, index, 1, axis), (axis,))

    def rank_of(k):
        peer = me ^ k
        return (peer % n_w) * n_ctx + peer // n_w

    def ring(take, swap, pieces):
        both_ways = (forward, backward)
        one, two = take(0, lax.rem(spot + 7, n_group)), take(1, lax.rem(spot + 1, n_group))
        for s in range(n_group - 1):
            came = yield (one, two), both_ways
            one = came[0] + take(0, lax.rem(spot + 14 - s, n_group))
            two = came[1] + take(1, lax.rem(spot + 2 + s, n_group))
        pairs, (blocks, join) = [], swap(one, two)
        for block in blocks:
            came = yield tuple(block[1:]), (mate, across, diagonal)
            pairs.append(join([block[0], *came]))
        for pair in pairs:
            pieces.extend(pair)
        for s in range(n_group - 1):
            for c, pair in enumerate(pairs):
                pairs[c] = yield pair, both_ways
                pieces.extend(pairs[c])

    class Stream:
        def __init__(self, steps):
            self.steps, self.result, self.came = steps, None, None
            self.pending = next(steps)

        def advance(self, came):
            try:
                self.pending = self.steps.send(came)
            except StopIteration as stop:
                self.pending, self.result = None, stop.value

    order_token = [me]

    def tick(values, *streams):
        live = [stream for stream in streams if stream is not None and stream.pending is not None]
        if not live:
            return values
        arrived, values = hold(([stream.came for stream in live if stream.came], values))
        for stream in live:
            if stream.came:
                stream.advance(arrived.pop(0))
        live = [stream for stream in live if stream.pending is not None]
        operands, values, order_token[0] = hold(
            ([stream.pending[0] for stream in live], values, order_token[0])
        )
        for stream, sent in zip(live, operands):
            stream.came = [send(x) for send, x in zip(stream.pending[1], sent)]
        return values

    def piece_of(cut, index, h):
        zero = jnp.zeros((), index.dtype)
        starts = (zero, index, zero + h, zero, zero)
        return lax.squeeze(
            lax.dynamic_slice(cut, starts, (n, 1, 1, part, cut.shape[4])), (1, 2)
        )

    def rows_cut(grad):
        return grad.reshape(n, n_group, 2, part, grad.shape[1])

    wide_pieces, narrow_pieces = [], []

    def wide_ring(grad_gate_up, grad_down):
        one, two = rows_cut(grad_gate_up), rows_cut(grad_down)

        def take(h, index):
            return jnp.concatenate([piece_of(x, index, h) for x in (one, two)], axis=-1)

        def swap(one, two):
            both = jnp.stack([one, two], axis=1)
            middle = 3 * units // 2

            def join(came):
                full = jnp.zeros((2, part, n * middle), bf16)
                for k in range(n):
                    full = lax.dynamic_update_slice_in_dim(full, came[k], rank_of(k) * middle, 2)
                return full[0], full[1]

            halves = [both[..., :middle], both[..., middle:]]
            return [[pick(half, me ^ k, 0) for k in range(n)] for half in halves], join

        return ring(take, swap, wide_pieces)

    def small_ring(grad_qkv, grad_out):
        one, two = rows_cut(grad_qkv), rows_cut(grad_out)

        def take(h, index):
            return jnp.concatenate([piece_of(x, index, h) for x in (one, two)], axis=-1)

        def swap(one, two):
            both = jnp.stack([one, two], axis=1)
            own = jnp.concatenate([both[k, :, :, 3 * width :] for k in range(n)], axis=2)

            def join(came):
                stacked = jnp.stack(came)
                came = [pick(stacked, me ^ r, 0) for r in range(n)]
                full = jnp.concatenate(
                    [came[r][:, :, k * width : (k + 1) * width] for k in range(3) for r in range(n)]
                    + [own],
                    axis=2,
                )
                return full[0], full[1]

            return [[pick(both, me ^ k, 0)[:, :, : 3 * width] for k in range(n)]], join

        return ring(take, swap, narrow_pieces)

    def sum_ring(small):
        for axis, bit, count in (
            ("wshard", 1, n_w),
            ("ctx", 1, n_ctx),
            ("group", 1, n_group),
            ("group", 2, n_group),
            ("group", 4, n_group),
        ):
            pairs = [(g, g ^ bit) for g in range(count)]
            came = yield (small,), (lambda x: lax.ppermute(x, axis, pairs),)
            small = small + came[0]
        return small

    def scatter_near(partial):
        sent = partial.reshape(n, rows, -1)
        if not fast:
            total = lax.psum_scatter(to_relative(sent), peer_axes, scatter_dimension=0, tiled=False)
            return total.astype(f32), None
        got = mate(jnp.stack([sent[1], sent[3]]))
        near = sent[0].astype(f32) + got[0].astype(f32)
        return near, (sent[2].astype(f32) + got[1].astype(f32)).astype(bf16)

    def scatter_far(near, away):
        return near + across(away).astype(f32) if fast else near

    attended, out_mine, out_other, gate_up_mine = hold(
        (attended, out_weight, out_other, gate_up_mine)
    )
    gate_up = in_order(gate_up_mine, gate_up_given)
    if fast:
        attended_far, attended_mate = across(attended), mate(attended)
        attended_far, gate_up = hold((attended_far, gate_up))
        attended_blocks = [attended, attended_mate, attended_far, mate(attended_far)]
    else:
        attended_blocks = gather_blocks(attended)
    out_full = in_order(out_mine, out_other)
    out_full = jnp.pad(out_full, ((0, n * width - out_full.shape[0]), (0, 0)))
    out_blocks = [lax.dynamic_slice_in_dim(out_full, (me ^ k) * width, width, 0) for k in range(n)]
    out_relative = jnp.concatenate(out_blocks, axis=0)
    by_rows = [
        jnp.concatenate(
            [attended_blocks[k][(m ^ k) * rows : ((m ^ k) + 1) * rows] for m in range(n)]
        )
        for k in range(n)
    ]
    attended_all = jnp.concatenate(by_rows, axis=1)
    residual_all = x_all.astype(f32) + forward_product(
        attended_all, out_relative
    )
    residual = residual_all[:rows]
    normed_ff = rms_norm(residual_all, gain_feedforward).astype(bf16)
    gate_up_proj = forward_product(normed_ff, gate_up)
    gate_proj, up_proj = gate_up_proj[:, :units], gate_up_proj[:, units:]

    def activate(gate_in, up_in):
        return jax.nn.gelu(gate_in, approximate=True) * up_in

    hidden_wide, activate_back = jax.vjp(activate, gate_proj, up_proj)
    hidden = hidden_wide.astype(bf16)
    d_hidden = backward_product(dy, down_own)
    d_gate_wide, d_up_wide = activate_back(d_hidden)
    d_gate_up = jnp.concatenate([d_gate_wide.astype(bf16), d_up_wide.astype(bf16)], axis=1)

    grad_gate_up = weight_product(normed_ff, d_gate_up).astype(bf16)
    grad_down = weight_product(dy, hidden).astype(bf16)
    wide = Stream(wide_ring(grad_gate_up, grad_down)) if fast else None
    d_gate_up, hidden = tick((d_gate_up, hidden), wide)

    back = backward_product(d_gate_up, gate_up).astype(bf16)
    back, hidden = tick((back, hidden), wide)
    near, away = scatter_near(back)
    out_partial = forward_product(hidden, down_own).astype(bf16)
    near, away, out_partial = tick((near, away, out_partial), wide)
    d_normed_ff = scatter_far(near, away)
    d_normed_ff, residual = tick((d_normed_ff, residual), wide)
    norm_ff_back = jax.vjp(rms_norm, residual, gain_feedforward)[1]
    d_residual_norm, grad_gain_ff = norm_ff_back(d_normed_ff)
    d_residual = dy[:rows].astype(f32) + d_residual_norm
    branch = d_residual.astype(bf16)

    if fast:
        d_rows = backward_product(branch, out_relative).astype(bf16)
        d_rows = [d_rows[:, k * width : (k + 1) * width] for k in range(n)]
        d_rows = [d_rows[0], mate(d_rows[1]), across(d_rows[2]), diagonal(d_rows[3])]
        d_attended, branch = hold((jnp.concatenate(d_rows), branch))
    else:
        branch_blocks = gather_blocks(branch)
        d_attended = backward_product(jnp.concatenate(branch_blocks), out_blocks[0]).astype(bf16)
    d_attended, branch = tick((d_attended, branch), wide)
    if fast:
        branch_blocks = gather_blocks(branch)
    d_qkv, d_table = pl.pallas_call(
        functools.partial(attend_back_kernel, rows, n, heads_here, size, seqs, buckets),
        out_shape=(
            jax.ShapeDtypeStruct((tokens, 3 * width), bf16),
            jax.ShapeDtypeStruct((buckets, 128), f32),
        ),
        grid_spec=pltpu.PrefetchScalarGridSpec(
            num_scalar_prefetch=2,
            grid=(n,),
            in_specs=[
                whole((tokens, 3 * width)),
                whole((heads_here, 5, rows, rows)),
                whole((heads_here, tokens)),
                whole((tokens, width)),
                whole((tokens, width)),
            ],
            out_specs=[whole((tokens, 3 * width)), whole((buckets, 128))],
            scratch_shapes=[
                pltpu.VMEM((heads_here, n, size, rows), f32),
                pltpu.VMEM((heads_here, 5, rows, rows), f32),
                pltpu.VMEM((heads_here, tokens), f32),
            ],
        ),
        compiler_params=params,
        cost_estimate=pl.CostEstimate(
            flops=40 * tokens * tokens * width,
            bytes_accessed=16 * tokens * width,
            transcendentals=tokens * tokens * heads_here,
        ),
        name="attend_back",
    )(me_1, lengths_row, qkv, bias, lse, attended_wide, d_attended)
    d_qkv, branch_far, out_partial = tick((d_qkv, branch_blocks[2], out_partial), wide)
    branch_blocks[2] = branch_far
    grad_qkv = weight_product(normed, d_qkv).astype(bf16)
    grad_out = sum(
        weight_product(branch_blocks[k], attended[k * rows : (k + 1) * rows]) for k in range(n)
    ).astype(bf16)
    grad_qkv, grad_out = [
        with_layout_constraint(grad, Layout(major_to_minor=(0, 1))) for grad in (grad_qkv, grad_out)
    ]
    grad_qkv, grad_out, d_qkv = tick((grad_qkv, grad_out, d_qkv), wide)
    back = backward_product(d_qkv, qkv_weight).astype(bf16)
    narrow = Stream(small_ring(grad_qkv, grad_out)) if fast else None
    (back,) = tick((back,), wide, narrow)

    near, away = scatter_near(back)
    near, away = tick((near, away), narrow)
    (away,) = tick((away,), wide)
    d_normed = scatter_far(near, away)
    tick((), narrow)
    tick((), wide)
    d_normed, x_own = tick((d_normed, x_all[:rows]), narrow)
    norm_attn_back = jax.vjp(rms_norm, x_own.astype(f32), gain_attention)[1]
    d_input_norm, grad_gain_attn = norm_attn_back(d_normed)
    input_grad = (d_residual + d_input_norm).astype(bf16)
    out_near, out_away = scatter_near(out_partial)
    out_away, grad_gain_attn = tick((out_away, grad_gain_attn), wide)
    outputs = (residual + scatter_far(out_near, out_away)).astype(bf16)

    table_here = jnp.pad(d_table[:, :heads_here], ((0, 0), (0, n * heads_here)))
    table_here = jnp.roll(table_here, me * heads_here, axis=1)[:, :heads]
    small = jnp.concatenate([grad_gain_attn, grad_gain_ff, table_here.reshape(-1)])
    if fast:
        sums = Stream(sum_ring(small))
        while wide.pending or narrow.pending or sums.pending:
            tick((), narrow, sums)
            tick((), wide)
        small = sums.result
    else:
        small = lax.psum(small, ("group",) + peer_axes)
    share = model // n
    gains = [lax.dynamic_slice_in_dim(small, k * model + order_token[0] * share, share) for k in range(2)]
    grad_table = small[2 * model :].reshape(buckets, heads)

    if fast:
        own_rows, all_heads = model // n, n * width
        wide_shape, down_shape = (own_rows, hidden_units), (hidden_units, own_rows)
        out_shapes = [wide_shape, wide_shape, down_shape]
        out_shapes += [(own_rows, all_heads)] * 3 + [(width, model)]
        scratch = [wide_shape, wide_shape, wide_shape, down_shape]
        scratch += [(own_rows, all_heads)] * 3 + [(n, own_rows, width), (width, model)]
        total_gate, total_up, total_down, *total_qkv, total_out = pl.pallas_call(
            functools.partial(
                place_kernel, n_group, part, n * units, hidden_units, all_heads, width
            ),
            out_shape=[jax.ShapeDtypeStruct(shape, f32) for shape in out_shapes],
            in_specs=[pl.BlockSpec(memory_space=pltpu.SMEM)]
            + [pl.BlockSpec(memory_space=pltpu.VMEM)] * (6 * n_group),
            out_specs=[pl.BlockSpec(memory_space=pl.ANY)] * 7,
            scratch_shapes=[pltpu.VMEM(shape, f32) for shape in scratch]
            + [pltpu.SemaphoreType.DMA((7,))],
            compiler_params=params,
            name="place",
        )(spot.reshape(1).astype(jnp.int32), *wide_pieces, *narrow_pieces)
    else:

        def place_columns(grad, which, wide, total):
            full = jnp.zeros((grad.shape[0], n * wide), bf16)
            full = lax.dynamic_update_slice_in_dim(full, grad, which * wide, 1)
            return full[:, :total]

        def finish(full, dim):
            full = lax.psum_scatter(full, peer_axes, scatter_dimension=dim, tiled=True)
            return lax.psum(full, "group").astype(f32)

        total_qkv = [
            finish(
                place_columns(grad_qkv[:, k * width : (k + 1) * width], me, width, heads * size), 0
            )
            for k in range(3)
        ]
        total_out = finish(place_columns(grad_out, me, width, heads * size).T, 0)
        total_gate = finish(place_columns(grad_gate_up[:, :units], rank, units, hidden_units), 0)
        total_up = finish(place_columns(grad_gate_up[:, units:], rank, units, hidden_units), 0)
        total_down = finish(place_columns(grad_down, rank, units, hidden_units).T, 1)
    return (
        outputs,
        input_grad,
        gains[0],
        total_qkv[0],
        total_qkv[1],
        total_qkv[2],
        total_out,
        grad_table,
        gains[1],
        total_gate,
        total_up,
        total_down,
    )


def solution(mesh):
    sizes = (mesh.shape["group"], mesh.shape["ctx"], mesh.shape["wshard"])
    return jax.shard_map(
        functools.partial(per_device, sizes),
        mesh=mesh,
        in_specs=(
            P(("group", "ctx", "wshard"), None),
            P(("group", "ctx", "wshard"), None),
            P("group", None),
            P("group", None),
            P(),
            P("wshard", None),
            P("wshard", None),
            P("wshard", None),
            P("wshard", None),
            P(),
            P(),
            P("wshard", None),
            P("wshard", None),
            P("wshard", None),
        ),
        out_specs=(
            P(("group", "ctx", "wshard"), None),
            P(("group", "ctx", "wshard"), None),
            P(("ctx", "wshard")),
            P(("ctx", "wshard"), None),
            P(("ctx", "wshard"), None),
            P(("ctx", "wshard"), None),
            P(("ctx", "wshard"), None),
            P(),
            P(("ctx", "wshard")),
            P(("ctx", "wshard"), None),
            P(("ctx", "wshard"), None),
            P(None, ("ctx", "wshard")),
        ),
        check_vma=False,
    )
```

```python
import functools

import jax
import jax.numpy as jnp
from jax import lax
from jax.experimental import pallas as pl
from jax.experimental.layout import Layout, with_layout_constraint
from jax.experimental.pallas import tpu as pltpu
from jax.sharding import PartitionSpec as P

epsilon = 1e-06
highest = lax.Precision.HIGHEST
thresholds = (12, 16, 23, 32, 46, 64, 91)
masked_out = -1e30
bf16 = jnp.bfloat16
f32 = jnp.float32
peer_axes = ("ctx", "wshard")
vmem_bytes = 60 * 1024 * 1024

ladder_ring = (0, 2, 4, 6, 7, 5, 3, 1)


def bucket_of(offset):
    distance = jnp.abs(offset)
    beyond = 8 + sum(((distance >= border).astype(jnp.int32) for border in thresholds))
    near_far = jnp.where(distance < 8, distance, beyond)
    return jnp.where(offset > 0, 16, 0) + near_far


def rms_norm(values, gain_vector):
    return (
        values
        * lax.rsqrt(jnp.mean(values * values, axis=-1, keepdims=True) + epsilon)
        * gain_vector
    )


def dot(left_side, right_side, dims, precision=None):
    return lax.dot_general(
        left_side, right_side, (dims, ((), ())), precision=precision, preferred_element_type=f32
    )


def forward_product(left_side, right_side):
    return dot(left_side, right_side, ((1,), (0,)))


def backward_product(left_side, right_side):
    return dot(left_side, right_side, ((1,), (1,)))


def weight_product(left_side, right_side):
    return dot(left_side, right_side, ((0,), (0,)))


def iota(shape, dim):
    return lax.broadcasted_iota(jnp.int32, shape, dim)


def arrange_kernel(rows, count, me_ref, order_ref, gain_ref, weight_ref, *refs):
    blocks, (x_ref, normed_ref, qkv_ref) = refs[:-3], refs[-3:]
    me = me_ref[0]
    first = (me ^ pl.program_id(0)) * rows
    tokens = first + iota((rows, rows), 0)
    total = None
    for k in range(count):
        places = order_ref[pl.ds(me ^ k, 1), :]
        chosen = (places == tokens).astype(f32).astype(bf16)
        part = forward_product(chosen, blocks[k][...])
        total = part if total is None else total + part
    x_ref[...] = total.astype(bf16)
    normed = rms_norm(total, gain_ref[...]).astype(bf16)
    normed_ref[...] = normed
    qkv_ref[...] = forward_product(normed, weight_ref[...]).astype(bf16)


def own_heads_kernel(width, count, n_w, me_ref, *refs):
    mine, given, out_ref = refs[:3], refs[3:6], refs[6]
    me = me_ref[0]
    half, columns = mine[0].shape
    for m in range(count):

        @pl.when(me == m)
        def _():
            for t in range(3):
                for w in range(n_w):
                    source = mine[t] if m % n_w == w else given[t]
                    place = slice(w * half, (w + 1) * half), slice(t * width, (t + 1) * width)
                    if (m + 1) * width <= columns:
                        out_ref[place] = source[:, m * width : (m + 1) * width]
                    else:
                        out_ref[place] = jnp.zeros((half, width), out_ref.dtype)


def bias_kernel(rows, heads_here, heads, buckets, me_ref, table_ref, out_ref):
    lanes = iota((8, 4 * rows), 1)
    ids = bucket_of(2 * rows - lanes)
    for h in range(heads_here):
        head = jnp.minimum(me_ref[0] * heads_here + h, heads - 1)
        base = jnp.zeros((8, 4 * rows), f32)
        for b in range(buckets):
            base = jnp.where(ids == b, table_ref[b, head], base)
        wide = jnp.broadcast_to(base[0:1], (rows, 4 * rows))
        rolled = pltpu.roll(wide, 0, 1, stride=1, stride_axis=0)
        out_ref[h, 0] = jnp.full((rows, rows), table_ref[buckets // 2 - 1, head], f32)
        out_ref[h, 4] = jnp.full((rows, rows), table_ref[buckets - 1, head], f32)
        for delta in (1, 0, -1):
            start = rows + rows * (1 - delta)
            out_ref[h, delta + 2] = rolled[:, start : start + rows]


def span_of(lengths_ref, seqs, first, last, rows, total):
    low, high, end = 0, total, 0
    ends = []
    for s in range(seqs):
        end = end + lengths_ref[s]
        ends.append(end)
    for s in range(seqs):
        low = jnp.where(ends[s] <= first, ends[s], low)
    for s in reversed(range(seqs)):
        high = jnp.where(ends[s] > last, ends[s], high)
    high = jnp.minimum(high, total)
    return ends, low // rows, (high + rows - 1) // rows


def sequence_ids(ends, first, shape, dim):
    places = first + iota(shape, dim)
    ids = jnp.zeros(shape, jnp.int32)
    for end in ends:
        ids = ids + (places >= end).astype(jnp.int32)
    return ids


def attend_kernel(
    rows, count, heads_here, size, seqs, me_ref, lengths_ref, qkv_ref, bias_ref, att_ref, wide_ref, lse_ref
):
    me = me_ref[0]
    width = heads_here * size
    here = pl.program_id(0)
    block = me ^ here
    ends, low, high = span_of(
        lengths_ref, seqs, block * rows, block * rows + rows - 1, rows, count * rows
    )
    query_seq = sequence_ids(ends, block * rows, (1, rows), 1)
    start = pl.multiple_of(here * rows, rows)
    queries = qkv_ref[pl.ds(start, rows), :][:, :width]

    def step(key_block, carry):
        at = pl.multiple_of((key_block ^ me) * rows, rows)
        own = qkv_ref[pl.ds(at, rows), :]
        delta = jnp.clip(key_block - block, -2, 2) + 2
        same = sequence_ids(ends, key_block * rows, (rows, 1), 0) == query_seq
        after = []
        for h in range(heads_here):
            top, total, acc = carry[h]
            query = queries[:, h * size : (h + 1) * size]
            key = own[:, width + h * size : width + (h + 1) * size]
            value = own[:, 2 * width + h * size : 2 * width + (h + 1) * size]
            scores = backward_product(key, query) + bias_ref[h, delta]
            scores = jnp.where(same, scores, masked_out)
            top_next = jnp.maximum(top, jnp.max(scores, axis=0, keepdims=True))
            probs = jnp.exp(scores - top_next)
            fade = jnp.exp(top - top_next)
            total = total * fade + jnp.sum(probs, axis=0, keepdims=True)
            acc = acc * fade + weight_product(value, probs.astype(bf16))
            after.append((top_next, total, acc))
        return tuple(after)

    fresh = (
        jnp.full((1, rows), masked_out, f32),
        jnp.zeros((1, rows), f32),
        jnp.zeros((size, rows), f32),
    )
    done = lax.fori_loop(low, high, step, (fresh,) * heads_here)
    for h in range(heads_here):
        top, total, acc = done[h]
        lse_ref[h : h + 1, :] = top + jnp.log(total)
        out = (acc / total).T
        wide_ref[:, h * size : (h + 1) * size] = out
        att_ref[:, h * size : (h + 1) * size] = out.astype(bf16)


def attend_back_kernel(
    rows,
    count,
    heads_here,
    size,
    seqs,
    buckets,
    me_ref,
    lengths_ref,
    qkv_ref,
    bias_ref,
    lse_ref,
    wide_ref,
    d_att_ref,
    dqkv_ref,
    table_ref,
    dq_ref,
    sums_ref,
    delta_ref,
):
    me = me_ref[0]
    width = heads_here * size
    here = pl.program_id(0)
    block = me ^ here

    @pl.when(here == 0)
    def _():
        dq_ref[...] = jnp.zeros_like(dq_ref)
        sums_ref[...] = jnp.zeros_like(sums_ref)
        for k in range(count):
            part = slice(k * rows, (k + 1) * rows)
            both = d_att_ref[part, :].astype(f32) * wide_ref[part, :]
            for h in range(heads_here):
                delta_ref[h : h + 1, part] = jnp.sum(
                    both[:, h * size : (h + 1) * size].T, axis=0, keepdims=True
                )

    ends, low, high = span_of(
        lengths_ref, seqs, block * rows, block * rows + rows - 1, rows, count * rows
    )
    key_seq = sequence_ids(ends, block * rows, (rows, 1), 0)
    start = pl.multiple_of(here * rows, rows)
    own = qkv_ref[pl.ds(start, rows), :]

    def step(query_block, carry):
        rel = query_block ^ me
        at = pl.multiple_of(rel * rows, rows)
        queries = qkv_ref[pl.ds(at, rows), :][:, :width]
        d_outs = d_att_ref[pl.ds(at, rows), :]
        near = jnp.clip(block - query_block, -2, 2) + 2
        same = key_seq == sequence_ids(ends, query_block * rows, (1, rows), 1)
        after = []
        for h in range(heads_here):
            d_key, d_value = carry[h]
            key = own[:, width + h * size : width + (h + 1) * size]
            value = own[:, 2 * width + h * size : 2 * width + (h + 1) * size]
            query = queries[:, h * size : (h + 1) * size]
            d_out = d_outs[:, h * size : (h + 1) * size]
            scores = backward_product(key, query) + bias_ref[h, near]
            lse = lse_ref[h : h + 1, pl.ds(at, rows)]
            soft = jnp.where(same, jnp.exp(scores - lse), 0.0)
            d_probs = backward_product(value, d_out)
            d_scores = (soft * (d_probs - delta_ref[h : h + 1, pl.ds(at, rows)])).astype(bf16)
            sums_ref[h, near] += d_scores.astype(f32)
            d_value = d_value + forward_product(soft.astype(bf16), d_out)
            d_key = d_key + forward_product(d_scores, query)
            dq_ref[h, rel] += weight_product(key, d_scores)
            after.append((d_key, d_value))
        return tuple(after)

    zero = jnp.zeros((rows, size), f32)
    done = lax.fori_loop(low, high, step, ((zero, zero),) * heads_here)
    for h in range(heads_here):
        d_key, d_value = done[h]
        dqkv_ref[pl.ds(start, rows), width + h * size : width + (h + 1) * size] = d_key.astype(bf16)
        dqkv_ref[pl.ds(start, rows), 2 * width + h * size : 2 * width + (h + 1) * size] = (
            d_value.astype(bf16)
        )

    @pl.when(here == count - 1)
    def _():
        for h in range(heads_here):
            for k in range(count):
                dqkv_ref[k * rows : (k + 1) * rows, h * size : (h + 1) * size] = (
                    dq_ref[h, k].T.astype(bf16)
                )
        turned = (iota((rows, rows), 0) + iota((rows, rows), 1) == rows - 1).astype(f32)
        ids = bucket_of(2 * rows - 1 - iota((buckets, 4 * rows), 1))
        mine = ids == iota((buckets, 4 * rows), 0)
        bucket_rows = iota((buckets, 1), 0)
        lanes = iota((buckets, 128), 1)
        table = jnp.zeros((buckets, 128), f32)
        for h in range(heads_here):
            strip = jnp.concatenate(
                [forward_product_exact(turned, sums_ref[h, d]) for d in (3, 2, 1)]
                + [jnp.zeros((rows, rows), f32)],
                axis=1,
            )
            diagonals = jnp.sum(
                pltpu.roll(strip, 0, 1, stride=1, stride_axis=0), axis=0, keepdims=True
            )
            column = jnp.sum(jnp.where(mine, diagonals, 0.0), axis=1, keepdims=True)
            column = column + jnp.where(bucket_rows == buckets // 2 - 1, jnp.sum(sums_ref[h, 0]), 0.0)
            column = column + jnp.where(bucket_rows == buckets - 1, jnp.sum(sums_ref[h, 4]), 0.0)
            table = jnp.where(lanes == h, column, table)
        table_ref[...] = table


def place_kernel(groups, part, count, units_all, hidden_units, spot_ref, *refs):
    spot = spot_ref[0]
    wide, refs = refs[: 4 * groups], refs[4 * groups :]
    outs, (gate, up, down, turned), sems = refs[:3], refs[3:-1], refs[-1]
    units = units_all // count
    middle = 3 * units // 2

    def row_of(j, h):
        return piece_row(spot, groups, part, j, h)

    def copy(k, source):
        return pltpu.make_async_copy(source, outs[k], sems.at[k])

    def gather(target, t):
        for c in range(2):
            low, high = max(c * middle, t * units), min((c + 1) * middle, (t + 1) * units)
            for r in range(count):
                first = r * units + low - t * units
                size = min(high - low, hidden_units - first)
                if low >= high or size <= 0:
                    continue
                start = r * middle + low - c * middle
                for j in range(groups):
                    for h in range(2):
                        block = wide[(j * 2 + c) * 2 + h]
                        target[pl.ds(row_of(j, h), part), first : first + size] = (
                            block[:, start : start + size].astype(f32)
                        )

    gather(gate, 0)
    copy(0, gate).start()
    gather(up, 1)
    copy(1, up).start()
    gather(down, 2)
    for first in range(0, hidden_units, 128):
        turned[first : first + 128, :] = down[:, first : first + 128].T
    copy(2, turned).start()
    for k, source in enumerate((gate, up, turned)):
        copy(k, source).wait()


def piece_row(spot, groups, part, j, h):
    index = lax.rem(spot + groups - j, groups) if h == 0 else lax.rem(spot + j, groups)
    return pl.multiple_of((2 * index + h) * part, 8)


def place_heads_kernel(groups, part, count, width, spot_ref, *refs):
    spot = spot_ref[0]
    narrow, outs, out_rows = refs[: 2 * groups], refs[2 * groups : -1], refs[-1]
    heads_all = count * width
    for j in range(groups):
        for h in range(2):
            rows = pl.ds(piece_row(spot, groups, part, j, h), part)
            for k in range(3):
                outs[k][rows, :] = (
                    narrow[j * 2 + h][:, k * heads_all : (k + 1) * heads_all].astype(f32)
                )
            for q in range(count):
                first = 3 * heads_all + q * width
                out_rows[q, rows, :] = narrow[j * 2 + h][:, first : first + width].astype(f32)
    size = out_rows.shape[1]
    for q in range(count):
        outs[3][:, q * size : (q + 1) * size] = out_rows[q].T


def forward_product_exact(left_side, right_side):
    return dot(left_side, right_side, ((1,), (0,)), highest)


def whole(shape):
    return pl.BlockSpec(shape, lambda *_: (0,) * len(shape))


def per_device(
    sizes,
    inputs,
    out_grad,
    lengths,
    permutation,
    gain_attention,
    query_weight,
    key_weight,
    value_weight,
    out_weight,
    bucket_bias,
    gain_feedforward,
    gate_weight,
    up_weight,
    down_weight,
):
    n_group, n_ctx, n_w = sizes
    n = n_ctx * n_w
    fast = (n_group, n_ctx, n_w) == (8, 2, 2)
    rows, model = inputs.shape
    buckets, heads = bucket_bias.shape
    hidden_units = gate_weight.shape[1]
    size = query_weight.shape[1] // heads
    seqs = lengths.shape[1]
    tokens = rows * n
    heads_here = -(-heads // n)
    width = heads_here * size
    units = -(-hidden_units // (128 * n)) * 128
    ctx, wsh = lax.axis_index("ctx"), lax.axis_index("wshard")
    me = lax.axis_index(peer_axes)
    rank = wsh * n_ctx + ctx
    flip_w = [(0, 1), (1, 0)]


    def mate(block):
        return lax.ppermute(block, "wshard", flip_w)

    def across(block):
        return lax.ppermute(block, "ctx", flip_w)

    def to_relative(stacked):
        return jnp.take(stacked, me ^ lax.iota(jnp.int32, n), axis=0)

    def gather_blocks(block):
        if fast:
            far = across(block)
            return [block, mate(block), far, mate(far)]
        stacked = to_relative(lax.all_gather(block, peer_axes, axis=0, tiled=False))
        return [stacked[k] for k in range(n)]

    def columns_of(weight, which, wide):
        over = max(0, n * wide - weight.shape[1])
        padded = jnp.pad(weight, ((0, 0), (0, over))) if over else weight
        return lax.dynamic_slice_in_dim(padded, which * wide, wide, 1)

    def own_columns(parts, wide, which):
        return jnp.concatenate([columns_of(part, which, wide) for part in parts], axis=1)

    def in_order(mine, given):
        upper = jnp.where(wsh == 0, mine, given)
        lower = jnp.where(wsh == 0, given, mine)
        return jnp.concatenate([upper, lower], axis=0)

    hold = lax.optimization_barrier

    if fast:
        row_far, row_mate = across(inputs), mate(inputs)
    heads_mine = (query_weight, key_weight, value_weight)
    heads_given = [mate(weight) for weight in heads_mine]
    out_other = mate(out_weight)
    gate_up_mine = own_columns((gate_weight, up_weight), units, rank)
    gate_up_sent = own_columns((gate_weight, up_weight), units, (1 - wsh) * n_ctx + ctx)
    half = down_weight.shape[0]
    extra = n_ctx * units - half
    down_other = mate(down_weight[:extra])
    down_wide = jnp.concatenate(
        [
            down_weight,
            jnp.where(wsh == 0, down_other, jnp.zeros_like(down_other)),
            jnp.zeros_like(down_other),
        ]
    )
    down_own = lax.dynamic_slice_in_dim(down_wide, wsh * extra + ctx * units, units, 0)
    me_1 = me.reshape(1).astype(jnp.int32)
    order = permutation.reshape(n, rows)
    params = pltpu.CompilerParams(vmem_limit_bytes=vmem_bytes)
    qkv_weight = pl.pallas_call(
        functools.partial(own_heads_kernel, width, n, n_w),
        out_shape=jax.ShapeDtypeStruct((model, 3 * width), bf16),
        in_specs=[pl.BlockSpec(memory_space=pltpu.SMEM)]
        + [pl.BlockSpec(memory_space=pltpu.VMEM)] * 6,
        out_specs=pl.BlockSpec(memory_space=pltpu.VMEM),
        compiler_params=params,
        name="own_heads",
    )(me_1, *heads_mine, *heads_given)
    bias = pl.pallas_call(
        functools.partial(bias_kernel, rows, heads_here, heads, buckets),
        out_shape=jax.ShapeDtypeStruct((heads_here, 5, rows, rows), f32),
        in_specs=[
            pl.BlockSpec(memory_space=pltpu.SMEM),
            pl.BlockSpec(memory_space=pltpu.SMEM),
        ],
        out_specs=pl.BlockSpec(memory_space=pltpu.VMEM),
        compiler_params=params,
        name="bias_strips",
    )(me_1, bucket_bias)
    if fast:
        row_far, out_grad, qkv_weight, bias, gate_up_mine, gate_up_sent = hold(
            (row_far, out_grad, qkv_weight, bias, gate_up_mine, gate_up_sent)
        )
        row_blocks = [inputs, row_mate, row_far, mate(row_far)]
    else:
        row_blocks = gather_blocks(inputs)
    gate_up_given = mate(gate_up_sent)
    dy = jnp.concatenate(gather_blocks(out_grad))

    x_all, normed, qkv = pl.pallas_call(
        functools.partial(arrange_kernel, rows, n),
        out_shape=(
            jax.ShapeDtypeStruct((tokens, model), bf16),
            jax.ShapeDtypeStruct((tokens, model), bf16),
            jax.ShapeDtypeStruct((tokens, 3 * width), bf16),
        ),
        grid_spec=pltpu.PrefetchScalarGridSpec(
            num_scalar_prefetch=1,
            grid=(n,),
            in_specs=[whole((n, rows)), whole((1, model)), whole((model, 3 * width))]
            + [whole((rows, model))] * n,
            out_specs=[
                pl.BlockSpec((rows, model), lambda t, *_: (t, 0)),
                pl.BlockSpec((rows, model), lambda t, *_: (t, 0)),
                pl.BlockSpec((rows, 3 * width), lambda t, *_: (t, 0)),
            ],
        ),
        compiler_params=params,
        cost_estimate=pl.CostEstimate(
            flops=2 * tokens * model * (tokens + 3 * width),
            bytes_accessed=8 * tokens * model,
            transcendentals=0,
        ),
        name="arrange_project",
    )(me_1, order, gain_attention.reshape(1, model), qkv_weight, *row_blocks)
    lengths_row = lengths.reshape(seqs)
    attended, attended_wide, lse = pl.pallas_call(
        functools.partial(attend_kernel, rows, n, heads_here, size, seqs),
        out_shape=(
            jax.ShapeDtypeStruct((tokens, width), bf16),
            jax.ShapeDtypeStruct((tokens, width), f32),
            jax.ShapeDtypeStruct((heads_here, tokens), f32),
        ),
        grid_spec=pltpu.PrefetchScalarGridSpec(
            num_scalar_prefetch=2,
            grid=(n,),
            in_specs=[whole((tokens, 3 * width)), whole((heads_here, 5, rows, rows))],
            out_specs=[
                pl.BlockSpec((rows, width), lambda t, *_: (t, 0)),
                pl.BlockSpec((rows, width), lambda t, *_: (t, 0)),
                pl.BlockSpec((heads_here, rows), lambda t, *_: (0, t)),
            ],
        ),
        compiler_params=params,
        cost_estimate=pl.CostEstimate(
            flops=16 * tokens * tokens * width,
            bytes_accessed=16 * tokens * width,
            transcendentals=tokens * tokens * heads_here,
        ),
        name="attend",
    )(me_1, lengths_row, qkv, bias)

    strip = model // n // n_group
    part = strip // 2
    if fast:
        group = lax.axis_index("group")
        spot = jnp.where(group % 2 == 0, group // 2, n_group - 1 - group // 2)
        ahead = [(ladder_ring[k], ladder_ring[(k + 1) % n_group]) for k in range(n_group)]
        behind = [(b, a) for a, b in ahead]

    def forward(block):
        return lax.ppermute(block, "group", ahead)

    def backward(block):
        return lax.ppermute(block, "group", behind)

    def diagonal(block):
        return lax.ppermute(block, peer_axes, [(q, q ^ 3) for q in range(n)])

    def pick(array, index, axis):
        return lax.squeeze(lax.dynamic_slice_in_dim(array, index, 1, axis), (axis,))

    def rank_of(k):
        peer = me ^ k
        return (peer % n_w) * n_ctx + peer // n_w

    def ring(take, swap, pieces):
        both_ways = (forward, backward)
        one, two = take(0, lax.rem(spot + 7, n_group)), take(1, lax.rem(spot + 1, n_group))
        for s in range(n_group - 1):
            came = yield (one, two), both_ways
            one = came[0] + take(0, lax.rem(spot + 14 - s, n_group))
            two = came[1] + take(1, lax.rem(spot + 2 + s, n_group))
        pairs, (blocks, join) = [], swap(one, two)
        for block in blocks:
            came = yield tuple(block[1:]), (mate, across, diagonal)
            pairs.append(join([block[0], *came]))
        for pair in pairs:
            pieces.extend(pair)
        for s in range(n_group - 1):
            for c, pair in enumerate(pairs):
                pairs[c] = yield pair, both_ways
                pieces.extend(pairs[c])

    class Stream:
        def __init__(self, steps):
            self.steps, self.result, self.came = steps, None, None
            self.pending = next(steps)

        def advance(self, came):
            try:
                self.pending = self.steps.send(came)
            except StopIteration as stop:
                self.pending, self.result = None, stop.value

    order_token = [me]

    def tick(values, *streams):
        live = [stream for stream in streams if stream is not None and stream.pending is not None]
        if not live:
            return values
        arrived, values = hold(([stream.came for stream in live if stream.came], values))
        for stream in live:
            if stream.came:
                stream.advance(arrived.pop(0))
        live = [stream for stream in live if stream.pending is not None]
        operands, values, order_token[0] = hold(
            ([stream.pending[0] for stream in live], values, order_token[0])
        )
        for stream, sent in zip(live, operands):
            stream.came = [send(x) for send, x in zip(stream.pending[1], sent)]
        return values

    def piece_of(cut, index, h):
        zero = jnp.zeros((), index.dtype)
        starts = (zero, index, zero + h, zero, zero)
        return lax.squeeze(
            lax.dynamic_slice(cut, starts, (n, 1, 1, part, cut.shape[4])), (1, 2)
        )

    def rows_cut(grad):
        return grad.reshape(n, n_group, 2, part, grad.shape[1])

    wide_pieces, narrow_pieces = [], []

    def wide_ring(grad_gate_up, grad_down):
        one, two = rows_cut(grad_gate_up), rows_cut(grad_down)

        def take(h, index):
            return jnp.concatenate([piece_of(x, index, h) for x in (one, two)], axis=-1)

        def swap(one, two):
            both = jnp.stack([one, two], axis=1)
            middle = 3 * units // 2

            def join(came):
                full = jnp.zeros((2, part, n * middle), bf16)
                for k in range(n):
                    full = lax.dynamic_update_slice_in_dim(full, came[k], rank_of(k) * middle, 2)
                return full[0], full[1]

            halves = [both[..., :middle], both[..., middle:]]
            return [[pick(half, me ^ k, 0) for k in range(n)] for half in halves], join

        return ring(take, swap, wide_pieces)

    def small_ring(grad_qkv, grad_out):
        one, two = rows_cut(grad_qkv), rows_cut(grad_out)

        def take(h, index):
            return jnp.concatenate([piece_of(x, index, h) for x in (one, two)], axis=-1)

        def swap(one, two):
            both = jnp.stack([one, two], axis=1)
            own = jnp.concatenate([both[k, :, :, 3 * width :] for k in range(n)], axis=2)

            def join(came):
                stacked = jnp.stack(came)
                came = [pick(stacked, me ^ r, 0) for r in range(n)]
                full = jnp.concatenate(
                    [came[r][:, :, k * width : (k + 1) * width] for k in range(3) for r in range(n)]
                    + [own],
                    axis=2,
                )
                return full[0], full[1]

            return [[pick(both, me ^ k, 0)[:, :, : 3 * width] for k in range(n)]], join

        return ring(take, swap, narrow_pieces)

    def sum_ring(small):
        for axis, bit, count in (
            ("wshard", 1, n_w),
            ("ctx", 1, n_ctx),
            ("group", 1, n_group),
            ("group", 2, n_group),
            ("group", 4, n_group),
        ):
            pairs = [(g, g ^ bit) for g in range(count)]
            came = yield (small,), (lambda x: lax.ppermute(x, axis, pairs),)
            small = small + came[0]
        return small

    def scatter_near(partial):
        sent = partial.reshape(n, rows, -1)
        if not fast:
            total = lax.psum_scatter(to_relative(sent), peer_axes, scatter_dimension=0, tiled=False)
            return total.astype(f32), None
        got = mate(jnp.stack([sent[1], sent[3]]))
        near = sent[0].astype(f32) + got[0].astype(f32)
        return near, (sent[2].astype(f32) + got[1].astype(f32)).astype(bf16)

    def scatter_far(near, away):
        return near + across(away).astype(f32) if fast else near

    attended, out_mine, out_other, gate_up_mine = hold(
        (attended, out_weight, out_other, gate_up_mine)
    )
    gate_up = in_order(gate_up_mine, gate_up_given)
    if fast:
        attended_far, attended_mate = across(attended), mate(attended)
        attended_far, gate_up = hold((attended_far, gate_up))
        attended_blocks = [attended, attended_mate, attended_far, mate(attended_far)]
    else:
        attended_blocks = gather_blocks(attended)
    out_full = in_order(out_mine, out_other)
    out_full = jnp.pad(out_full, ((0, n * width - out_full.shape[0]), (0, 0)))
    out_blocks = [lax.dynamic_slice_in_dim(out_full, (me ^ k) * width, width, 0) for k in range(n)]
    out_relative = jnp.concatenate(out_blocks, axis=0)
    by_rows = [
        jnp.concatenate(
            [attended_blocks[k][(m ^ k) * rows : ((m ^ k) + 1) * rows] for m in range(n)]
        )
        for k in range(n)
    ]
    attended_all = jnp.concatenate(by_rows, axis=1)
    residual_all = x_all.astype(f32) + forward_product(
        attended_all, out_relative
    )
    residual = residual_all[:rows]
    normed_ff = rms_norm(residual_all, gain_feedforward).astype(bf16)
    gate_up_proj = forward_product(normed_ff, gate_up)
    gate_proj, up_proj = gate_up_proj[:, :units], gate_up_proj[:, units:]

    def activate(gate_in, up_in):
        return jax.nn.gelu(gate_in, approximate=True) * up_in

    hidden_wide, activate_back = jax.vjp(activate, gate_proj, up_proj)
    hidden = hidden_wide.astype(bf16)
    d_hidden = backward_product(dy, down_own)
    d_gate_wide, d_up_wide = activate_back(d_hidden)
    d_gate_up = jnp.concatenate([d_gate_wide.astype(bf16), d_up_wide.astype(bf16)], axis=1)

    grad_gate_up = weight_product(normed_ff, d_gate_up).astype(bf16)
    grad_down = weight_product(dy, hidden).astype(bf16)
    wide = Stream(wide_ring(grad_gate_up, grad_down)) if fast else None
    d_gate_up, hidden = tick((d_gate_up, hidden), wide)

    back = backward_product(d_gate_up, gate_up).astype(bf16)
    back, hidden = tick((back, hidden), wide)
    near, away = scatter_near(back)
    out_partial = forward_product(hidden, down_own).astype(bf16)
    near, away, out_partial = tick((near, away, out_partial), wide)
    d_normed_ff = scatter_far(near, away)
    d_normed_ff, residual = tick((d_normed_ff, residual), wide)
    norm_ff_back = jax.vjp(rms_norm, residual, gain_feedforward)[1]
    d_residual_norm, grad_gain_ff = norm_ff_back(d_normed_ff)
    d_residual = dy[:rows].astype(f32) + d_residual_norm
    branch = d_residual.astype(bf16)

    if fast:
        d_rows = backward_product(branch, out_relative).astype(bf16)
        d_rows = [d_rows[:, k * width : (k + 1) * width] for k in range(n)]
        d_rows = [d_rows[0], mate(d_rows[1]), across(d_rows[2]), diagonal(d_rows[3])]
        d_attended, branch = hold((jnp.concatenate(d_rows), branch))
    else:
        branch_blocks = gather_blocks(branch)
        d_attended = backward_product(jnp.concatenate(branch_blocks), out_blocks[0]).astype(bf16)
    d_attended, branch = tick((d_attended, branch), wide)
    if fast:
        branch_blocks = gather_blocks(branch)
    d_qkv, d_table = pl.pallas_call(
        functools.partial(attend_back_kernel, rows, n, heads_here, size, seqs, buckets),
        out_shape=(
            jax.ShapeDtypeStruct((tokens, 3 * width), bf16),
            jax.ShapeDtypeStruct((buckets, 128), f32),
        ),
        grid_spec=pltpu.PrefetchScalarGridSpec(
            num_scalar_prefetch=2,
            grid=(n,),
            in_specs=[
                whole((tokens, 3 * width)),
                whole((heads_here, 5, rows, rows)),
                whole((heads_here, tokens)),
                whole((tokens, width)),
                whole((tokens, width)),
            ],
            out_specs=[whole((tokens, 3 * width)), whole((buckets, 128))],
            scratch_shapes=[
                pltpu.VMEM((heads_here, n, size, rows), f32),
                pltpu.VMEM((heads_here, 5, rows, rows), f32),
                pltpu.VMEM((heads_here, tokens), f32),
            ],
        ),
        compiler_params=params,
        cost_estimate=pl.CostEstimate(
            flops=40 * tokens * tokens * width,
            bytes_accessed=16 * tokens * width,
            transcendentals=tokens * tokens * heads_here,
        ),
        name="attend_back",
    )(me_1, lengths_row, qkv, bias, lse, attended_wide, d_attended)
    d_qkv, branch_far, out_partial = tick((d_qkv, branch_blocks[2], out_partial), wide)
    branch_blocks[2] = branch_far
    grad_qkv = weight_product(normed, d_qkv).astype(bf16)
    grad_out = sum(
        weight_product(branch_blocks[k], attended[k * rows : (k + 1) * rows]) for k in range(n)
    ).astype(bf16)
    grad_qkv, grad_out = [
        with_layout_constraint(grad, Layout(major_to_minor=(0, 1))) for grad in (grad_qkv, grad_out)
    ]
    grad_qkv, grad_out, d_qkv = tick((grad_qkv, grad_out, d_qkv), wide)
    back = backward_product(d_qkv, qkv_weight).astype(bf16)
    narrow = Stream(small_ring(grad_qkv, grad_out)) if fast else None
    (back,) = tick((back,), wide, narrow)

    near, away = scatter_near(back)
    near, away = tick((near, away), narrow)
    (away,) = tick((away,), wide)
    d_normed = scatter_far(near, away)
    for stream in (narrow, wide, narrow, wide, narrow, wide):
        tick((), stream)
    d_normed, x_own = tick((d_normed, x_all[:rows]), narrow)
    norm_attn_back = jax.vjp(rms_norm, x_own.astype(f32), gain_attention)[1]
    d_input_norm, grad_gain_attn = norm_attn_back(d_normed)
    input_grad = (d_residual + d_input_norm).astype(bf16)
    out_near, out_away = scatter_near(out_partial)
    out_away, grad_gain_attn = tick((out_away, grad_gain_attn), wide)
    outputs = (residual + scatter_far(out_near, out_away)).astype(bf16)

    table_here = jnp.pad(d_table[:, :heads_here], ((0, 0), (0, n * heads_here)))
    table_here = jnp.roll(table_here, me * heads_here, axis=1)[:, :heads]
    small = jnp.concatenate([grad_gain_attn, grad_gain_ff, table_here.reshape(-1)])
    if fast:
        sums = Stream(sum_ring(small))
        own_rows, all_heads = model // n, n * width
        spot_1 = spot.reshape(1).astype(jnp.int32)
        in_vmem = pl.BlockSpec(memory_space=pltpu.VMEM)
        while narrow.pending or sums.pending or len(wide_pieces) < 4 * n_group - 2:
            tick((), narrow, sums)
            if len(wide_pieces) < 4 * n_group - 2:
                tick((), wide)
        heads_grads = pl.pallas_call(
            functools.partial(place_heads_kernel, n_group, part, n, width),
            out_shape=[jax.ShapeDtypeStruct((own_rows, all_heads), f32)] * 3
            + [jax.ShapeDtypeStruct((width, model), f32)],
            in_specs=[pl.BlockSpec(memory_space=pltpu.SMEM)] + [in_vmem] * (2 * n_group),
            out_specs=[in_vmem] * 4,
            scratch_shapes=[pltpu.VMEM((n, own_rows, width), f32)],
            compiler_params=params,
            name="place_heads",
        )(spot_1, *narrow_pieces)
        heads_grads = tick(heads_grads, wide)
        small = sums.result
    else:
        small = lax.psum(small, ("group",) + peer_axes)
    share = model // n
    gains = [lax.dynamic_slice_in_dim(small, k * model + order_token[0] * share, share) for k in range(2)]
    grad_table = small[2 * model :].reshape(buckets, heads)

    if fast:
        *total_qkv, total_out = heads_grads
        wide_shape, down_shape = (own_rows, hidden_units), (hidden_units, own_rows)
        total_gate, total_up, total_down = pl.pallas_call(
            functools.partial(place_kernel, n_group, part, n, n * units, hidden_units),
            out_shape=[
                jax.ShapeDtypeStruct(shape, f32) for shape in (wide_shape, wide_shape, down_shape)
            ],
            in_specs=[pl.BlockSpec(memory_space=pltpu.SMEM)] + [in_vmem] * (4 * n_group),
            out_specs=[pl.BlockSpec(memory_space=pl.ANY)] * 3,
            scratch_shapes=[pltpu.VMEM(wide_shape, f32)] * 3
            + [pltpu.VMEM(down_shape, f32), pltpu.SemaphoreType.DMA((3,))],
            compiler_params=params,
            name="place",
        )(spot_1, *wide_pieces)
    else:

        def place_columns(grad, which, wide, total):
            full = jnp.zeros((grad.shape[0], n * wide), bf16)
            full = lax.dynamic_update_slice_in_dim(full, grad, which * wide, 1)
            return full[:, :total]

        def finish(full, dim):
            full = lax.psum_scatter(full, peer_axes, scatter_dimension=dim, tiled=True)
            return lax.psum(full, "group").astype(f32)

        total_qkv = [
            finish(
                place_columns(grad_qkv[:, k * width : (k + 1) * width], me, width, heads * size), 0
            )
            for k in range(3)
        ]
        total_out = finish(place_columns(grad_out, me, width, heads * size).T, 0)
        total_gate = finish(place_columns(grad_gate_up[:, :units], rank, units, hidden_units), 0)
        total_up = finish(place_columns(grad_gate_up[:, units:], rank, units, hidden_units), 0)
        total_down = finish(place_columns(grad_down, rank, units, hidden_units).T, 1)
    return (
        outputs,
        input_grad,
        gains[0],
        total_qkv[0],
        total_qkv[1],
        total_qkv[2],
        total_out,
        grad_table,
        gains[1],
        total_gate,
        total_up,
        total_down,
    )


def solution(mesh):
    sizes = (mesh.shape["group"], mesh.shape["ctx"], mesh.shape["wshard"])
    return jax.shard_map(
        functools.partial(per_device, sizes),
        mesh=mesh,
        in_specs=(
            P(("group", "ctx", "wshard"), None),
            P(("group", "ctx", "wshard"), None),
            P("group", None),
            P("group", None),
            P(),
            P("wshard", None),
            P("wshard", None),
            P("wshard", None),
            P("wshard", None),
            P(),
            P(),
            P("wshard", None),
            P("wshard", None),
            P("wshard", None),
        ),
        out_specs=(
            P(("group", "ctx", "wshard"), None),
            P(("group", "ctx", "wshard"), None),
            P(("ctx", "wshard")),
            P(("ctx", "wshard"), None),
            P(("ctx", "wshard"), None),
            P(("ctx", "wshard"), None),
            P(("ctx", "wshard"), None),
            P(),
            P(("ctx", "wshard")),
            P(("ctx", "wshard"), None),
            P(("ctx", "wshard"), None),
            P(None, ("ctx", "wshard")),
        ),
        check_vma=False,
    )
```

```python
import functools

import jax
import jax.numpy as jnp
from jax import lax
from jax.experimental import pallas as pl
from jax.experimental.layout import Layout, with_layout_constraint
from jax.experimental.pallas import tpu as pltpu
from jax.sharding import PartitionSpec as P

epsilon = 1e-06
highest = lax.Precision.HIGHEST
thresholds = (12, 16, 23, 32, 46, 64, 91)
masked_out = -1e30
bf16 = jnp.bfloat16
f32 = jnp.float32
peer_axes = ("ctx", "wshard")
vmem_bytes = 60 * 1024 * 1024

ladder_ring = (0, 2, 4, 6, 7, 5, 3, 1)


def bucket_of(offset):
    distance = jnp.abs(offset)
    beyond = 8 + sum(((distance >= border).astype(jnp.int32) for border in thresholds))
    near_far = jnp.where(distance < 8, distance, beyond)
    return jnp.where(offset > 0, 16, 0) + near_far


def rms_norm(values, gain_vector):
    return (
        values
        * lax.rsqrt(jnp.mean(values * values, axis=-1, keepdims=True) + epsilon)
        * gain_vector
    )


def dot(left_side, right_side, dims, precision=None):
    return lax.dot_general(
        left_side, right_side, (dims, ((), ())), precision=precision, preferred_element_type=f32
    )


def forward_product(left_side, right_side):
    return dot(left_side, right_side, ((1,), (0,)))


def backward_product(left_side, right_side):
    return dot(left_side, right_side, ((1,), (1,)))


def weight_product(left_side, right_side):
    return dot(left_side, right_side, ((0,), (0,)))


def iota(shape, dim):
    return lax.broadcasted_iota(jnp.int32, shape, dim)


def arrange_kernel(rows, count, me_ref, order_ref, gain_ref, weight_ref, *refs):
    blocks, (x_ref, normed_ref, qkv_ref) = refs[:-3], refs[-3:]
    me = me_ref[0]
    first = (me ^ pl.program_id(0)) * rows
    tokens = first + iota((rows, rows), 0)
    total = None
    for k in range(count):
        places = order_ref[pl.ds(me ^ k, 1), :]
        chosen = (places == tokens).astype(f32).astype(bf16)
        part = forward_product(chosen, blocks[k][...])
        total = part if total is None else total + part
    x_ref[...] = total.astype(bf16)
    normed = rms_norm(total, gain_ref[...]).astype(bf16)
    normed_ref[...] = normed
    qkv_ref[...] = forward_product(normed, weight_ref[...]).astype(bf16)


def own_heads_kernel(width, count, n_w, me_ref, *refs):
    mine, given, out_ref = refs[:3], refs[3:6], refs[6]
    me = me_ref[0]
    half, columns = mine[0].shape
    for m in range(count):

        @pl.when(me == m)
        def _():
            for t in range(3):
                for w in range(n_w):
                    source = mine[t] if m % n_w == w else given[t]
                    place = slice(w * half, (w + 1) * half), slice(t * width, (t + 1) * width)
                    if (m + 1) * width <= columns:
                        out_ref[place] = source[:, m * width : (m + 1) * width]
                    else:
                        out_ref[place] = jnp.zeros((half, width), out_ref.dtype)


def bias_kernel(rows, heads_here, heads, buckets, me_ref, table_ref, out_ref):
    lanes = iota((8, 4 * rows), 1)
    ids = bucket_of(2 * rows - lanes)
    for h in range(heads_here):
        head = jnp.minimum(me_ref[0] * heads_here + h, heads - 1)
        base = jnp.zeros((8, 4 * rows), f32)
        for b in range(buckets):
            base = jnp.where(ids == b, table_ref[b, head], base)
        wide = jnp.broadcast_to(base[0:1], (rows, 4 * rows))
        rolled = pltpu.roll(wide, 0, 1, stride=1, stride_axis=0)
        out_ref[h, 0] = jnp.full((rows, rows), table_ref[buckets // 2 - 1, head], f32)
        out_ref[h, 4] = jnp.full((rows, rows), table_ref[buckets - 1, head], f32)
        for delta in (1, 0, -1):
            start = rows + rows * (1 - delta)
            out_ref[h, delta + 2] = rolled[:, start : start + rows]


def span_of(lengths_ref, seqs, first, last, rows, total):
    low, high, end = 0, total, 0
    ends = []
    for s in range(seqs):
        end = end + lengths_ref[s]
        ends.append(end)
    for s in range(seqs):
        low = jnp.where(ends[s] <= first, ends[s], low)
    for s in reversed(range(seqs)):
        high = jnp.where(ends[s] > last, ends[s], high)
    high = jnp.minimum(high, total)
    return ends, low // rows, (high + rows - 1) // rows


def sequence_ids(ends, first, shape, dim):
    places = first + iota(shape, dim)
    ids = jnp.zeros(shape, jnp.int32)
    for end in ends:
        ids = ids + (places >= end).astype(jnp.int32)
    return ids


def attend_kernel(
    rows, count, heads_here, size, seqs, me_ref, lengths_ref, qkv_ref, bias_ref, att_ref, wide_ref, lse_ref
):
    me = me_ref[0]
    width = heads_here * size
    here = pl.program_id(0)
    block = me ^ here
    ends, low, high = span_of(
        lengths_ref, seqs, block * rows, block * rows + rows - 1, rows, count * rows
    )
    query_seq = sequence_ids(ends, block * rows, (1, rows), 1)
    start = pl.multiple_of(here * rows, rows)
    queries = qkv_ref[pl.ds(start, rows), :][:, :width]

    def step(key_block, carry):
        at = pl.multiple_of((key_block ^ me) * rows, rows)
        own = qkv_ref[pl.ds(at, rows), :]
        delta = jnp.clip(key_block - block, -2, 2) + 2
        same = sequence_ids(ends, key_block * rows, (rows, 1), 0) == query_seq
        after = []
        for h in range(heads_here):
            top, total, acc = carry[h]
            query = queries[:, h * size : (h + 1) * size]
            key = own[:, width + h * size : width + (h + 1) * size]
            value = own[:, 2 * width + h * size : 2 * width + (h + 1) * size]
            scores = backward_product(key, query) + bias_ref[h, delta]
            scores = jnp.where(same, scores, masked_out)
            top_next = jnp.maximum(top, jnp.max(scores, axis=0, keepdims=True))
            probs = jnp.exp(scores - top_next)
            fade = jnp.exp(top - top_next)
            total = total * fade + jnp.sum(probs, axis=0, keepdims=True)
            acc = acc * fade + weight_product(value, probs.astype(bf16))
            after.append((top_next, total, acc))
        return tuple(after)

    fresh = (
        jnp.full((1, rows), masked_out, f32),
        jnp.zeros((1, rows), f32),
        jnp.zeros((size, rows), f32),
    )
    done = lax.fori_loop(low, high, step, (fresh,) * heads_here)
    for h in range(heads_here):
        top, total, acc = done[h]
        lse_ref[h : h + 1, :] = top + jnp.log(total)
        out = (acc / total).T
        wide_ref[:, h * size : (h + 1) * size] = out
        att_ref[:, h * size : (h + 1) * size] = out.astype(bf16)


def attend_back_kernel(
    rows,
    count,
    heads_here,
    size,
    seqs,
    buckets,
    me_ref,
    lengths_ref,
    qkv_ref,
    bias_ref,
    lse_ref,
    wide_ref,
    d_att_ref,
    dqkv_ref,
    table_ref,
    dq_ref,
    sums_ref,
    delta_ref,
):
    me = me_ref[0]
    width = heads_here * size
    here = pl.program_id(0)
    block = me ^ here

    @pl.when(here == 0)
    def _():
        dq_ref[...] = jnp.zeros_like(dq_ref)
        sums_ref[...] = jnp.zeros_like(sums_ref)
        for k in range(count):
            part = slice(k * rows, (k + 1) * rows)
            both = d_att_ref[part, :].astype(f32) * wide_ref[part, :]
            for h in range(heads_here):
                delta_ref[h : h + 1, part] = jnp.sum(
                    both[:, h * size : (h + 1) * size].T, axis=0, keepdims=True
                )

    ends, low, high = span_of(
        lengths_ref, seqs, block * rows, block * rows + rows - 1, rows, count * rows
    )
    key_seq = sequence_ids(ends, block * rows, (rows, 1), 0)
    start = pl.multiple_of(here * rows, rows)
    own = qkv_ref[pl.ds(start, rows), :]

    def step(query_block, carry):
        rel = query_block ^ me
        at = pl.multiple_of(rel * rows, rows)
        queries = qkv_ref[pl.ds(at, rows), :][:, :width]
        d_outs = d_att_ref[pl.ds(at, rows), :]
        near = jnp.clip(block - query_block, -2, 2) + 2
        same = key_seq == sequence_ids(ends, query_block * rows, (1, rows), 1)
        after = []
        for h in range(heads_here):
            d_key, d_value = carry[h]
            key = own[:, width + h * size : width + (h + 1) * size]
            value = own[:, 2 * width + h * size : 2 * width + (h + 1) * size]
            query = queries[:, h * size : (h + 1) * size]
            d_out = d_outs[:, h * size : (h + 1) * size]
            scores = backward_product(key, query) + bias_ref[h, near]
            lse = lse_ref[h : h + 1, pl.ds(at, rows)]
            soft = jnp.where(same, jnp.exp(scores - lse), 0.0)
            d_probs = backward_product(value, d_out)
            d_scores = (soft * (d_probs - delta_ref[h : h + 1, pl.ds(at, rows)])).astype(bf16)
            sums_ref[h, near] += d_scores.astype(f32)
            d_value = d_value + forward_product(soft.astype(bf16), d_out)
            d_key = d_key + forward_product(d_scores, query)
            dq_ref[h, rel] += weight_product(key, d_scores)
            after.append((d_key, d_value))
        return tuple(after)

    zero = jnp.zeros((rows, size), f32)
    done = lax.fori_loop(low, high, step, ((zero, zero),) * heads_here)
    for h in range(heads_here):
        d_key, d_value = done[h]
        dqkv_ref[pl.ds(start, rows), width + h * size : width + (h + 1) * size] = d_key.astype(bf16)
        dqkv_ref[pl.ds(start, rows), 2 * width + h * size : 2 * width + (h + 1) * size] = (
            d_value.astype(bf16)
        )

    @pl.when(here == count - 1)
    def _():
        for h in range(heads_here):
            for k in range(count):
                dqkv_ref[k * rows : (k + 1) * rows, h * size : (h + 1) * size] = (
                    dq_ref[h, k].T.astype(bf16)
                )
        turned = (iota((rows, rows), 0) + iota((rows, rows), 1) == rows - 1).astype(f32)
        ids = bucket_of(2 * rows - 1 - iota((buckets, 4 * rows), 1))
        mine = ids == iota((buckets, 4 * rows), 0)
        bucket_rows = iota((buckets, 1), 0)
        lanes = iota((buckets, 128), 1)
        table = jnp.zeros((buckets, 128), f32)
        for h in range(heads_here):
            strip = jnp.concatenate(
                [forward_product_exact(turned, sums_ref[h, d]) for d in (3, 2, 1)]
                + [jnp.zeros((rows, rows), f32)],
                axis=1,
            )
            diagonals = jnp.sum(
                pltpu.roll(strip, 0, 1, stride=1, stride_axis=0), axis=0, keepdims=True
            )
            column = jnp.sum(jnp.where(mine, diagonals, 0.0), axis=1, keepdims=True)
            column = column + jnp.where(bucket_rows == buckets // 2 - 1, jnp.sum(sums_ref[h, 0]), 0.0)
            column = column + jnp.where(bucket_rows == buckets - 1, jnp.sum(sums_ref[h, 4]), 0.0)
            table = jnp.where(lanes == h, column, table)
        table_ref[...] = table


def place_kernel(groups, part, count, units_all, hidden_units, spot_ref, *refs):
    spot = spot_ref[0]
    wide, refs = refs[: 4 * groups], refs[4 * groups :]
    outs, (up, down, turned), sems = refs[:2], refs[2:-1], refs[-1]
    units = units_all // count
    middle = 3 * units // 2

    def row_of(j, h):
        return piece_row(spot, groups, part, j, h)

    def copy(k, source):
        return pltpu.make_async_copy(source, outs[k], sems.at[k])

    def gather(target, t):
        for c in range(2):
            low, high = max(c * middle, t * units), min((c + 1) * middle, (t + 1) * units)
            for r in range(count):
                first = r * units + low - t * units
                size = min(high - low, hidden_units - first)
                if low >= high or size <= 0:
                    continue
                start = r * middle + low - c * middle
                for j in range(groups):
                    for h in range(2):
                        block = wide[(j * 2 + c) * 2 + h]
                        target[pl.ds(row_of(j, h), part), first : first + size] = (
                            block[:, start : start + size].astype(f32)
                        )

    gather(up, 1)
    copy(0, up).start()
    gather(down, 2)
    for first in range(0, hidden_units, 128):
        turned[first : first + 128, :] = down[:, first : first + 128].T
    copy(1, turned).start()
    for k, source in enumerate((up, turned)):
        copy(k, source).wait()


def piece_row(spot, groups, part, j, h):
    index = lax.rem(spot + groups - j, groups) if h == 0 else lax.rem(spot + j, groups)
    return pl.multiple_of((2 * index + h) * part, 8)


def place_gate_kernel(groups, part, count, units, hidden_units, spot_ref, *refs):
    spot, pieces, out_ref = spot_ref[0], refs[:-1], refs[-1]
    middle = pieces[0].shape[1] // count
    for j in range(groups):
        for h in range(2):
            rows = pl.ds(piece_row(spot, groups, part, j, h), part)
            for r in range(count):
                first = r * units
                size = min(units, hidden_units - first)
                out_ref[rows, first : first + size] = (
                    pieces[j * 2 + h][:, r * middle : r * middle + size].astype(f32)
                )


def place_heads_kernel(groups, part, count, width, spot_ref, *refs):
    spot = spot_ref[0]
    narrow, outs, out_rows = refs[: 2 * groups], refs[2 * groups : -1], refs[-1]
    heads_all = count * width
    for j in range(groups):
        for h in range(2):
            rows = pl.ds(piece_row(spot, groups, part, j, h), part)
            for k in range(3):
                outs[k][rows, :] = (
                    narrow[j * 2 + h][:, k * heads_all : (k + 1) * heads_all].astype(f32)
                )
            for q in range(count):
                first = 3 * heads_all + q * width
                out_rows[q, rows, :] = narrow[j * 2 + h][:, first : first + width].astype(f32)
    size = out_rows.shape[1]
    for q in range(count):
        outs[3][:, q * size : (q + 1) * size] = out_rows[q].T


def forward_product_exact(left_side, right_side):
    return dot(left_side, right_side, ((1,), (0,)), highest)


def whole(shape):
    return pl.BlockSpec(shape, lambda *_: (0,) * len(shape))


def per_device(
    sizes,
    inputs,
    out_grad,
    lengths,
    permutation,
    gain_attention,
    query_weight,
    key_weight,
    value_weight,
    out_weight,
    bucket_bias,
    gain_feedforward,
    gate_weight,
    up_weight,
    down_weight,
):
    n_group, n_ctx, n_w = sizes
    n = n_ctx * n_w
    fast = (n_group, n_ctx, n_w) == (8, 2, 2)
    rows, model = inputs.shape
    buckets, heads = bucket_bias.shape
    hidden_units = gate_weight.shape[1]
    size = query_weight.shape[1] // heads
    seqs = lengths.shape[1]
    tokens = rows * n
    heads_here = -(-heads // n)
    width = heads_here * size
    units = -(-hidden_units // (128 * n)) * 128
    ctx, wsh = lax.axis_index("ctx"), lax.axis_index("wshard")
    me = lax.axis_index(peer_axes)
    rank = wsh * n_ctx + ctx
    flip_w = [(0, 1), (1, 0)]


    def mate(block):
        return lax.ppermute(block, "wshard", flip_w)

    def across(block):
        return lax.ppermute(block, "ctx", flip_w)

    def to_relative(stacked):
        return jnp.take(stacked, me ^ lax.iota(jnp.int32, n), axis=0)

    def gather_blocks(block):
        if fast:
            far = across(block)
            return [block, mate(block), far, mate(far)]
        stacked = to_relative(lax.all_gather(block, peer_axes, axis=0, tiled=False))
        return [stacked[k] for k in range(n)]

    def columns_of(weight, which, wide):
        over = max(0, n * wide - weight.shape[1])
        padded = jnp.pad(weight, ((0, 0), (0, over))) if over else weight
        return lax.dynamic_slice_in_dim(padded, which * wide, wide, 1)

    def own_columns(parts, wide, which):
        return jnp.concatenate([columns_of(part, which, wide) for part in parts], axis=1)

    def in_order(mine, given):
        upper = jnp.where(wsh == 0, mine, given)
        lower = jnp.where(wsh == 0, given, mine)
        return jnp.concatenate([upper, lower], axis=0)

    hold = lax.optimization_barrier

    if fast:
        row_far, row_mate = across(inputs), mate(inputs)
    heads_mine = (query_weight, key_weight, value_weight)
    heads_given = [mate(weight) for weight in heads_mine]
    out_other = mate(out_weight)
    gate_up_mine = own_columns((gate_weight, up_weight), units, rank)
    gate_up_sent = own_columns((gate_weight, up_weight), units, (1 - wsh) * n_ctx + ctx)
    half = down_weight.shape[0]
    extra = n_ctx * units - half
    down_other = mate(down_weight[:extra])
    down_wide = jnp.concatenate(
        [
            down_weight,
            jnp.where(wsh == 0, down_other, jnp.zeros_like(down_other)),
            jnp.zeros_like(down_other),
        ]
    )
    down_own = lax.dynamic_slice_in_dim(down_wide, wsh * extra + ctx * units, units, 0)
    me_1 = me.reshape(1).astype(jnp.int32)
    order = permutation.reshape(n, rows)
    params = pltpu.CompilerParams(vmem_limit_bytes=vmem_bytes)
    qkv_weight = pl.pallas_call(
        functools.partial(own_heads_kernel, width, n, n_w),
        out_shape=jax.ShapeDtypeStruct((model, 3 * width), bf16),
        in_specs=[pl.BlockSpec(memory_space=pltpu.SMEM)]
        + [pl.BlockSpec(memory_space=pltpu.VMEM)] * 6,
        out_specs=pl.BlockSpec(memory_space=pltpu.VMEM),
        compiler_params=params,
        name="own_heads",
    )(me_1, *heads_mine, *heads_given)
    bias = pl.pallas_call(
        functools.partial(bias_kernel, rows, heads_here, heads, buckets),
        out_shape=jax.ShapeDtypeStruct((heads_here, 5, rows, rows), f32),
        in_specs=[
            pl.BlockSpec(memory_space=pltpu.SMEM),
            pl.BlockSpec(memory_space=pltpu.SMEM),
        ],
        out_specs=pl.BlockSpec(memory_space=pltpu.VMEM),
        compiler_params=params,
        name="bias_strips",
    )(me_1, bucket_bias)
    if fast:
        row_far, out_grad, qkv_weight, bias, gate_up_mine, gate_up_sent = hold(
            (row_far, out_grad, qkv_weight, bias, gate_up_mine, gate_up_sent)
        )
        row_blocks = [inputs, row_mate, row_far, mate(row_far)]
    else:
        row_blocks = gather_blocks(inputs)
    gate_up_given = mate(gate_up_sent)
    dy = jnp.concatenate(gather_blocks(out_grad))

    x_all, normed, qkv = pl.pallas_call(
        functools.partial(arrange_kernel, rows, n),
        out_shape=(
            jax.ShapeDtypeStruct((tokens, model), bf16),
            jax.ShapeDtypeStruct((tokens, model), bf16),
            jax.ShapeDtypeStruct((tokens, 3 * width), bf16),
        ),
        grid_spec=pltpu.PrefetchScalarGridSpec(
            num_scalar_prefetch=1,
            grid=(n,),
            in_specs=[whole((n, rows)), whole((1, model)), whole((model, 3 * width))]
            + [whole((rows, model))] * n,
            out_specs=[
                pl.BlockSpec((rows, model), lambda t, *_: (t, 0)),
                pl.BlockSpec((rows, model), lambda t, *_: (t, 0)),
                pl.BlockSpec((rows, 3 * width), lambda t, *_: (t, 0)),
            ],
        ),
        compiler_params=params,
        cost_estimate=pl.CostEstimate(
            flops=2 * tokens * model * (tokens + 3 * width),
            bytes_accessed=8 * tokens * model,
            transcendentals=0,
        ),
        name="arrange_project",
    )(me_1, order, gain_attention.reshape(1, model), qkv_weight, *row_blocks)
    lengths_row = lengths.reshape(seqs)
    attended, attended_wide, lse = pl.pallas_call(
        functools.partial(attend_kernel, rows, n, heads_here, size, seqs),
        out_shape=(
            jax.ShapeDtypeStruct((tokens, width), bf16),
            jax.ShapeDtypeStruct((tokens, width), f32),
            jax.ShapeDtypeStruct((heads_here, tokens), f32),
        ),
        grid_spec=pltpu.PrefetchScalarGridSpec(
            num_scalar_prefetch=2,
            grid=(n,),
            in_specs=[whole((tokens, 3 * width)), whole((heads_here, 5, rows, rows))],
            out_specs=[
                pl.BlockSpec((rows, width), lambda t, *_: (t, 0)),
                pl.BlockSpec((rows, width), lambda t, *_: (t, 0)),
                pl.BlockSpec((heads_here, rows), lambda t, *_: (0, t)),
            ],
        ),
        compiler_params=params,
        cost_estimate=pl.CostEstimate(
            flops=16 * tokens * tokens * width,
            bytes_accessed=16 * tokens * width,
            transcendentals=tokens * tokens * heads_here,
        ),
        name="attend",
    )(me_1, lengths_row, qkv, bias)

    strip = model // n // n_group
    part = strip // 2
    if fast:
        group = lax.axis_index("group")
        spot = jnp.where(group % 2 == 0, group // 2, n_group - 1 - group // 2)
        ahead = [(ladder_ring[k], ladder_ring[(k + 1) % n_group]) for k in range(n_group)]
        behind = [(b, a) for a, b in ahead]

    def forward(block):
        return lax.ppermute(block, "group", ahead)

    def backward(block):
        return lax.ppermute(block, "group", behind)

    def diagonal(block):
        return lax.ppermute(block, peer_axes, [(q, q ^ 3) for q in range(n)])

    def pick(array, index, axis):
        return lax.squeeze(lax.dynamic_slice_in_dim(array, index, 1, axis), (axis,))

    def rank_of(k):
        peer = me ^ k
        return (peer % n_w) * n_ctx + peer // n_w

    def ring(take, swap, pieces):
        both_ways = (forward, backward)
        one, two = take(0, lax.rem(spot + 7, n_group)), take(1, lax.rem(spot + 1, n_group))
        for s in range(n_group - 1):
            came = yield (one, two), both_ways
            one = came[0] + take(0, lax.rem(spot + 14 - s, n_group))
            two = came[1] + take(1, lax.rem(spot + 2 + s, n_group))
        pairs, (blocks, join) = [], swap(one, two)
        for block in blocks:
            came = yield tuple(block[1:]), (mate, across, diagonal)
            pairs.append(join([block[0], *came]))
        for pair in pairs:
            pieces.extend(pair)
        for s in range(n_group - 1):
            for c, pair in enumerate(pairs):
                pairs[c] = yield pair, both_ways
                pieces.extend(pairs[c])

    class Stream:
        def __init__(self, steps):
            self.steps, self.result, self.came = steps, None, None
            self.pending = next(steps)

        def advance(self, came):
            try:
                self.pending = self.steps.send(came)
            except StopIteration as stop:
                self.pending, self.result = None, stop.value

    order_token = [me]

    def tick(values, *streams):
        live = [stream for stream in streams if stream is not None and stream.pending is not None]
        if not live:
            return values
        arrived, values = hold(([stream.came for stream in live if stream.came], values))
        for stream in live:
            if stream.came:
                stream.advance(arrived.pop(0))
        live = [stream for stream in live if stream.pending is not None]
        operands, values, order_token[0] = hold(
            ([stream.pending[0] for stream in live], values, order_token[0])
        )
        for stream, sent in zip(live, operands):
            stream.came = [send(x) for send, x in zip(stream.pending[1], sent)]
        return values

    def piece_of(cut, index, h):
        zero = jnp.zeros((), index.dtype)
        starts = (zero, index, zero + h, zero, zero)
        return lax.squeeze(
            lax.dynamic_slice(cut, starts, (n, 1, 1, part, cut.shape[4])), (1, 2)
        )

    def rows_cut(grad):
        return grad.reshape(n, n_group, 2, part, grad.shape[1])

    wide_pieces, narrow_pieces = [], []

    def wide_ring(grad_gate_up, grad_down):
        one, two = rows_cut(grad_gate_up), rows_cut(grad_down)

        def take(h, index):
            return jnp.concatenate([piece_of(x, index, h) for x in (one, two)], axis=-1)

        def swap(one, two):
            both = jnp.stack([one, two], axis=1)
            middle = 3 * units // 2

            def join(came):
                full = jnp.zeros((2, part, n * middle), bf16)
                for k in range(n):
                    full = lax.dynamic_update_slice_in_dim(full, came[k], rank_of(k) * middle, 2)
                return full[0], full[1]

            halves = [both[..., :middle], both[..., middle:]]
            return [[pick(half, me ^ k, 0) for k in range(n)] for half in halves], join

        return ring(take, swap, wide_pieces)

    def small_ring(grad_qkv, grad_out):
        one, two = rows_cut(grad_qkv), rows_cut(grad_out)

        def take(h, index):
            return jnp.concatenate([piece_of(x, index, h) for x in (one, two)], axis=-1)

        def swap(one, two):
            both = jnp.stack([one, two], axis=1)
            own = jnp.concatenate([both[k, :, :, 3 * width :] for k in range(n)], axis=2)

            def join(came):
                stacked = jnp.stack(came)
                came = [pick(stacked, me ^ r, 0) for r in range(n)]
                full = jnp.concatenate(
                    [came[r][:, :, k * width : (k + 1) * width] for k in range(3) for r in range(n)]
                    + [own],
                    axis=2,
                )
                return full[0], full[1]

            return [[pick(both, me ^ k, 0)[:, :, : 3 * width] for k in range(n)]], join

        return ring(take, swap, narrow_pieces)

    def sum_ring(small):
        for axis, bit, count in (
            ("wshard", 1, n_w),
            ("ctx", 1, n_ctx),
            ("group", 1, n_group),
            ("group", 2, n_group),
            ("group", 4, n_group),
        ):
            pairs = [(g, g ^ bit) for g in range(count)]
            came = yield (small,), (lambda x: lax.ppermute(x, axis, pairs),)
            small = small + came[0]
        return small

    def scatter_near(partial):
        sent = partial.reshape(n, rows, -1)
        if not fast:
            total = lax.psum_scatter(to_relative(sent), peer_axes, scatter_dimension=0, tiled=False)
            return total.astype(f32), None
        got = mate(jnp.stack([sent[1], sent[3]]))
        near = sent[0].astype(f32) + got[0].astype(f32)
        return near, (sent[2].astype(f32) + got[1].astype(f32)).astype(bf16)

    def scatter_far(near, away):
        return near + across(away).astype(f32) if fast else near

    attended, out_mine, out_other, gate_up_mine = hold(
        (attended, out_weight, out_other, gate_up_mine)
    )
    gate_up = in_order(gate_up_mine, gate_up_given)
    if fast:
        attended_far, attended_mate = across(attended), mate(attended)
        attended_far, gate_up = hold((attended_far, gate_up))
        attended_blocks = [attended, attended_mate, attended_far, mate(attended_far)]
    else:
        attended_blocks = gather_blocks(attended)
    out_full = in_order(out_mine, out_other)
    out_full = jnp.pad(out_full, ((0, n * width - out_full.shape[0]), (0, 0)))
    out_blocks = [lax.dynamic_slice_in_dim(out_full, (me ^ k) * width, width, 0) for k in range(n)]
    out_relative = jnp.concatenate(out_blocks, axis=0)
    by_rows = [
        jnp.concatenate(
            [attended_blocks[k][(m ^ k) * rows : ((m ^ k) + 1) * rows] for m in range(n)]
        )
        for k in range(n)
    ]
    attended_all = jnp.concatenate(by_rows, axis=1)
    residual_all = x_all.astype(f32) + forward_product(
        attended_all, out_relative
    )
    residual = residual_all[:rows]
    normed_ff = rms_norm(residual_all, gain_feedforward).astype(bf16)
    gate_up_proj = forward_product(normed_ff, gate_up)
    gate_proj, up_proj = gate_up_proj[:, :units], gate_up_proj[:, units:]

    def activate(gate_in, up_in):
        return jax.nn.gelu(gate_in, approximate=True) * up_in

    hidden_wide, activate_back = jax.vjp(activate, gate_proj, up_proj)
    hidden = hidden_wide.astype(bf16)
    d_hidden = backward_product(dy, down_own)
    d_gate_wide, d_up_wide = activate_back(d_hidden)
    d_gate_up = jnp.concatenate([d_gate_wide.astype(bf16), d_up_wide.astype(bf16)], axis=1)

    grad_gate_up = weight_product(normed_ff, d_gate_up).astype(bf16)
    grad_down = weight_product(dy, hidden).astype(bf16)
    wide = Stream(wide_ring(grad_gate_up, grad_down)) if fast else None
    d_gate_up, hidden = tick((d_gate_up, hidden), wide)

    back = backward_product(d_gate_up, gate_up).astype(bf16)
    back, hidden = tick((back, hidden), wide)
    near, away = scatter_near(back)
    out_partial = forward_product(hidden, down_own).astype(bf16)
    near, away, out_partial = tick((near, away, out_partial), wide)
    d_normed_ff = scatter_far(near, away)
    d_normed_ff, residual = tick((d_normed_ff, residual), wide)
    norm_ff_back = jax.vjp(rms_norm, residual, gain_feedforward)[1]
    d_residual_norm, grad_gain_ff = norm_ff_back(d_normed_ff)
    d_residual = dy[:rows].astype(f32) + d_residual_norm
    branch = d_residual.astype(bf16)

    if fast:
        d_rows = backward_product(branch, out_relative).astype(bf16)
        d_rows = [d_rows[:, k * width : (k + 1) * width] for k in range(n)]
        d_rows = [d_rows[0], mate(d_rows[1]), across(d_rows[2]), diagonal(d_rows[3])]
        d_attended, branch = hold((jnp.concatenate(d_rows), branch))
    else:
        branch_blocks = gather_blocks(branch)
        d_attended = backward_product(jnp.concatenate(branch_blocks), out_blocks[0]).astype(bf16)
    d_attended, branch = tick((d_attended, branch), wide)
    if fast:
        branch_blocks = gather_blocks(branch)
    d_qkv, d_table = pl.pallas_call(
        functools.partial(attend_back_kernel, rows, n, heads_here, size, seqs, buckets),
        out_shape=(
            jax.ShapeDtypeStruct((tokens, 3 * width), bf16),
            jax.ShapeDtypeStruct((buckets, 128), f32),
        ),
        grid_spec=pltpu.PrefetchScalarGridSpec(
            num_scalar_prefetch=2,
            grid=(n,),
            in_specs=[
                whole((tokens, 3 * width)),
                whole((heads_here, 5, rows, rows)),
                whole((heads_here, tokens)),
                whole((tokens, width)),
                whole((tokens, width)),
            ],
            out_specs=[whole((tokens, 3 * width)), whole((buckets, 128))],
            scratch_shapes=[
                pltpu.VMEM((heads_here, n, size, rows), f32),
                pltpu.VMEM((heads_here, 5, rows, rows), f32),
                pltpu.VMEM((heads_here, tokens), f32),
            ],
        ),
        compiler_params=params,
        cost_estimate=pl.CostEstimate(
            flops=40 * tokens * tokens * width,
            bytes_accessed=16 * tokens * width,
            transcendentals=tokens * tokens * heads_here,
        ),
        name="attend_back",
    )(me_1, lengths_row, qkv, bias, lse, attended_wide, d_attended)
    d_qkv, branch_far, out_partial = tick((d_qkv, branch_blocks[2], out_partial), wide)
    branch_blocks[2] = branch_far
    grad_qkv = weight_product(normed, d_qkv).astype(bf16)
    grad_out = sum(
        weight_product(branch_blocks[k], attended[k * rows : (k + 1) * rows]) for k in range(n)
    ).astype(bf16)
    grad_qkv, grad_out = [
        with_layout_constraint(grad, Layout(major_to_minor=(0, 1))) for grad in (grad_qkv, grad_out)
    ]
    grad_qkv, grad_out, d_qkv = tick((grad_qkv, grad_out, d_qkv), wide)
    back = backward_product(d_qkv, qkv_weight).astype(bf16)
    narrow = Stream(small_ring(grad_qkv, grad_out)) if fast else None
    (back,) = tick((back,), wide, narrow)

    near, away = scatter_near(back)
    near, away = tick((near, away), narrow)
    (away,) = tick((away,), wide)
    d_normed = scatter_far(near, away)
    for stream in (narrow, wide, narrow, wide, narrow, wide):
        tick((), stream)
    d_normed, x_own = tick((d_normed, x_all[:rows]), narrow)
    norm_attn_back = jax.vjp(rms_norm, x_own.astype(f32), gain_attention)[1]
    d_input_norm, grad_gain_attn = norm_attn_back(d_normed)
    input_grad = (d_residual + d_input_norm).astype(bf16)
    out_near, out_away = scatter_near(out_partial)
    out_away, grad_gain_attn = tick((out_away, grad_gain_attn), wide)
    outputs = (residual + scatter_far(out_near, out_away)).astype(bf16)

    table_here = jnp.pad(d_table[:, :heads_here], ((0, 0), (0, n * heads_here)))
    table_here = jnp.roll(table_here, me * heads_here, axis=1)[:, :heads]
    small = jnp.concatenate([grad_gain_attn, grad_gain_ff, table_here.reshape(-1)])
    if fast:
        sums = Stream(sum_ring(small))
        own_rows, all_heads = model // n, n * width
        spot_1 = spot.reshape(1).astype(jnp.int32)
        in_vmem = pl.BlockSpec(memory_space=pltpu.VMEM)
        rounds = 0
        while narrow.pending or sums.pending or len(wide_pieces) < 4 * n_group - 2:
            rounds += 1
            tick((), narrow, sums)
            if rounds == n_group:
                outputs, input_grad = tick((outputs, input_grad), wide)
            elif len(wide_pieces) < 4 * n_group - 2:
                tick((), wide)
        heads_grads = pl.pallas_call(
            functools.partial(place_heads_kernel, n_group, part, n, width),
            out_shape=[jax.ShapeDtypeStruct((own_rows, all_heads), f32)] * 3
            + [jax.ShapeDtypeStruct((width, model), f32)],
            in_specs=[pl.BlockSpec(memory_space=pltpu.SMEM)] + [in_vmem] * (2 * n_group),
            out_specs=[in_vmem] * 4,
            scratch_shapes=[pltpu.VMEM((n, own_rows, width), f32)],
            compiler_params=params,
            name="place_heads",
        )(spot_1, *narrow_pieces)
        total_gate = pl.pallas_call(
            functools.partial(place_gate_kernel, n_group, part, n, units, hidden_units),
            out_shape=jax.ShapeDtypeStruct((own_rows, hidden_units), f32),
            in_specs=[pl.BlockSpec(memory_space=pltpu.SMEM)] + [in_vmem] * (2 * n_group),
            out_specs=in_vmem,
            compiler_params=params,
            name="place_gate",
        )(spot_1, *[wide_pieces[4 * j + h] for j in range(n_group) for h in range(2)])
        heads_grads, total_gate = tick((heads_grads, total_gate), wide)
        small = sums.result
    else:
        small = lax.psum(small, ("group",) + peer_axes)
    share = model // n
    gains = [lax.dynamic_slice_in_dim(small, k * model + order_token[0] * share, share) for k in range(2)]
    grad_table = small[2 * model :].reshape(buckets, heads)

    if fast:
        *total_qkv, total_out = heads_grads
        wide_shape, down_shape = (own_rows, hidden_units), (hidden_units, own_rows)
        total_up, total_down = pl.pallas_call(
            functools.partial(place_kernel, n_group, part, n, n * units, hidden_units),
            out_shape=[
                jax.ShapeDtypeStruct(shape, f32) for shape in (wide_shape, down_shape)
            ],
            in_specs=[pl.BlockSpec(memory_space=pltpu.SMEM)] + [in_vmem] * (4 * n_group),
            out_specs=[pl.BlockSpec(memory_space=pl.ANY)] * 2,
            scratch_shapes=[pltpu.VMEM(wide_shape, f32)] * 2
            + [pltpu.VMEM(down_shape, f32), pltpu.SemaphoreType.DMA((2,))],
            compiler_params=params,
            name="place",
        )(spot_1, *wide_pieces)
    else:

        def place_columns(grad, which, wide, total):
            full = jnp.zeros((grad.shape[0], n * wide), bf16)
            full = lax.dynamic_update_slice_in_dim(full, grad, which * wide, 1)
            return full[:, :total]

        def finish(full, dim):
            full = lax.psum_scatter(full, peer_axes, scatter_dimension=dim, tiled=True)
            return lax.psum(full, "group").astype(f32)

        total_qkv = [
            finish(
                place_columns(grad_qkv[:, k * width : (k + 1) * width], me, width, heads * size), 0
            )
            for k in range(3)
        ]
        total_out = finish(place_columns(grad_out, me, width, heads * size).T, 0)
        total_gate = finish(place_columns(grad_gate_up[:, :units], rank, units, hidden_units), 0)
        total_up = finish(place_columns(grad_gate_up[:, units:], rank, units, hidden_units), 0)
        total_down = finish(place_columns(grad_down, rank, units, hidden_units).T, 1)
    return (
        outputs,
        input_grad,
        gains[0],
        total_qkv[0],
        total_qkv[1],
        total_qkv[2],
        total_out,
        grad_table,
        gains[1],
        total_gate,
        total_up,
        total_down,
    )


def solution(mesh):
    sizes = (mesh.shape["group"], mesh.shape["ctx"], mesh.shape["wshard"])
    return jax.shard_map(
        functools.partial(per_device, sizes),
        mesh=mesh,
        in_specs=(
            P(("group", "ctx", "wshard"), None),
            P(("group", "ctx", "wshard"), None),
            P("group", None),
            P("group", None),
            P(),
            P("wshard", None),
            P("wshard", None),
            P("wshard", None),
            P("wshard", None),
            P(),
            P(),
            P("wshard", None),
            P("wshard", None),
            P("wshard", None),
        ),
        out_specs=(
            P(("group", "ctx", "wshard"), None),
            P(("group", "ctx", "wshard"), None),
            P(("ctx", "wshard")),
            P(("ctx", "wshard"), None),
            P(("ctx", "wshard"), None),
            P(("ctx", "wshard"), None),
            P(("ctx", "wshard"), None),
            P(),
            P(("ctx", "wshard")),
            P(("ctx", "wshard"), None),
            P(("ctx", "wshard"), None),
            P(None, ("ctx", "wshard")),
        ),
        check_vma=False,
    )
```
